32 devices in a mesh: wide: 8 (over z, x), narrow: 4 (over y, core).
Axes of the slice: x: 2, y: 2, z: 4, core: 2. Of those that a mesh axis runs over, the one named last changes fastest.
Arguments:
- layer_input: bfloat16 [8192, 1536], P('wide'), may hold values from -6 to 6
- grad_out: bfloat16 [8192, 1536], P('wide'), may hold values from -6 to 6
- segment_ids: int32 [8192], P('wide'), may hold values from 0 to 8191, as said below
- positions: int32 [8192], P('wide'), may hold values from 0 to 4095, as said below
- norm_gains: float32 [2, 1536], P(None, ('wide', 'narrow')), may hold values from 0.5 to 1.5
- norm_gains_first: float32 [2, 1536], P(None, ('wide', 'narrow')), may hold values from -3 to 3
- norm_gains_second: float32 [2, 1536], P(None, ('wide', 'narrow')), may hold values from 0.1 to 10
- query_weight: float32 [1536, 1536], P('wide', 'narrow'), may hold values from -0.15625 to 0.15625
- query_weight_first: float32 [1536, 1536], P('wide', 'narrow'), may hold values from -3 to 3
- query_weight_second: float32 [1536, 1536], P('wide', 'narrow'), may hold values from 0.1 to 10
- query_bias: float32 [12, 128], P('narrow', 'wide'), may hold values from -3 to 3
- query_bias_first: float32 [12, 128], P('narrow', 'wide'), may hold values from -3 to 3
- query_bias_second: float32 [12, 128], P('narrow', 'wide'), may hold values from 0.1 to 10
- keyvalue_weight: float32 [1536, 512], P(('wide', 'narrow')), may hold values from -0.15625 to 0.15625
- keyvalue_weight_first: float32 [1536, 512], P(('wide', 'narrow')), may hold values from -3 to 3
- keyvalue_weight_second: float32 [1536, 512], P(('wide', 'narrow')), may hold values from 0.1 to 10
- keyvalue_bias: float32 [512], P(('wide', 'narrow')), may hold values from -3 to 3
- keyvalue_bias_first: float32 [512], P(('wide', 'narrow')), may hold values from -3 to 3
- keyvalue_bias_second: float32 [512], P(('wide', 'narrow')), may hold values from 0.1 to 10
- output_weight: float32 [1536, 1536], P('narrow', 'wide'), may hold values from -1.25 to 1.25
- output_weight_first: float32 [1536, 1536], P('narrow', 'wide'), may hold values from -3 to 3
- output_weight_second: float32 [1536, 1536], P('narrow', 'wide'), may hold values from 0.1 to 10
- gateup_weight: float32 [1536, 2, 8960], P('wide', None, 'narrow'), may hold values from -0.15625 to 0.15625
- gateup_weight_first: float32 [1536, 2, 8960], P('wide', None, 'narrow'), may hold values from -3 to 3
- gateup_weight_second: float32 [1536, 2, 8960], P('wide', None, 'narrow'), may hold values from 0.1 to 10
- down_weight: float32 [8960, 1536], P('narrow', 'wide'), may hold values from -0.0625 to 0.0625
- down_weight_first: float32 [8960, 1536], P('narrow', 'wide'), may hold values from -3 to 3
- down_weight_second: float32 [8960, 1536], P('narrow', 'wide'), may hold values from 0.1 to 10
Outputs:
- layer_output: bfloat16 [8192, 1536], P('wide')
- input_grad: bfloat16 [8192, 1536], P('wide')
- grad_norm_gains: float32 [2, 1536], P(None, ('wide', 'narrow'))
- update_norm_gains: float32 [2, 1536], P(None, ('wide', 'narrow'))
- grad_query_weight: float32 [1536, 1536], P('wide', 'narrow')
- update_query_weight: float32 [1536, 1536], P('wide', 'narrow')
- grad_query_bias: float32 [12, 128], P('narrow', 'wide')
- update_query_bias: float32 [12, 128], P('narrow', 'wide')
- grad_keyvalue_weight: float32 [1536, 512], P(('wide', 'narrow'))
- update_keyvalue_weight: float32 [1536, 512], P(('wide', 'narrow'))
- grad_keyvalue_bias: float32 [512], P(('wide', 'narrow'))
- update_keyvalue_bias: float32 [512], P(('wide', 'narrow'))
- grad_output_weight: float32 [1536, 1536], P('narrow', 'wide')
- update_output_weight: float32 [1536, 1536], P('narrow', 'wide')
- grad_gateup_weight: float32 [1536, 2, 8960], P('wide', None, 'narrow')
- update_gateup_weight: float32 [1536, 2, 8960], P('wide', None, 'narrow')
- grad_down_weight: float32 [8960, 1536], P('narrow', 'wide')
- update_down_weight: float32 [8960, 1536], P('narrow', 'wide')
The draws below stay inside these ranges and needn't reach their ends.
Inputs may be any that keep to these rules, and one draw needn't show every extreme that they name: `segment_ids`: each token's value is the index of the first token of its segment, so it never falls along the tokens; every segment lies inside one aligned row of 4096 tokens; the last token of all is a segment by itself; in every draw at least one row is a single segment. `positions`: each token's value counts the tokens before it in its segment.
All inputs are finite; a program needn't handle non-finite values.
Results may differ from the reference program's by a relative error of at most 0.024.
Values may be sent and summed in bfloat16 or wider, within the bound.
No kernel may reach another device: no remote copies, remote signals or barrier semaphores. Data moves between devices by JAX's collectives and lax.ppermute only.
A program may use at most 320 MiB of HBM per device.

```python
import math
import jax
import jax.numpy as jnp
from jax import lax

D = 1536
H = 12
KV = 2
HD = 128
FF = 8960
LENGTH = 4096
TOKENS = 8192


def segment_layout(key):
    index = jnp.arange(TOKENS, dtype=jnp.int32)
    within = index % LENGTH
    row_of = index // LENGTH
    whole = jax.random.randint(jax.random.fold_in(key, 11), (), 0, TOKENS // LENGTH - 1)
    marks = jax.random.randint(jax.random.fold_in(key, 12), (TOKENS,), 0, max(LENGTH // 4, 2))
    start = (within == 0) | (marks == 0) & (row_of != whole) | (index == TOKENS - 1)
    begin = lax.cummax(jnp.where(start, index, 0), axis=0).astype(jnp.int32)
    return (begin, (index - begin).astype(jnp.int32))


def draw_segment_ids(key, part):
    return segment_layout(key)[0]


def draw_positions(key, part):
    return segment_layout(key)[1]


def spiked(array, own_key, source, target, shards_of, factor):
    owner, partner = [(jnp.arange(array.shape[axis_at]) // (array.shape[axis_at] // shards_of)).reshape([-1 if axis == axis_at else 1 for axis in range(array.ndim)]) for axis_at in (source, target)]
    chosen = jax.random.permutation(own_key, shards_of)[partner]
    strong = (owner == chosen) | (owner == (partner + shards_of // 2) % shards_of)
    return jnp.where(strong, factor * array, array)


def levels(stream_key, extent, cuts, smallest, largest):
    loudness = 1.0
    for dim, blocks in cuts:
        steps = jax.random.uniform(jax.random.fold_in(jax.random.fold_in(stream_key, 6), dim), (blocks,), jnp.float32, smallest / len(cuts), largest / len(cuts))
        loudness = loudness * jnp.repeat(jnp.exp(steps), extent[dim] // blocks).reshape((-1,) + (1,) * (len(extent) - 1 - dim))
    return loudness


def normal_values(rng, shape, width, reach, pieces=(), kind=jnp.bfloat16):
    values = jax.random.normal(rng, shape, jnp.float32) * width
    if len(pieces) > 0:
        values = levels(rng, shape, pieces, -0.22, 0.18) * values
    return jnp.clip(values, min=-reach, max=reach).astype(kind)


def gaussian_with(key, extent, spread, most, pieces, heavy, held_as=jnp.bfloat16):
    values = spread * jax.random.normal(key, extent, jnp.float32)
    if pieces:
        values = values * levels(key, extent, pieces, -0.22, 0.18)
    return jnp.clip(spiked(values, jax.random.fold_in(key, 3), *heavy), -most, most).astype(held_as)


def setup_inputs(seed: int = 0) -> dict:
    key_list = jax.random.split(jax.random.key(seed), 29)
    return {
        "layer_input": gaussian_with(key_list[0], (TOKENS, D), 1.0, 6.0, ((0, 8),), (0, 1, 8, 2.0)),
        "grad_out": gaussian_with(key_list[1], (TOKENS, D), 1.0, 6.0, ((0, 8),), (0, 1, 8, 2.0)),
        "segment_ids": draw_segment_ids(jax.random.fold_in(key_list[28], 71), 0),
        "positions": draw_positions(jax.random.fold_in(key_list[28], 71), 0),
        "norm_gains": jnp.clip(1.0 + 0.1 * jax.random.normal(key_list[4], (2, D), jnp.float32), 0.5, 1.5),
        "norm_gains_first": normal_values(key_list[5], (2, D), 0.5, 3.0, ((1, 32),), jnp.float32),
        "norm_gains_second": jnp.clip(jnp.exp(math.log(10.0) - 4.6051702 * jax.random.uniform(key_list[6], (2, D), jnp.float32) ** levels(key_list[6], (2, D), ((1, 32),), -0.2, 0.2)), 0.1, 10.0),
        "query_weight": normal_values(key_list[7], (D, H * HD), D ** -0.5, 0.15625, ((0, 8), (1, 4)), jnp.float32),
        "query_weight_first": normal_values(key_list[8], (D, H * HD), 0.5, 3.0, ((0, 8), (1, 4)), jnp.float32),
        "query_weight_second": jnp.clip(jnp.exp(math.log(10.0) - 4.6051702 * jax.random.uniform(key_list[9], (D, H * HD), jnp.float32) ** levels(key_list[9], (D, H * HD), ((0, 8), (1, 4)), -0.2, 0.2)), 0.1, 10.0),
        "query_bias": normal_values(key_list[10], (H, HD), 0.5, 3.0, ((0, 4), (1, 8)), jnp.float32),
        "query_bias_first": normal_values(key_list[11], (H, HD), 0.5, 3.0, ((0, 4), (1, 8)), jnp.float32),
        "query_bias_second": jnp.clip(jnp.exp(math.log(10.0) - 4.6051702 * jax.random.uniform(key_list[12], (H, HD), jnp.float32) ** levels(key_list[12], (H, HD), ((0, 4), (1, 8)), -0.2, 0.2)), 0.1, 10.0),
        "keyvalue_weight": normal_values(key_list[13], (D, 2 * KV * HD), D ** -0.5, 0.15625, ((0, 32),), jnp.float32),
        "keyvalue_weight_first": normal_values(key_list[14], (D, 2 * KV * HD), 0.5, 3.0, ((0, 32),), jnp.float32),
        "keyvalue_weight_second": jnp.clip(jnp.exp(math.log(10.0) - 4.6051702 * jax.random.uniform(key_list[15], (D, 2 * KV * HD), jnp.float32) ** levels(key_list[15], (D, 2 * KV * HD), ((0, 32),), -0.2, 0.2)), 0.1, 10.0),
        "keyvalue_bias": normal_values(key_list[16], (2 * KV * HD,), 0.5, 3.0, ((0, 32),), jnp.float32),
        "keyvalue_bias_first": normal_values(key_list[17], (2 * KV * HD,), 0.5, 3.0, ((0, 32),), jnp.float32),
        "keyvalue_bias_second": jnp.clip(jnp.exp(math.log(10.0) - 4.6051702 * jax.random.uniform(key_list[18], (2 * KV * HD,), jnp.float32) ** levels(key_list[18], (2 * KV * HD,), ((0, 32),), -0.2, 0.2)), 0.1, 10.0),
        "output_weight": normal_values(key_list[19], (H * HD, D), (H * HD // 64) ** -0.5, 1.25, ((0, 4), (1, 8)), jnp.float32),
        "output_weight_first": normal_values(key_list[20], (H * HD, D), 0.5, 3.0, ((0, 4), (1, 8)), jnp.float32),
        "output_weight_second": jnp.clip(jnp.exp(math.log(10.0) - 4.6051702 * jax.random.uniform(key_list[21], (H * HD, D), jnp.float32) ** levels(key_list[21], (H * HD, D), ((0, 4), (1, 8)), -0.2, 0.2)), 0.1, 10.0),
        "gateup_weight": normal_values(key_list[22], (D, 2, FF), D ** -0.5, 0.15625, ((0, 8), (2, 4)), jnp.float32),
        "gateup_weight_first": normal_values(key_list[23], (D, 2, FF), 0.5, 3.0, ((0, 8), (2, 4)), jnp.float32),
        "gateup_weight_second": jnp.clip(jnp.exp(math.log(10.0) - 4.6051702 * jax.random.uniform(key_list[24], (D, 2, FF), jnp.float32) ** levels(key_list[24], (D, 2, FF), ((0, 8), (2, 4)), -0.2, 0.2)), 0.1, 10.0),
        "down_weight": normal_values(key_list[25], (FF, D), FF ** -0.5, 0.0625, ((0, 4), (1, 8)), jnp.float32),
        "down_weight_first": normal_values(key_list[26], (FF, D), 0.5, 3.0, ((0, 4), (1, 8)), jnp.float32),
        "down_weight_second": jnp.clip(jnp.exp(math.log(10.0) - 4.6051702 * jax.random.uniform(key_list[27], (FF, D), jnp.float32) ** levels(key_list[27], (FF, D), ((0, 4), (1, 8)), -0.2, 0.2)), 0.1, 10.0),
    }


@jax.custom_vjp
def low(v):
    return lax.optimization_barrier(v.astype(jnp.bfloat16)).astype(jnp.float32)

@jax.custom_vjp
def low_back(v):
    return v

def low_keep(v):
    return (low(v), None)

def low_pass(kept, grad):
    return (grad,)

def back_keep(v):
    return (v, None)

def back_low(kept, grad):
    return (low(grad),)
low.defvjp(low_keep, low_pass)
low_back.defvjp(back_keep, back_low)
norm_eps = 1e-06
rope_base = 1000000.0
beta_first = 0.9
beta_second = 0.95
adam_eps = 1e-08
decay_rate = 0.1
first_fix = 1.0 - 0.9 ** 10
second_fix = 1.0 - 0.95 ** 10
masked_score = -1e+30

def matmul(left, right):
    return jnp.dot(left, right, precision=lax.Precision.HIGHEST, preferred_element_type=jnp.float32)

def rotate(values, positions, sign):
    half = values.shape[-1] // 2
    freqs = rope_base ** (-2.0 * jnp.arange(half, dtype=jnp.float32) / values.shape[-1])
    angles = positions.astype(jnp.float32)[:, None] * freqs[None, :]
    cosine = jnp.cos(angles)[:, None, :]
    sine = sign * jnp.sin(angles)[:, None, :]
    first = values[..., :half]
    second = values[..., half:]
    return jnp.concatenate([first * cosine - second * sine, second * cosine + first * sine], axis=-1)

def head_attention(query, key, value, segments):
    scores = low_back(matmul(query, key.T))
    order = jnp.arange(query.shape[0], dtype=jnp.int32)
    allowed = (segments[:, None] == segments[None, :]) & (order[None, :] <= order[:, None])
    probs = jax.nn.softmax(jnp.where(allowed, scores, masked_score), axis=-1)
    return matmul(low(probs), value)

def row_attention(carry, row):
    query, key, value, segments = row
    checked = jax.checkpoint(head_attention)
    heads = lax.map(lambda item: checked(item[0], item[1], item[2], segments), (query, key, value))
    return (carry, heads)

def forward(input_float, norm_gains, query_weight, query_bias, keyvalue_weight, keyvalue_bias, output_weight, gateup_weight, down_weight, segment_ids, positions):
    tokens = input_float.shape[0]
    rows = tokens // LENGTH
    w_gains = low(norm_gains)
    w_query = low(query_weight)
    b_query = low(query_bias)
    w_keyvalue = low(keyvalue_weight)
    b_keyvalue = low(keyvalue_bias)
    w_output = low(output_weight)
    w_gateup = low(gateup_weight)
    w_down = low(down_weight)
    inverse_one = lax.rsqrt(lax.optimization_barrier(jnp.mean(input_float * input_float, axis=-1, keepdims=True)) + norm_eps)
    unit_one = input_float * inverse_one
    normed_one = low(unit_one * w_gains[0])
    query = low_back(matmul(normed_one, w_query) + b_query.reshape(-1))
    pair = low_back(matmul(normed_one, w_keyvalue) + b_keyvalue)
    queries = low(rotate(query.reshape(tokens, H, HD), positions, 1.0) * HD ** (-0.5))
    keys = low(rotate(pair[:, :KV * HD].reshape(tokens, KV, HD), positions, 1.0))
    values = low(pair[:, KV * HD:].reshape(tokens, KV, HD))
    keys = jnp.repeat(keys, H // KV, axis=1)
    values = jnp.repeat(values, H // KV, axis=1)

    def arrange(block):
        return block.reshape(rows, LENGTH, H, HD).transpose(0, 2, 1, 3)
    unused, heads = lax.scan(row_attention, jnp.zeros((), jnp.float32), (arrange(queries), arrange(keys), arrange(values), segment_ids.reshape(rows, LENGTH)))
    attention = low_back(low(heads.transpose(0, 2, 1, 3).reshape(tokens, H * HD)))
    residual = input_float + low_back(matmul(attention, w_output))
    inverse_two = lax.rsqrt(lax.optimization_barrier(jnp.mean(residual * residual, axis=-1, keepdims=True)) + norm_eps)
    unit_two = residual * inverse_two
    normed_two = low(unit_two * w_gains[1])
    gate_up = matmul(normed_two, w_gateup.reshape(D, 2 * FF))
    gate = low_back(gate_up[:, :FF])
    upward = low_back(gate_up[:, FF:])
    hidden = low(jax.nn.silu(gate) * upward)
    return residual + low_back(matmul(hidden, w_down))

def adam_update(grad, master, first, second, decay, count):
    mean_grad = grad / count
    first_new = beta_first * first + (1.0 - beta_first) * mean_grad
    second_new = beta_second * second + (1.0 - beta_second) * mean_grad * mean_grad
    update = first_new / first_fix / (jnp.sqrt(second_new / second_fix) + adam_eps)
    if decay:
        update = update + decay_rate * master
    return (grad, update)

def reference(layer_input, grad_out, segment_ids, positions, norm_gains, norm_gains_first, norm_gains_second, query_weight, query_weight_first, query_weight_second, query_bias, query_bias_first, query_bias_second, keyvalue_weight, keyvalue_weight_first, keyvalue_weight_second, keyvalue_bias, keyvalue_bias_first, keyvalue_bias_second, output_weight, output_weight_first, output_weight_second, gateup_weight, gateup_weight_first, gateup_weight_second, down_weight, down_weight_first, down_weight_second):
    masters = (norm_gains, query_weight, query_bias, keyvalue_weight, keyvalue_bias, output_weight, gateup_weight, down_weight)

    def run(input_float, *weights):
        return forward(input_float, *weights, segment_ids, positions)
    result, pull = jax.vjp(run, layer_input.astype(jnp.float32), *masters)
    grads = pull(grad_out.astype(jnp.float32))
    layer_output = result.astype(jnp.bfloat16)
    input_grad = grads[0].astype(jnp.bfloat16)
    count = float(TOKENS)
    gains_update = adam_update(grads[1], norm_gains, norm_gains_first, norm_gains_second, False, count)
    query_update = adam_update(grads[2], query_weight, query_weight_first, query_weight_second, True, count)
    qbias_update = adam_update(grads[3], query_bias, query_bias_first, query_bias_second, False, count)
    keyvalue_update = adam_update(grads[4], keyvalue_weight, keyvalue_weight_first, keyvalue_weight_second, True, count)
    kvbias_update = adam_update(grads[5], keyvalue_bias, keyvalue_bias_first, keyvalue_bias_second, False, count)
    output_update = adam_update(grads[6], output_weight, output_weight_first, output_weight_second, True, count)
    gateup_update = adam_update(grads[7], gateup_weight, gateup_weight_first, gateup_weight_second, True, count)
    down_update = adam_update(grads[8], down_weight, down_weight_first, down_weight_second, True, count)
    return (layer_output, input_grad, *gains_update, *query_update, *qbias_update, *keyvalue_update, *kvbias_update, *output_update, *gateup_update, *down_update)
```

```python
import jax
import jax.numpy as jnp
from jax import lax
from jax.experimental import pallas as pl
from jax.experimental.pallas import tpu as pltpu
from jax.sharding import Mesh
from jax.sharding import PartitionSpec as P

D = 1536
H = 12
KV = 2
HD = 128
LENGTH = 4096
LANES = 128

norm_eps = 1e-06
rope_base = 1000000.0
beta_first = 0.9
beta_second = 0.95
adam_eps = 1e-08
decay_rate = 0.1
first_fix = 1.0 - 0.9**10
second_fix = 1.0 - 0.95**10
masked_score = -1e30

WIDE = ("hi", "lo", "x")
NARROW = ("y", "c")
BLOCK_Q = 256
BLOCK_K = 512


def low(a):
    return a.astype(jnp.bfloat16)


def wide_float(a):
    return a.astype(jnp.float32)


def matmul(left, right):
    return jnp.dot(left, right, preferred_element_type=jnp.float32)


def matmul_nt(left, right):
    return lax.dot_general(left, right, (((1,), (1,)), ((), ())), preferred_element_type=jnp.float32)


def matmul_tn(left, right):
    return lax.dot_general(left, right, (((0,), (0,)), ((), ())), preferred_element_type=jnp.float32)


def swap(block, axis, distance=1):
    size = 1
    for name in axis if isinstance(axis, tuple) else (axis,):
        size *= lax.axis_size(name)
    return lax.ppermute(block, axis, [(i, i ^ distance) for i in range(size)])


def pick(stacked, index):
    return lax.dynamic_index_in_dim(stacked, index, axis=0, keepdims=False)


def pair(mine, other, index):
    return jnp.where(index == 0, jnp.stack([mine, other]), jnp.stack([other, mine]))


def place_blocks(blocks):
    lead = tuple(blocks[0][2])
    tail = blocks[0][0].shape
    full = jnp.zeros(lead + tail, blocks[0][0].dtype)
    for block, index, _ in blocks:
        start = tuple(index) + (0,) * len(tail)
        full = lax.dynamic_update_slice(full, block.reshape((1,) * len(lead) + tail), start)
    return full


def gather_wide(block):
    hi, lo, x = (lax.axis_index(name) for name in WIDE)
    count = lax.axis_size("hi")
    both = pair(block, swap(block, "lo"), lo)
    lead = (count, 2)
    columns = [both] + [swap(both, "hi", d) for d in range(1, count)]
    placed = []
    for d, column in enumerate(columns):
        other = swap(column, "x")
        for at, part in ((x, column), (1 - x, other)):
            placed.append((part, hi ^ d, at))
    full = jnp.zeros((count, 2, 2) + block.shape, block.dtype)
    for part, at_hi, at_x in placed:
        full = lax.dynamic_update_slice(
            full, part[None, :, None], (at_hi, 0, at_x) + (0,) * block.ndim
        )
    return full.reshape((count * 4,) + block.shape)


def scatter_wide(parts):
    hi, lo, x = (lax.axis_index(name) for name in WIDE)
    count = lax.axis_size("hi")
    shape = parts.shape[1:]
    parts = parts.reshape((count, 2, 2) + shape)
    kept = lax.dynamic_index_in_dim(parts, x, axis=2, keepdims=False)
    sent = lax.dynamic_index_in_dim(parts, 1 - x, axis=2, keepdims=False)
    parts = low(wide_float(kept) + wide_float(swap(sent, "x")))
    total = wide_float(pick(parts, hi))
    for d in range(1, count):
        total = total + wide_float(swap(pick(parts, hi ^ d), "hi", d))
    kept, sent = pick(total, lo), low(pick(total, 1 - lo))
    return kept + wide_float(swap(sent, "lo"))


def gather_hidden(shard):
    hi, lo, x = (lax.axis_index(name) for name in WIDE)
    count = lax.axis_size("hi")
    rows, half = shard.shape[0], shard.shape[1] // 2
    mine = lax.dynamic_slice_in_dim(shard, lo * half, half, axis=1)
    sent = lax.dynamic_slice_in_dim(shard, (1 - lo) * half, half, axis=1)
    both = pair(mine, swap(sent, "lo"), lo)
    columns = [both] + [swap(both, "hi", d) for d in range(1, count)]
    full = jnp.zeros((count, 2, 2, rows, half), shard.dtype)
    for d, column in enumerate(columns):
        for at_x, part in ((x, column), (1 - x, swap(column, "x"))):
            full = lax.dynamic_update_slice(full, part[None, :, None], (hi ^ d, 0, at_x, 0, 0))
    return full.reshape(count * 4 * rows, half)


def scatter_hidden(grad):
    hi, lo, x = (lax.axis_index(name) for name in WIDE)
    count = lax.axis_size("hi")
    rows, half = grad.shape[0] // (count * 4), grad.shape[1]
    parts = grad.reshape(count, 2, 2, rows, half)
    kept = lax.dynamic_index_in_dim(parts, x, axis=2, keepdims=False)
    sent = lax.dynamic_index_in_dim(parts, 1 - x, axis=2, keepdims=False)
    parts = low(wide_float(kept) + wide_float(swap(sent, "x")))
    total = wide_float(pick(parts, hi))
    for d in range(1, count):
        total = total + wide_float(swap(pick(parts, hi ^ d), "hi", d))
    total = low(total)
    mine, other = pick(total, lo), swap(pick(total, 1 - lo), "lo")
    first = jnp.where(lo == 0, mine, other)
    second = jnp.where(lo == 0, other, mine)
    return wide_float(jnp.concatenate([first, second], axis=1))


def exchange_narrow(blocks):
    y, c = (lax.axis_index(name) for name in NARROW)
    shape = blocks.shape[2:]
    flat = blocks.reshape((4,) + shape)
    me = y * 2 + c
    got = [pick(flat, me)] + [swap(pick(flat, me ^ d), NARROW, d) for d in range(1, 4)]
    near, far = pair(got[0], got[1], c), pair(got[2], got[3], c)
    return pair(near, far, y)


def gather_tokens(block):
    y, c = (lax.axis_index(name) for name in NARROW)
    both = pair(block, swap(block, "y"), y)
    both = both.reshape((-1,) + block.shape[1:])
    every = pair(both, swap(both, "c"), c)
    return every.reshape((-1,) + block.shape[1:])


def rotation(positions):
    half = HD // 2
    freqs = rope_base ** (-2.0 * jnp.arange(half, dtype=jnp.float32) / HD)
    angles = positions.astype(jnp.float32)[:, None] * freqs[None, :]
    return jnp.cos(angles)[:, None, :], jnp.sin(angles)[:, None, :]


def rotate(values, cosine, sine):
    half = values.shape[-1] // 2
    first = values[..., :half]
    second = values[..., half:]
    return jnp.concatenate(
        [first * cosine - second * sine, second * cosine + first * sine], axis=-1
    )


def rms_back(grad_unit, unit, inverse):
    return inverse * (grad_unit - unit * jnp.mean(grad_unit * unit, axis=-1, keepdims=True))


def adam_update(grad, master, first, second, decay, count):
    mean_grad = grad / count
    first_new = beta_first * first + (1.0 - beta_first) * mean_grad
    second_new = beta_second * second + (1.0 - beta_second) * mean_grad * mean_grad
    update = first_new / first_fix / (jnp.sqrt(second_new / second_fix) + adam_eps)
    if decay:
        update = update + decay_rate * master
    return (grad, update)


def stacked_heads(ref, heads):
    return jnp.concatenate([ref[:, h * HD : (h + 1) * HD] for h in range(heads)], axis=0)


def attention_forward(queries, keys, values, begins, starts, place):
    tokens, columns = queries.shape
    heads = columns // HD
    length = keys.shape[0]
    rows = heads * BLOCK_Q

    def kernel(starts_ref, place_ref, q_ref, k_ref, v_ref, begin_ref, o_ref, lse_ref):
        step = pl.program_id(0)
        base = place_ref[0] * tokens + step * BLOCK_Q
        q = stacked_heads(q_ref, heads)
        row = base + lax.broadcasted_iota(jnp.int32, (BLOCK_Q, 1), 0)
        row = jnp.concatenate([row] * heads, axis=0)
        begin = jnp.concatenate([begin_ref[...]] * heads, axis=0)

        def body(j, carry):
            top, total, acc = carry
            at = pl.multiple_of(j * BLOCK_K, BLOCK_K)
            k = k_ref[pl.ds(at, BLOCK_K), :]
            v = v_ref[pl.ds(at, BLOCK_K), :]
            s = matmul_nt(q, k)
            col = at + lax.broadcasted_iota(jnp.int32, (1, BLOCK_K), 1)
            s = jnp.where((col <= row) & (col >= begin), s, masked_score)
            new_top = jnp.maximum(top, jnp.max(s, axis=1, keepdims=True))
            p = jnp.exp(s - new_top)
            scale = jnp.exp(top - new_top)
            total = scale * total + jnp.sum(p, axis=1, keepdims=True)
            acc = scale * acc + matmul(low(p), v)
            return new_top, total, acc

        first = starts_ref[step] // BLOCK_K
        last = (base + BLOCK_Q - 1) // BLOCK_K
        top, total, acc = lax.fori_loop(
            first,
            last + 1,
            body,
            (
                jnp.full((rows, 1), masked_score, jnp.float32),
                jnp.zeros((rows, 1), jnp.float32),
                jnp.zeros((rows, HD), jnp.float32),
            ),
        )
        out = acc / total
        for h in range(heads):
            o_ref[:, h * HD : (h + 1) * HD] = out[h * BLOCK_Q : (h + 1) * BLOCK_Q]
        lse_ref[...] = (top + jnp.log(total)).reshape(heads, BLOCK_Q, 1)

    block = pl.BlockSpec((BLOCK_Q, columns), lambda i, *_: (i, 0))
    whole = pl.BlockSpec((length, HD), lambda i, *_: (0, 0))
    return pl.pallas_call(
        kernel,
        grid_spec=pltpu.PrefetchScalarGridSpec(
            num_scalar_prefetch=2,
            grid=(tokens // BLOCK_Q,),
            in_specs=[block, whole, whole, pl.BlockSpec((BLOCK_Q, 1), lambda i, *_: (i, 0))],
            out_specs=[block, pl.BlockSpec((heads, BLOCK_Q, 1), lambda i, *_: (0, i, 0))],
        ),
        out_shape=[
            jax.ShapeDtypeStruct((tokens, columns), jnp.float32),
            jax.ShapeDtypeStruct((heads, tokens, 1), jnp.float32),
        ],
        compiler_params=pltpu.CompilerParams(dimension_semantics=("arbitrary",)),
        name="attention_forward",
    )(starts, place, queries, keys, values, begins)


def attention_backward(queries, keys, values, begins, starts, place, grads, lse, outputs):
    tokens, columns = queries.shape
    heads = columns // HD
    length = keys.shape[0]
    rows = heads * BLOCK_Q

    def kernel(
        starts_ref, place_ref, q_ref, k_ref, v_ref, begin_ref, g_ref, lse_ref, o_ref,
        dq_ref, dk_ref, dv_ref,
    ):
        step = pl.program_id(0)

        @pl.when(step == 0)
        def _():
            dk_ref[...] = jnp.zeros_like(dk_ref)
            dv_ref[...] = jnp.zeros_like(dv_ref)

        base = place_ref[0] * tokens + step * BLOCK_Q
        q = stacked_heads(q_ref, heads)
        g = stacked_heads(g_ref, heads)
        delta = jnp.sum(wide_float(g) * stacked_heads(o_ref, heads), axis=1, keepdims=True)
        lse = lse_ref[...].reshape(rows, 1)
        row = base + lax.broadcasted_iota(jnp.int32, (BLOCK_Q, 1), 0)
        row = jnp.concatenate([row] * heads, axis=0)
        begin = jnp.concatenate([begin_ref[...]] * heads, axis=0)

        def body(j, dq):
            at = pl.multiple_of(j * BLOCK_K, BLOCK_K)
            k = k_ref[pl.ds(at, BLOCK_K), :]
            v = v_ref[pl.ds(at, BLOCK_K), :]
            col = at + lax.broadcasted_iota(jnp.int32, (1, BLOCK_K), 1)
            s = jnp.where((col <= row) & (col >= begin), matmul_nt(q, k), masked_score)
            p = jnp.exp(s - lse)
            dp = matmul_nt(g, v)
            ds = low(p * (dp - delta))
            dk_ref[pl.ds(at, BLOCK_K), :] += matmul_tn(ds, q)
            dv_ref[pl.ds(at, BLOCK_K), :] += matmul_tn(low(p), g)
            return dq + matmul(ds, k)

        first = starts_ref[step] // BLOCK_K
        last = (base + BLOCK_Q - 1) // BLOCK_K
        dq = lax.fori_loop(first, last + 1, body, jnp.zeros((rows, HD), jnp.float32))
        for h in range(heads):
            dq_ref[:, h * HD : (h + 1) * HD] = dq[h * BLOCK_Q : (h + 1) * BLOCK_Q]

    block = pl.BlockSpec((BLOCK_Q, columns), lambda i, *_: (i, 0))
    whole = pl.BlockSpec((length, HD), lambda i, *_: (0, 0))
    return pl.pallas_call(
        kernel,
        grid_spec=pltpu.PrefetchScalarGridSpec(
            num_scalar_prefetch=2,
            grid=(tokens // BLOCK_Q,),
            in_specs=[
                block,
                whole,
                whole,
                pl.BlockSpec((BLOCK_Q, 1), lambda i, *_: (i, 0)),
                block,
                pl.BlockSpec((heads, BLOCK_Q, 1), lambda i, *_: (0, i, 0)),
                block,
            ],
            out_specs=[block, whole, whole],
        ),
        out_shape=[
            jax.ShapeDtypeStruct((tokens, columns), jnp.float32),
            jax.ShapeDtypeStruct((length, HD), jnp.float32),
            jax.ShapeDtypeStruct((length, HD), jnp.float32),
        ],
        compiler_params=pltpu.CompilerParams(dimension_semantics=("arbitrary",)),
        name="attention_backward",
    )(starts, place, queries, keys, values, begins, grads, lse, outputs)


def local(
    layer_input,
    grad_out,
    segment_ids,
    positions,
    norm_gains,
    norm_gains_first,
    norm_gains_second,
    query_weight,
    query_weight_first,
    query_weight_second,
    query_bias,
    query_bias_first,
    query_bias_second,
    keyvalue_weight,
    keyvalue_weight_first,
    keyvalue_weight_second,
    keyvalue_bias,
    keyvalue_bias_first,
    keyvalue_bias_second,
    output_weight,
    output_weight_first,
    output_weight_second,
    gateup_weight,
    gateup_weight_first,
    gateup_weight_second,
    down_weight,
    down_weight_first,
    down_weight_second,
):
    hi, lo, x, y, c = (lax.axis_index(name) for name in WIDE + NARROW)
    wide = lax.axis_size("hi") * 4
    tokens = layer_input.shape[0]
    quarter = tokens // 4
    heads = query_bias.shape[0]
    head_scale = HD ** (-0.5)
    token_count = float(tokens * wide)
    rows = D // wide
    narrow_rows = rows // 4
    bias_part = query_bias.shape[1]
    kv_part = keyvalue_bias.shape[0]
    column_block = c * KV + y
    hidden = gateup_weight.shape[2]
    half = -(-hidden // (2 * LANES)) * LANES
    padding = 2 * half - hidden
    own = c * 2 + y

    kv_columns = low(keyvalue_weight).reshape(narrow_rows, 2, KV, HD)
    kv_columns = jnp.transpose(kv_columns, (2, 1, 0, 3))
    small = jnp.concatenate([low(norm_gains).reshape(-1), low(keyvalue_bias)])
    small = jnp.pad(small, (0, HD - small.shape[0])).reshape(1, 1, 1, HD)
    small = jnp.pad(small, ((0, 0), (0, 0), (0, 15), (0, 0)))
    blocks = jnp.concatenate([kv_columns, jnp.broadcast_to(small, (2, 2, 16, HD))], axis=2)
    blocks = exchange_narrow(blocks).reshape(4, narrow_rows + 16, HD)
    kv_mine = blocks[:, :narrow_rows].reshape(rows, HD)
    small_row = blocks[:, narrow_rows].reshape(1, 4 * HD)
    bias_row = jnp.pad(low(query_bias).reshape(1, -1), ((0, 0), (0, 4 * HD - heads * bias_part)))
    extra = jnp.pad(jnp.concatenate([small_row, bias_row]), ((0, 14), (0, 0)))
    packed = jnp.concatenate(
        [jnp.concatenate([low(query_weight), kv_mine], axis=1), extra], axis=0
    )
    packed = gather_wide(packed)
    w_qkv = packed[:, :rows].reshape(D, 4 * HD)
    small_all = wide_float(packed[:, rows]).reshape(wide, 4, HD)
    gains = small_all[:, :, : 2 * narrow_rows].reshape(wide, 4, 2, narrow_rows)
    gains = jnp.transpose(gains, (2, 0, 1, 3)).reshape(2, D)
    b_kv = small_all[:, :, 2 * narrow_rows : 2 * narrow_rows + kv_part].reshape(2 * KV, HD)
    b_query = wide_float(packed[:, rows + 1, : heads * bias_part]).reshape(wide, heads, bias_part)
    b_query = jnp.transpose(b_query, (1, 0, 2)).reshape(heads * HD)
    b_qkv = jnp.concatenate([b_query, pick(b_kv, column_block)])
    gain_one, gain_two = gains[0], gains[1]

    w_output = gather_wide(low(output_weight).T)
    w_output = w_output.reshape(D, heads * HD)

    def padded(shard):
        return jnp.pad(low(shard), ((0, 0), (0, padding)))

    w_gate = gather_hidden(padded(gateup_weight[:, 0]))
    w_up = gather_hidden(padded(gateup_weight[:, 1]))
    w_down = gather_hidden(padded(down_weight.T))

    input_float = wide_float(layer_input)
    inverse_one = lax.rsqrt(jnp.mean(input_float * input_float, axis=-1, keepdims=True) + norm_eps)
    normed_one = low(input_float * inverse_one * gain_one)
    linear = (matmul(normed_one, w_qkv) + b_qkv).reshape(tokens, 4, HD)
    cosine, sine = rotation(positions)
    kv_cosine = jnp.where(c == 0, cosine, 1.0)
    kv_sine = jnp.where(c == 0, sine, 0.0)
    queries = low(rotate(linear[:, :heads], cosine, sine) * head_scale).reshape(tokens, heads * HD)
    kv_own = low(rotate(linear[:, heads:], kv_cosine, kv_sine)).reshape(tokens, HD)
    both = pair(kv_own, swap(kv_own, "x"), x)
    kv_row = pair(both, swap(both, "lo"), lo).reshape(4 * tokens, HD)
    kv_other = swap(kv_row, "c")
    keys = jnp.where(c == 0, kv_row, kv_other)
    values = jnp.where(c == 0, kv_other, kv_row)
    begins = segment_ids - hi * (4 * tokens)
    starts = begins[::BLOCK_Q]
    begins = begins[:, None]
    place = (lo * 2 + x).reshape(1).astype(jnp.int32)
    attention, log_total = attention_forward(queries, keys, values, begins, starts, place)
    attention_low = low(attention)

    def halves(block):
        split = block.reshape(2, -1, block.shape[-1])
        return pick(split, c), pick(split, 1 - c)

    def scatter_narrow(kept, sent):
        total = (kept + wide_float(swap(low(sent), "c"))).reshape(2, quarter, D)
        return pick(total, y) + wide_float(swap(low(pick(total, 1 - y)), "y"))

    attention_kept, attention_sent = halves(attention_low)
    sent = matmul_nt(attention_sent, w_output)
    attention_out = scatter_narrow(matmul_nt(attention_kept, w_output), sent)
    residual = wide_float(pick(layer_input.reshape(4, quarter, D), own)) + attention_out
    inverse_two = lax.rsqrt(jnp.mean(residual * residual, axis=-1, keepdims=True) + norm_eps)
    unit_two = residual * inverse_two
    normed_two = low(unit_two * gain_two)

    by_y = swap(normed_two, "y")
    by_lo = swap(normed_two, "lo")
    by_both = swap(by_y, "lo")
    core_tokens = jnp.concatenate([normed_two, by_y, by_lo, by_both])
    ff_input = jnp.concatenate([core_tokens, swap(core_tokens, "c")])
    grad_blocks = grad_out.reshape(4, quarter, D)
    grad_own = pick(grad_blocks, own)
    grad_near = jnp.concatenate([grad_own, pick(grad_blocks, c * 2 + 1 - y)])
    grad_far = swap(grad_near, "lo")
    grad_core = jnp.concatenate(
        [pick(grad_blocks, (1 - c) * 2 + y), pick(grad_blocks, (1 - c) * 2 + 1 - y)]
    )
    ff_grad = jnp.concatenate([grad_near, grad_far, grad_core, swap(grad_far, "c")])

    gate = matmul(ff_input, w_gate)
    upward = matmul(ff_input, w_up)
    grad_hidden = matmul(ff_grad, w_down)
    logistic = jax.nn.sigmoid(gate)
    active = gate * logistic
    hidden_low = low(active * upward)
    grad_gate = low(grad_hidden * upward * logistic * (1.0 + gate * (1.0 - logistic)))
    grad_upward = low(grad_hidden * active)

    def scatter_group(kept, sent):
        total = kept + wide_float(swap(low(sent), "c"))
        total = total.reshape(2, 2, quarter, D)
        total = total[:, 0] + wide_float(swap(low(total[:, 1]), "y"))
        return total[0] + wide_float(swap(low(total[1]), "lo"))

    count = 4 * quarter

    def feed_back(at):
        part = slice(at * count, (at + 1) * count)
        return matmul_nt(grad_gate[part], w_gate) + matmul_nt(grad_upward[part], w_up)

    grad_sent = feed_back(1)
    grad_normed_two = scatter_group(feed_back(0), grad_sent)
    grad_residual = wide_float(grad_own) + rms_back(
        grad_normed_two * gain_two, unit_two, inverse_two
    )
    residual_low = gather_tokens(low(grad_residual))

    mlp_sent = matmul_nt(hidden_low[count:], w_down)
    mlp_out = scatter_group(matmul_nt(hidden_low[:count], w_down), mlp_sent)
    layer_output = gather_tokens(low(residual + mlp_out))

    summed_down = scatter_hidden(low(matmul_tn(ff_grad, hidden_low)))
    summed_gate = scatter_hidden(low(matmul_tn(ff_input, grad_gate)))
    summed_up = scatter_hidden(low(matmul_tn(ff_input, grad_upward)))

    grad_attention = low(matmul(residual_low, w_output))
    summed_output = scatter_wide(
        low(matmul_tn(residual_low, attention_low)).reshape(wide, rows, heads * HD)
    )
    grad_queries, grad_keys, grad_values = attention_backward(
        queries, keys, values, begins, starts, place, grad_attention, log_total, attention
    )
    kv_sent = low(jnp.where(c == 0, grad_values, grad_keys))
    kv_grad = jnp.where(c == 0, grad_keys, grad_values) + wide_float(swap(kv_sent, "c"))
    kv_grad = kv_grad.reshape(2, 2 * tokens, HD)
    kv_grad = pick(kv_grad, lo) + wide_float(swap(low(pick(kv_grad, 1 - lo)), "lo"))
    kv_grad = kv_grad.reshape(2, tokens, HD)
    kv_grad = pick(kv_grad, x) + wide_float(swap(low(pick(kv_grad, 1 - x)), "x"))
    kv_grad = rotate(kv_grad[:, None], kv_cosine, -kv_sine)
    query_grad = rotate(
        grad_queries.reshape(tokens, heads, HD) * head_scale, cosine, -sine
    )
    grad_linear = low(jnp.concatenate([query_grad, kv_grad], axis=1)).reshape(tokens, 4 * HD)

    linear_kept, linear_sent = halves(grad_linear)
    part_sent = matmul_nt(linear_sent, w_qkv)
    grad_normed_one = scatter_narrow(matmul_nt(linear_kept, w_qkv), part_sent)
    own_input = wide_float(pick(layer_input.reshape(4, quarter, D), own))
    own_inverse = lax.rsqrt(jnp.mean(own_input * own_input, axis=-1, keepdims=True) + norm_eps)
    input_grad = gather_tokens(
        low(
            grad_residual
            + rms_back(grad_normed_one * gain_one, own_input * own_inverse, own_inverse)
        )
    )

    grad_qkv = low(matmul_tn(normed_one, grad_linear)).reshape(wide, rows, 4 * HD)
    bias_sums = jnp.sum(wide_float(grad_linear), axis=0).reshape(4, HD)
    bias_query = jnp.transpose(bias_sums[:heads].reshape(heads, wide, bias_part), (1, 0, 2))
    bias_query = bias_query.reshape(wide, heads * bias_part)
    bias_kv = lax.dynamic_update_slice(
        jnp.zeros((2 * KV, HD), jnp.float32), bias_sums[heads:], (column_block, 0)
    ).reshape(wide, 4 * kv_part)
    bias_all = jnp.concatenate([bias_query, bias_kv], axis=1)
    bias_all = jnp.pad(bias_all, ((0, 0), (0, 4 * HD - bias_all.shape[1])))
    extra = jnp.pad(low(bias_all)[:, None], ((0, 0), (0, 15), (0, 0)))
    summed = scatter_wide(jnp.concatenate([grad_qkv, extra], axis=1))
    summed_query = summed[:rows, : heads * HD]
    summed_kv = summed[:rows, heads * HD :]
    summed_query_bias = summed[rows, : heads * bias_part].reshape(heads, bias_part)
    kv_bias = summed[rows, heads * bias_part : heads * bias_part + 4 * kv_part]

    my_gains = lax.dynamic_slice_in_dim(gains, (hi * 4 + lo * 2 + x) * rows, rows, axis=1)
    my_w = wide_float(lax.dynamic_slice_in_dim(w_qkv, (hi * 4 + lo * 2 + x) * rows, rows, axis=0))
    grad_gain_one = jnp.sum(summed[:rows] * my_w, axis=1) / my_gains[0]
    summed_gateup = jnp.stack([summed_gate[:, :hidden], summed_up[:, :hidden]], axis=1)
    grad_gain_two = (
        jnp.sum(summed_gateup * wide_float(low(gateup_weight)), axis=(1, 2)) / my_gains[1]
    )
    gain_parts = jnp.stack([grad_gain_one, grad_gain_two]).reshape(2, 4, narrow_rows)
    gain_parts = jnp.transpose(gain_parts, (1, 0, 2)).reshape(4, 2 * narrow_rows)
    last = jnp.concatenate([gain_parts, kv_bias.reshape(4, kv_part)], axis=1)
    last = jnp.pad(last, ((0, 0), (0, HD - last.shape[1])))[:, None]
    last = jnp.pad(last, ((0, 0), (0, 7), (0, 0)))
    last = jnp.concatenate([summed_kv.reshape(4, narrow_rows, HD), last], axis=1)
    last = exchange_narrow(last.reshape((2, 2) + last.shape[1:]))
    summed_keyvalue = jnp.transpose(last[:, :, :narrow_rows], (2, 1, 0, 3))
    summed_keyvalue = summed_keyvalue.reshape(narrow_rows, 2 * KV * HD)
    small_sums = jnp.sum(last[:, :, narrow_rows], axis=(0, 1))
    summed_gains = small_sums[: 2 * narrow_rows].reshape(2, narrow_rows)
    summed_keyvalue_bias = small_sums[2 * narrow_rows : 2 * narrow_rows + kv_part]
    summed_down = summed_down[:, :hidden].T
    summed_output = summed_output.T

    gains_update = adam_update(
        summed_gains, norm_gains, norm_gains_first, norm_gains_second, False, token_count
    )
    query_update = adam_update(
        summed_query, query_weight, query_weight_first, query_weight_second, True, token_count
    )
    qbias_update = adam_update(
        summed_query_bias, query_bias, query_bias_first, query_bias_second, False, token_count
    )
    keyvalue_update = adam_update(
        summed_keyvalue,
        keyvalue_weight,
        keyvalue_weight_first,
        keyvalue_weight_second,
        True,
        token_count,
    )
    kvbias_update = adam_update(
        summed_keyvalue_bias,
        keyvalue_bias,
        keyvalue_bias_first,
        keyvalue_bias_second,
        False,
        token_count,
    )
    output_update = adam_update(
        summed_output, output_weight, output_weight_first, output_weight_second, True, token_count
    )
    gateup_update = adam_update(
        summed_gateup, gateup_weight, gateup_weight_first, gateup_weight_second, True, token_count
    )
    down_update = adam_update(
        summed_down, down_weight, down_weight_first, down_weight_second, True, token_count
    )
    return (
        layer_output,
        input_grad,
        *gains_update,
        *query_update,
        *qbias_update,
        *keyvalue_update,
        *kvbias_update,
        *output_update,
        *gateup_update,
        *down_update,
    )


def solution(mesh):
    devices = mesh.devices.reshape(-1, 2, 2, 2, 2)
    split = Mesh(devices, WIDE + NARROW)
    token_matrix = P(WIDE, None)
    token_vector = P(WIDE)
    gains = P(None, WIDE + NARROW)
    query = P(WIDE, NARROW)
    by_narrow = P(NARROW, WIDE)
    keyvalue = P(WIDE + NARROW, None)
    keyvalue_bias = P(WIDE + NARROW)
    gateup = P(WIDE, None, NARROW)
    parameters = (gains, query, by_narrow, keyvalue, keyvalue_bias, by_narrow, gateup, by_narrow)
    in_specs = (token_matrix, token_matrix, token_vector, token_vector)
    out_specs = (token_matrix, token_matrix)
    for spec in parameters:
        in_specs += (spec,) * 3
        out_specs += (spec,) * 2
    return jax.shard_map(local, mesh=split, in_specs=in_specs, out_specs=out_specs, check_vma=False)
```

```python
import jax
import jax.numpy as jnp
from jax import lax
from jax.experimental import pallas as pl
from jax.experimental.pallas import tpu as pltpu
from jax.sharding import Mesh
from jax.sharding import PartitionSpec as P

D = 1536
H = 12
KV = 2
HD = 128
LENGTH = 4096
LANES = 128

norm_eps = 1e-06
rope_base = 1000000.0
beta_first = 0.9
beta_second = 0.95
adam_eps = 1e-08
decay_rate = 0.1
first_fix = 1.0 - 0.9**10
second_fix = 1.0 - 0.95**10
masked_score = -1e30

WIDE = ("hi", "lo", "x")
NARROW = ("y", "c")
BLOCK_Q = 256
BLOCK_K = 512


def low(a):
    return a.astype(jnp.bfloat16)


def wide_float(a):
    return a.astype(jnp.float32)


def matmul(left, right):
    return jnp.dot(left, right, preferred_element_type=jnp.float32)


def matmul_nt(left, right):
    return lax.dot_general(left, right, (((1,), (1,)), ((), ())), preferred_element_type=jnp.float32)


def matmul_tn(left, right):
    return lax.dot_general(left, right, (((0,), (0,)), ((), ())), preferred_element_type=jnp.float32)


def swap(block, axis, distance=1):
    size = 1
    for name in axis if isinstance(axis, tuple) else (axis,):
        size *= lax.axis_size(name)
    return lax.ppermute(block, axis, [(i, i ^ distance) for i in range(size)])


def pick(stacked, index):
    return lax.dynamic_index_in_dim(stacked, index, axis=0, keepdims=False)


def pair(mine, other, index):
    return jnp.where(index == 0, jnp.stack([mine, other]), jnp.stack([other, mine]))


def after(value, *needed):
    return lax.optimization_barrier((value, needed))[0]


def wide_columns(block, cut):
    lo = lax.axis_index("lo")
    count = lax.axis_size("hi")
    mine = [block] + [swap(block, "hi", d) for d in range(1, count)]
    other = [swap(part, "lo") for part in mine]
    left = [pair(m[:, :cut], o[:, :cut], lo) for m, o in zip(mine, other)]
    right = [pair(m[:, cut:], o[:, cut:], lo) for m, o in zip(mine, other)]
    return left, right


def stack_rows(blocks, slots, into=None, count=None):
    height, width = blocks[0].shape
    count = len(blocks) if count is None else count
    olds = [] if into is None else [into]

    def kernel(slot_ref, *refs):
        out_ref, sem = refs[-2:]
        copies = []
        for i, block_ref in enumerate(refs[: len(blocks)]):
            start = pl.multiple_of(slot_ref[i] * height, 16)
            copies.append(
                pltpu.make_async_copy(block_ref, out_ref.at[pl.ds(start, height), :], sem.at[i])
            )
        for copy in copies:
            copy.start()
        for copy in copies:
            copy.wait()

    anywhere = pl.BlockSpec(memory_space=pl.ANY)
    slots = jnp.stack([jnp.asarray(slot, jnp.int32) for slot in slots])
    return pl.pallas_call(
        kernel,
        in_specs=[pl.BlockSpec(memory_space=pltpu.SMEM)]
        + [pl.BlockSpec(memory_space=pltpu.VMEM)] * len(blocks)
        + [anywhere] * len(olds),
        out_specs=anywhere,
        out_shape=jax.ShapeDtypeStruct((count * height, width), blocks[0].dtype),
        scratch_shapes=[pltpu.SemaphoreType.DMA((len(blocks),))],
        input_output_aliases={len(blocks) + 1: 0} if olds else {},
        name="stack_rows",
    )(slots, *blocks, *olds)


def assemble(columns, others, rows):
    count = len(columns)
    _, height, width = columns[0].shape
    kind = columns[0].dtype

    def kernel(at_ref, *refs):
        main_ref, extra_ref = refs[-2:]
        for d in range(count):
            for k in range(2):
                part = refs[2 * d + k]
                for low_bit in range(2):
                    index = (at_ref[0] ^ d) * 4 + low_bit * 2 + (at_ref[1] ^ k)
                    start = pl.multiple_of(index * rows, 16)
                    main_ref[pl.ds(start, rows), :] = part[low_bit, :rows]
                    extra_ref[index] = part[low_bit, rows:]

    parts = [part for both in zip(columns, others) for part in both]
    at = jnp.stack([lax.axis_index("hi"), lax.axis_index("x")]).astype(jnp.int32)
    return pl.pallas_call(
        kernel,
        in_specs=[pl.BlockSpec(memory_space=pltpu.SMEM)]
        + [pl.BlockSpec(memory_space=pltpu.VMEM)] * len(parts),
        out_specs=[pl.BlockSpec(memory_space=pltpu.VMEM)] * 2,
        out_shape=[
            jax.ShapeDtypeStruct((count * 4 * rows, width), kind),
            jax.ShapeDtypeStruct((count * 4, height - rows, width), kind),
        ],
        name="assemble",
    )(at, *parts)


def send_x(parts):
    x = lax.axis_index("x")
    parts = parts.reshape((-1, 2, 2) + parts.shape[1:])
    kept = lax.dynamic_index_in_dim(parts, x, axis=2, keepdims=False)
    sent = lax.dynamic_index_in_dim(parts, 1 - x, axis=2, keepdims=False)
    return kept, swap(sent, "x")


def send_hi(parts):
    hi = lax.axis_index("hi")
    turns = range(1, lax.axis_size("hi"))
    return [pick(parts, hi)] + [swap(pick(parts, hi ^ d), "hi", d) for d in turns]


def send_lo(parts):
    lo = lax.axis_index("lo")
    return pick(parts, lo), swap(low(pick(parts, 1 - lo)), "lo")


def add_up(parts):
    return sum(wide_float(part) for part in parts)


def send_hidden(total):
    x = lax.axis_index("x")
    total = total.reshape((2, -1) + total.shape[1:])
    return pick(total, x), swap(pick(total, 1 - x), "x")


def join_hidden(mine, other):
    x = lax.axis_index("x")
    first = jnp.where(x == 0, mine, other)
    second = jnp.where(x == 0, other, mine)
    return wide_float(jnp.concatenate([first, second], axis=1))


def hidden_pair(shards):
    x = lax.axis_index("x")
    half = shards[0].shape[1] // 2

    def part(at):
        return jnp.concatenate(
            [lax.dynamic_slice_in_dim(shard, at * half, half, axis=1) for shard in shards], axis=1
        )

    both = pair(part(x), swap(part(1 - x), "x"), x)
    return both.reshape((-1,) + both.shape[2:])


def exchange_narrow(blocks):
    y, c = (lax.axis_index(name) for name in NARROW)
    shape = blocks.shape[2:]
    flat = blocks.reshape((4,) + shape)
    me = y * 2 + c
    got = [pick(flat, me)] + [swap(pick(flat, me ^ d), NARROW, d) for d in range(1, 4)]
    near, far = pair(got[0], got[1], c), pair(got[2], got[3], c)
    return pair(near, far, y)


def gather_tokens(block, *needed):
    y, c = (lax.axis_index(name) for name in NARROW)
    by_y = after(swap(block, "y"), *needed)
    own = c * 2 + y
    return stack_rows(
        [block, by_y, swap(block, "c"), swap(by_y, "c")], [own, own ^ 1, own ^ 2, own ^ 3]
    )


def rotation(positions):
    half = HD // 2
    freqs = rope_base ** (-2.0 * jnp.arange(half, dtype=jnp.float32) / HD)
    angles = positions.astype(jnp.float32)[:, None] * freqs[None, :]
    cosine, sine = jnp.cos(angles), jnp.sin(angles)
    return jnp.concatenate([cosine, cosine], axis=1), jnp.concatenate([-sine, sine], axis=1)


def rms_back(grad_unit, unit, inverse):
    return inverse * (grad_unit - unit * jnp.mean(grad_unit * unit, axis=-1, keepdims=True))


def adam_update(grad, master, first, second, decay, count):
    mean_grad = grad / count
    first_new = beta_first * first + (1.0 - beta_first) * mean_grad
    second_new = beta_second * second + (1.0 - beta_second) * mean_grad * mean_grad
    update = first_new / first_fix / (jnp.sqrt(second_new / second_fix) + adam_eps)
    if decay:
        update = update + decay_rate * master
    return (grad, update)


def project(layer_input, weight, bias, cosine, sine, kv_cosine, kv_sine, heads):
    tokens = layer_input.shape[0]
    width = weight.shape[1]
    block = 256
    scale = HD ** (-0.5)

    def kernel(x_ref, w_ref, b_ref, c_ref, s_ref, kc_ref, ks_ref, a_ref, q_ref, kv_ref):
        x = wide_float(x_ref[...])
        inverse = lax.rsqrt(jnp.mean(x * x, axis=1, keepdims=True) + norm_eps)
        normed = low(x * inverse)
        a_ref[...] = normed
        linear = matmul(normed, w_ref[...]) + b_ref[...]
        for h in range(heads + 1):
            part = linear[:, h * HD : (h + 1) * HD]
            turned = pltpu.roll(part, HD // 2, axis=1)
            if h < heads:
                out = (part * c_ref[...] + turned * s_ref[...]) * scale
                q_ref[:, h * HD : (h + 1) * HD] = low(out)
            else:
                kv_ref[...] = low(part * kc_ref[...] + turned * ks_ref[...])

    def by_tokens(columns):
        return pl.BlockSpec((block, columns), lambda i: (i, 0))

    def whole(a):
        return pl.BlockSpec(a.shape, lambda i: (0, 0))

    return pl.pallas_call(
        kernel,
        grid=(tokens // block,),
        in_specs=[by_tokens(D), whole(weight), whole(bias)] + [by_tokens(HD)] * 4,
        out_specs=[by_tokens(D), by_tokens(heads * HD), by_tokens(HD)],
        out_shape=[
            jax.ShapeDtypeStruct((tokens, D), jnp.bfloat16),
            jax.ShapeDtypeStruct((tokens, heads * HD), jnp.bfloat16),
            jax.ShapeDtypeStruct((tokens, HD), jnp.bfloat16),
        ],
        name="project",
    )(layer_input, weight, bias, cosine, sine, kv_cosine, kv_sine)


def feed_forward(tokens_in, grads_in, w_gateup, half, at, count, into=None):
    tokens = tokens_in.shape[0]
    block = 512
    olds = [] if into is None else list(into)
    skip = at // block

    def kernel(b_ref, g_ref, wgu_ref, *refs):
        hid_ref, dgu_ref = refs[-2:]
        both = matmul(b_ref[...], wgu_ref[...])
        gate, upward = both[:, :half], both[:, half:]
        grad = wide_float(g_ref[...])
        logistic = jax.nn.sigmoid(gate)
        active = gate * logistic
        hid_ref[...] = low(active * upward)
        slope = logistic + active * (1.0 - logistic)
        dgu_ref[:, :half] = low(grad * upward * slope)
        dgu_ref[:, half:] = low(grad * active)

    def by_tokens(columns):
        return pl.BlockSpec((block, columns), lambda i: (i + skip, 0))

    return pl.pallas_call(
        kernel,
        grid=(count // block,),
        in_specs=[
            by_tokens(D),
            by_tokens(half),
            pl.BlockSpec(w_gateup.shape, lambda i: (0, 0), pipeline_mode=pl.Buffered(1)),
        ]
        + [pl.BlockSpec(memory_space=pl.ANY)] * len(olds),
        out_specs=[by_tokens(half), by_tokens(2 * half)],
        out_shape=[
            jax.ShapeDtypeStruct((tokens, half), jnp.bfloat16),
            jax.ShapeDtypeStruct((tokens, 2 * half), jnp.bfloat16),
        ],
        input_output_aliases={3: 0, 4: 1} if olds else {},
        name="feed_forward",
    )(tokens_in, grads_in, w_gateup, *olds)


def stacked_heads(ref, heads):
    return jnp.concatenate([ref[:, h * HD : (h + 1) * HD] for h in range(heads)], axis=0)


def attention_forward(queries, keys, values, begins, starts, place):
    tokens, columns = queries.shape
    heads = columns // HD
    length = keys.shape[0]
    rows = heads * BLOCK_Q

    def kernel(starts_ref, place_ref, q_ref, k_ref, v_ref, begin_ref, o_ref, lse_ref):
        step = pl.program_id(0)
        base = place_ref[0] * tokens + step * BLOCK_Q
        q = stacked_heads(q_ref, heads)
        row = base + lax.broadcasted_iota(jnp.int32, (BLOCK_Q, 1), 0)
        row = jnp.concatenate([row] * heads, axis=0)
        begin = jnp.concatenate([begin_ref[...]] * heads, axis=0)

        def body(j, carry):
            top, total, acc = carry
            at = pl.multiple_of(j * BLOCK_K, BLOCK_K)
            k = k_ref[pl.ds(at, BLOCK_K), :]
            v = v_ref[pl.ds(at, BLOCK_K), :]
            s = matmul_nt(q, k)
            col = at + lax.broadcasted_iota(jnp.int32, (1, BLOCK_K), 1)
            s = jnp.where((col <= row) & (col >= begin), s, masked_score)
            new_top = jnp.maximum(top, jnp.max(s, axis=1, keepdims=True))
            p = jnp.exp(s - new_top)
            scale = jnp.exp(top - new_top)
            total = scale * total + jnp.sum(p, axis=1, keepdims=True)
            acc = scale * acc + matmul(low(p), v)
            return new_top, total, acc

        first = starts_ref[step] // BLOCK_K
        last = (base + BLOCK_Q - 1) // BLOCK_K
        top, total, acc = lax.fori_loop(
            first,
            last + 1,
            body,
            (
                jnp.full((rows, 1), masked_score, jnp.float32),
                jnp.zeros((rows, 1), jnp.float32),
                jnp.zeros((rows, HD), jnp.float32),
            ),
        )
        out = acc / total
        for h in range(heads):
            o_ref[:, h * HD : (h + 1) * HD] = out[h * BLOCK_Q : (h + 1) * BLOCK_Q]
        lse_ref[...] = (top + jnp.log(total)).reshape(heads, BLOCK_Q, 1)

    block = pl.BlockSpec((BLOCK_Q, columns), lambda i, *_: (i, 0))
    whole = pl.BlockSpec((length, HD), lambda i, *_: (0, 0))
    return pl.pallas_call(
        kernel,
        grid_spec=pltpu.PrefetchScalarGridSpec(
            num_scalar_prefetch=2,
            grid=(tokens // BLOCK_Q,),
            in_specs=[block, whole, whole, pl.BlockSpec((BLOCK_Q, 1), lambda i, *_: (i, 0))],
            out_specs=[block, pl.BlockSpec((heads, BLOCK_Q, 1), lambda i, *_: (0, i, 0))],
        ),
        out_shape=[
            jax.ShapeDtypeStruct((tokens, columns), jnp.float32),
            jax.ShapeDtypeStruct((heads, tokens, 1), jnp.float32),
        ],
        compiler_params=pltpu.CompilerParams(dimension_semantics=("arbitrary",)),
        name="attention_forward",
    )(starts, place, queries, keys, values, begins)


def attention_backward(
    queries, keys, values, begins, starts, place, grads, lse, outputs, cosine, sine
):
    tokens, columns = queries.shape
    heads = columns // HD
    length = keys.shape[0]
    rows = heads * BLOCK_Q

    def kernel(
        starts_ref, place_ref, q_ref, k_ref, v_ref, begin_ref, g_ref, lse_ref, o_ref,
        c_ref, s_ref, dq_ref, dk_ref, dv_ref,
    ):
        step = pl.program_id(0)

        @pl.when(step == 0)
        def _():
            dk_ref[...] = jnp.zeros_like(dk_ref)
            dv_ref[...] = jnp.zeros_like(dv_ref)

        base = place_ref[0] * tokens + step * BLOCK_Q
        q = stacked_heads(q_ref, heads)
        g = stacked_heads(g_ref, heads)
        delta = jnp.sum(wide_float(g) * stacked_heads(o_ref, heads), axis=1, keepdims=True)
        lse = lse_ref[...].reshape(rows, 1)
        row = base + lax.broadcasted_iota(jnp.int32, (BLOCK_Q, 1), 0)
        row = jnp.concatenate([row] * heads, axis=0)
        begin = jnp.concatenate([begin_ref[...]] * heads, axis=0)

        def body(j, dq):
            at = pl.multiple_of(j * BLOCK_K, BLOCK_K)
            k = k_ref[pl.ds(at, BLOCK_K), :]
            v = v_ref[pl.ds(at, BLOCK_K), :]
            col = at + lax.broadcasted_iota(jnp.int32, (1, BLOCK_K), 1)
            s = jnp.where((col <= row) & (col >= begin), matmul_nt(q, k), masked_score)
            p = jnp.exp(s - lse)
            dp = matmul_nt(g, v)
            ds = low(p * (dp - delta))
            dk_ref[pl.ds(at, BLOCK_K), :] += matmul_tn(ds, q)
            dv_ref[pl.ds(at, BLOCK_K), :] += matmul_tn(low(p), g)
            return dq + matmul(ds, k)

        first = starts_ref[step] // BLOCK_K
        last = (base + BLOCK_Q - 1) // BLOCK_K
        dq = lax.fori_loop(first, last + 1, body, jnp.zeros((rows, HD), jnp.float32))
        for h in range(heads):
            part = dq[h * BLOCK_Q : (h + 1) * BLOCK_Q]
            turned = pltpu.roll(part, HD // 2, axis=1)
            part = (part * c_ref[...] - turned * s_ref[...]) * HD ** (-0.5)
            dq_ref[:, h * HD : (h + 1) * HD] = low(part)

    block = pl.BlockSpec((BLOCK_Q, columns), lambda i, *_: (i, 0))
    whole = pl.BlockSpec((length, HD), lambda i, *_: (0, 0))
    return pl.pallas_call(
        kernel,
        grid_spec=pltpu.PrefetchScalarGridSpec(
            num_scalar_prefetch=2,
            grid=(tokens // BLOCK_Q,),
            in_specs=[
                block,
                whole,
                whole,
                pl.BlockSpec((BLOCK_Q, 1), lambda i, *_: (i, 0)),
                block,
                pl.BlockSpec((heads, BLOCK_Q, 1), lambda i, *_: (0, i, 0)),
                block,
                pl.BlockSpec((BLOCK_Q, HD), lambda i, *_: (i, 0)),
                pl.BlockSpec((BLOCK_Q, HD), lambda i, *_: (i, 0)),
            ],
            out_specs=[block, whole, whole],
        ),
        out_shape=[
            jax.ShapeDtypeStruct((tokens, columns), jnp.bfloat16),
            jax.ShapeDtypeStruct((length, HD), jnp.float32),
            jax.ShapeDtypeStruct((length, HD), jnp.float32),
        ],
        compiler_params=pltpu.CompilerParams(dimension_semantics=("arbitrary",)),
        name="attention_backward",
    )(starts, place, queries, keys, values, begins, grads, lse, outputs, cosine, sine)


def local(
    layer_input,
    grad_out,
    segment_ids,
    positions,
    norm_gains,
    norm_gains_first,
    norm_gains_second,
    query_weight,
    query_weight_first,
    query_weight_second,
    query_bias,
    query_bias_first,
    query_bias_second,
    keyvalue_weight,
    keyvalue_weight_first,
    keyvalue_weight_second,
    keyvalue_bias,
    keyvalue_bias_first,
    keyvalue_bias_second,
    output_weight,
    output_weight_first,
    output_weight_second,
    gateup_weight,
    gateup_weight_first,
    gateup_weight_second,
    down_weight,
    down_weight_first,
    down_weight_second,
):
    hi, lo, x, y, c = (lax.axis_index(name) for name in WIDE + NARROW)
    wide = lax.axis_size("hi") * 4
    tokens = layer_input.shape[0]
    quarter = tokens // 4
    heads = query_bias.shape[0]
    token_count = float(tokens * wide)
    rows = D // wide
    narrow_rows = rows // 4
    bias_part = query_bias.shape[1]
    kv_part = keyvalue_bias.shape[0]
    column_block = c * KV + y
    hidden = gateup_weight.shape[2]
    half = -(-hidden // (2 * LANES)) * LANES
    padding = 2 * half - hidden
    own = c * 2 + y

    kv_columns = low(keyvalue_weight).reshape(narrow_rows, 2, KV, HD)
    kv_columns = jnp.transpose(kv_columns, (2, 1, 0, 3))
    small = jnp.concatenate([low(norm_gains).reshape(-1), low(keyvalue_bias)])
    small = jnp.pad(small, (0, HD - small.shape[0])).reshape(1, 1, 1, HD)
    small = jnp.pad(small, ((0, 0), (0, 0), (0, 15), (0, 0)))
    blocks = jnp.concatenate([kv_columns, jnp.broadcast_to(small, (2, 2, 16, HD))], axis=2)
    blocks = exchange_narrow(blocks).reshape(4, narrow_rows + 16, HD)
    kv_mine = blocks[:, :narrow_rows].reshape(rows, HD)
    small_row = blocks[:, narrow_rows].reshape(1, 4 * HD)
    row_gains = wide_float(blocks[:, narrow_rows, : 2 * narrow_rows])
    row_gains = jnp.transpose(row_gains.reshape(4, 2, narrow_rows), (1, 0, 2)).reshape(2, rows, 1)
    bias_row = jnp.pad(low(query_bias).reshape(1, -1), ((0, 0), (0, 4 * HD - heads * bias_part)))
    extra = jnp.pad(jnp.concatenate([small_row, bias_row]), ((0, 14), (0, 0)))
    my_qkv = wide_float(jnp.concatenate([low(query_weight), kv_mine], axis=1))
    packed = jnp.concatenate([low(my_qkv * row_gains[0]), extra], axis=0)
    side = jnp.pad(low(output_weight).T, ((0, 16), (0, 0)))
    packed = jnp.concatenate([packed, side], axis=1)
    columns, out_columns = wide_columns(packed, 4 * HD)
    others = [swap(column, "x") for column in columns]
    out_others = [swap(column, "x") for column in after(out_columns, others)]
    w_qkv, small_all = assemble(columns, others, rows)
    small_all = wide_float(small_all)
    b_query = small_all[:, 1, : heads * bias_part].reshape(wide, heads, bias_part)
    small_all = small_all[:, 0].reshape(wide, 4, HD)
    gains = small_all[:, :, : 2 * narrow_rows].reshape(wide, 4, 2, narrow_rows)
    gains = jnp.transpose(gains, (2, 0, 1, 3)).reshape(2, D)
    b_kv = small_all[:, :, 2 * narrow_rows : 2 * narrow_rows + kv_part].reshape(2 * KV, HD)
    b_query = jnp.transpose(b_query, (1, 0, 2)).reshape(heads * HD)
    b_qkv = jnp.concatenate([b_query, pick(b_kv, column_block)])
    gain_two = gains[1]

    def padded(shard):
        return jnp.pad(low(shard), ((0, 0), (0, padding)))

    down_shard = hidden_pair([padded(down_weight.T)])
    w_down = lax.all_gather(after(down_shard, columns), ("hi", "lo"), axis=0, tiled=True)
    gateup_shard = hidden_pair(
        after([padded(gateup_weight[:, 0]), padded(gateup_weight[:, 1])], packed)
    )
    w_gateup = lax.all_gather(gateup_shard, ("hi", "lo"), axis=0, tiled=True)

    cosine, sine = rotation(positions)
    kv_cosine = jnp.where(c == 0, cosine, 1.0)
    kv_sine = jnp.where(c == 0, sine, 0.0)
    normed_one, queries, kv_own = project(
        layer_input, w_qkv, b_qkv[None], cosine, sine, kv_cosine, kv_sine, heads
    )
    kv_own = after(kv_own, gateup_shard)
    both = pair(kv_own, swap(kv_own, "x"), x)
    kv_row = pair(both, swap(both, "lo"), lo).reshape(4 * tokens, HD)
    kv_other = swap(kv_row, "c")
    keys = jnp.where(c == 0, kv_row, kv_other)
    values = jnp.where(c == 0, kv_other, kv_row)
    begins = segment_ids - hi * (4 * tokens)
    starts = begins[::BLOCK_Q]
    begins = begins[:, None]
    place = (lo * 2 + x).reshape(1).astype(jnp.int32)
    grad_blocks = grad_out.reshape(4, quarter, D)
    grad_near = [pick(grad_blocks, own ^ d) for d in range(4)]
    grad_far = [swap(part, "x") for part in after(grad_near[:2], kv_row)]
    attention, log_total = attention_forward(queries, keys, values, begins, starts, place)
    w_output, _ = assemble(*after((out_columns, out_others), attention), rows)
    grad_far = after(grad_far, attention)
    ff_grad = stack_rows(grad_near + grad_far + [swap(part, "c") for part in grad_far], range(8))
    attention_low = low(attention)

    def halves(block):
        split = block.reshape(2, -1, block.shape[-1])
        return pick(split, c), pick(split, 1 - c)

    def send_core(kept, sent):
        return (kept + wide_float(swap(low(sent), "c"))).reshape(2, quarter, D)

    def send_y(total):
        return pick(total, y), swap(low(pick(total, 1 - y)), "y")

    attention_kept, attention_sent = halves(attention_low)
    sent = matmul_nt(attention_sent, w_output)
    out_total = send_core(matmul_nt(attention_kept, w_output), sent)
    out_parts = send_y(out_total)

    grad_hidden = low(matmul(after(ff_grad, out_total), w_down))
    out_parts = after(out_parts, grad_hidden)
    residual = wide_float(pick(layer_input.reshape(4, quarter, D), own)) + add_up(out_parts)
    inverse_two = lax.rsqrt(jnp.mean(residual * residual, axis=-1, keepdims=True) + norm_eps)
    unit_two = residual * inverse_two
    normed_two = low(unit_two * gain_two)

    by_y = swap(normed_two, "y")
    by_x = swap(normed_two, "x")
    by_both = [swap(by_y[:, : D // 2], "x"), swap(by_x[:, D // 2 :], "y")]
    count = 4 * quarter
    ff_input = stack_rows(
        [normed_two, by_y, swap(normed_two, "c"), swap(by_y, "c")], range(4), count=8
    )
    firsts = feed_forward(ff_input, grad_hidden, w_gateup, half, 0, count)
    by_x, by_both = after((by_x, by_both), firsts[0])
    by_both = jnp.concatenate(by_both, axis=1)
    ff_input = stack_rows(
        [by_x, by_both, swap(by_x, "c"), swap(by_both, "c")], range(4, 8), into=ff_input, count=8
    )
    hidden_all, both_all = feed_forward(
        ff_input, grad_hidden, w_gateup, half, count, count, into=firsts
    )

    half_d = D // 2

    def join_core(sums):
        return wide_float(sums[: 2 * quarter]) + wide_float(swap(sums[2 * quarter :], "c"))

    def first_sends(far_sums, near_sums):
        to_x = low(far_sums[:, :half_d])
        to_y = low(jnp.concatenate([near_sums[quarter:, half_d:], far_sums[quarter:, half_d:]]))
        return to_x, to_y

    def second_sends(far_sums, near_sums, from_x, from_y):
        left = near_sums[:, :half_d] + wide_float(from_x)
        right = near_sums[:quarter, half_d:] + wide_float(from_y[:quarter])
        to_x = low(far_sums[:quarter, half_d:] + wide_float(from_y[quarter:]))
        return (left[:quarter], right), (low(left[quarter:]), to_x)

    def finish_sums(kept, from_y, from_x):
        return jnp.concatenate([kept[0] + wide_float(from_y), kept[1] + wide_float(from_x)], axis=1)

    feed_far = low(matmul_nt(both_all[count:], w_gateup))
    feed_near = low(matmul_nt(after(both_all, feed_far)[:count], w_gateup))

    def over_rows(grad):
        return lax.psum_scatter(grad, ("hi", "lo"), scatter_dimension=0, tiled=True)

    far_sums, near_sums = join_core(feed_far), join_core(feed_near)
    to_x, to_y = first_sends(far_sums, near_sums)
    from_x, from_y = swap(to_x, "x"), swap(to_y, "y")
    ff_late, both_late = after((ff_input, both_all), to_x, to_y)
    grad_gateup = low(matmul_tn(ff_late, both_late))
    from_x, from_y = after((from_x, from_y), grad_gateup)
    kept, (to_y, to_x) = second_sends(far_sums, near_sums, from_x, from_y)
    from_x, from_y = swap(to_x, "x"), swap(to_y, "y")
    ff_late, hidden_all = after((ff_grad, hidden_all), to_x, to_y)
    grad_down = low(matmul_tn(ff_late, hidden_all))
    from_x, from_y = after((from_x, from_y), grad_down)
    rows_gateup, rows_down = over_rows(grad_gateup), over_rows(grad_down)
    grad_normed_two = finish_sums(kept, from_y, from_x)
    grad_residual = wide_float(grad_near[0]) + rms_back(
        grad_normed_two * gain_two, unit_two, inverse_two
    )

    residual_own = low(grad_residual)
    hidden_all = after(hidden_all, residual_own)
    mlp_far = low(matmul_nt(hidden_all[count:], w_down))
    mlp_near = low(matmul_nt(after(hidden_all, mlp_far)[:count], w_down))
    residual_low = gather_tokens(residual_own, mlp_near)

    grad_attention = low(matmul(residual_low, w_output))
    rows_output = over_rows(low(matmul_tn(residual_low, attention_low)))
    mlp_far, mlp_near = after((mlp_far, mlp_near), residual_low)
    mlp_far, mlp_near = join_core(mlp_far), join_core(mlp_near)
    to_x, to_y = first_sends(mlp_far, mlp_near)
    from_x, from_y = swap(to_x, "x"), swap(to_y, "y")
    grad_attention = after(grad_attention, to_x, to_y)
    grad_queries, grad_keys, grad_values = attention_backward(
        queries, keys, values, begins, starts, place, grad_attention, log_total, attention,
        cosine, sine,
    )
    kv_sent = low(jnp.where(c == 0, grad_values, grad_keys))
    kv_grad = jnp.where(c == 0, grad_keys, grad_values) + wide_float(swap(kv_sent, "c"))
    kv_grad = kv_grad.reshape(2, 2 * tokens, HD)
    kv_grad = pick(kv_grad, lo) + wide_float(swap(low(pick(kv_grad, 1 - lo)), "lo"))
    kv_grad = kv_grad.reshape(2, tokens, HD)
    kv_grad = after(kv_grad, rows_gateup)
    from_x, from_y = after((from_x, from_y), kv_grad)
    mlp_kept, (to_y, to_x) = second_sends(mlp_far, mlp_near, from_x, from_y)
    from_x, from_y = swap(to_x, "x"), swap(to_y, "y")
    kv_grad = pick(kv_grad, x) + wide_float(swap(low(pick(kv_grad, 1 - x)), "x"))
    turned = jnp.concatenate([kv_grad[:, HD // 2 :], kv_grad[:, : HD // 2]], axis=1)
    grad_kv = low(kv_grad * kv_cosine - turned * kv_sine)

    w_query, w_kv = w_qkv[:, : heads * HD], w_qkv[:, heads * HD :]

    def input_part(kv_part_grad, query_part_grad):
        return matmul_nt(query_part_grad, w_query) + matmul_nt(kv_part_grad, w_kv)

    query_kept, query_sent = halves(grad_queries)
    kv_kept, kv_sent = halves(grad_kv)
    part_sent = low(input_part(kv_sent, query_sent))
    part_kept = input_part(kv_kept, query_kept)
    part_total = send_core(part_kept, part_sent)
    part_parts = after(send_y(part_total), rows_down)
    rows_gateup, rows_down = after((rows_gateup, rows_down), grad_kv)
    parts_gateup = send_hidden(rows_gateup)
    parts_down = send_hidden(rows_down)
    parts_output = send_hidden(after(rows_output, part_total))
    from_x, from_y = after((from_x, from_y), part_total)
    layer_output = gather_tokens(low(residual + finish_sums(mlp_kept, from_y, from_x)))
    grad_normed_one = add_up(part_parts)
    own_input = wide_float(pick(layer_input.reshape(4, quarter, D), own))
    own_inverse = lax.rsqrt(jnp.mean(own_input * own_input, axis=-1, keepdims=True) + norm_eps)
    input_grad = gather_tokens(
        low(
            grad_residual
            + rms_back(grad_normed_one, own_input * own_inverse, own_inverse)
        )
    )

    sums_query = low(matmul_tn(normed_one, grad_queries)).reshape(wide, rows, heads * HD)
    hi_query = send_hi(low(add_up(after(send_x(sums_query), part_total))))
    lo_query = send_lo(add_up(after(hi_query, part_total)))
    grad_kv_weight = low(matmul_tn(normed_one, grad_kv)).reshape(wide, rows, HD)
    bias_query = jnp.sum(wide_float(grad_queries), axis=0).reshape(heads, wide, bias_part)
    bias_query = jnp.transpose(bias_query, (1, 0, 2)).reshape(wide, heads * bias_part)
    bias_kv = lax.dynamic_update_slice(
        jnp.zeros((2 * KV, HD), jnp.float32),
        jnp.sum(wide_float(grad_kv), axis=0, keepdims=True),
        (column_block, 0),
    ).reshape(wide, 4 * kv_part)
    bias_all = jnp.concatenate([bias_query, bias_kv], axis=1)
    bias_all = jnp.pad(bias_all, ((0, 0), (0, HD - bias_all.shape[1])))
    extra = jnp.pad(low(bias_all)[:, None], ((0, 0), (0, 15), (0, 0)))
    x_kv = send_x(jnp.concatenate([grad_kv_weight, extra], axis=1))
    hi_kv = send_hi(low(add_up(after(x_kv, part_total))))
    summed = add_up(send_lo(add_up(hi_kv)))
    parts_down, parts_gateup = after((parts_down, parts_gateup), part_total)
    summed_down = join_hidden(*parts_down)
    summed_gate = join_hidden(*(part[:, :half] for part in parts_gateup))
    summed_up = join_hidden(*(part[:, half:] for part in parts_gateup))
    summed_output = add_up(
        after(parts_output, part_total)
    )
    summed_query = add_up(lo_query)
    summed_kv = summed[:rows]
    summed_query_bias = summed[rows, : heads * bias_part].reshape(heads, bias_part)
    kv_bias = summed[rows, heads * bias_part : heads * bias_part + 4 * kv_part]

    grad_gain_one = jnp.sum(
        summed_query * my_qkv[:, : heads * HD], axis=1
    ) + jnp.sum(summed_kv * my_qkv[:, heads * HD :], axis=1)
    summed_query = summed_query * row_gains[0]
    summed_kv = summed_kv * row_gains[0]
    summed_gateup = jnp.stack([summed_gate[:, :hidden], summed_up[:, :hidden]], axis=1)
    grad_gain_two = (
        jnp.sum(summed_gateup * wide_float(low(gateup_weight)), axis=(1, 2)) / row_gains[1, :, 0]
    )
    gain_parts = jnp.stack([grad_gain_one, grad_gain_two]).reshape(2, 4, narrow_rows)
    gain_parts = jnp.transpose(gain_parts, (1, 0, 2)).reshape(4, 2 * narrow_rows)
    last = jnp.concatenate([gain_parts, kv_bias.reshape(4, kv_part)], axis=1)
    last = jnp.pad(last, ((0, 0), (0, HD - last.shape[1])))[:, None]
    last = jnp.pad(last, ((0, 0), (0, 7), (0, 0)))
    last = jnp.concatenate([summed_kv.reshape(4, narrow_rows, HD), last], axis=1)
    last = exchange_narrow(last.reshape((2, 2) + last.shape[1:]))
    summed_keyvalue = jnp.transpose(last[:, :, :narrow_rows], (2, 1, 0, 3))
    summed_keyvalue = summed_keyvalue.reshape(narrow_rows, 2 * KV * HD)
    small_sums = jnp.sum(last[:, :, narrow_rows], axis=(0, 1))
    summed_gains = small_sums[: 2 * narrow_rows].reshape(2, narrow_rows)
    summed_keyvalue_bias = small_sums[2 * narrow_rows : 2 * narrow_rows + kv_part]
    summed_down = summed_down[:, :hidden].T
    summed_output = summed_output.T

    gains_update = adam_update(
        summed_gains, norm_gains, norm_gains_first, norm_gains_second, False, token_count
    )
    query_update = adam_update(
        summed_query, query_weight, query_weight_first, query_weight_second, True, token_count
    )
    qbias_update = adam_update(
        summed_query_bias, query_bias, query_bias_first, query_bias_second, False, token_count
    )
    keyvalue_update = adam_update(
        summed_keyvalue,
        keyvalue_weight,
        keyvalue_weight_first,
        keyvalue_weight_second,
        True,
        token_count,
    )
    kvbias_update = adam_update(
        summed_keyvalue_bias,
        keyvalue_bias,
        keyvalue_bias_first,
        keyvalue_bias_second,
        False,
        token_count,
    )
    output_update = adam_update(
        summed_output, output_weight, output_weight_first, output_weight_second, True, token_count
    )
    gateup_update = adam_update(
        summed_gateup, gateup_weight, gateup_weight_first, gateup_weight_second, True, token_count
    )
    down_update = adam_update(
        summed_down, down_weight, down_weight_first, down_weight_second, True, token_count
    )
    return (
        layer_output,
        input_grad,
        *gains_update,
        *query_update,
        *qbias_update,
        *keyvalue_update,
        *kvbias_update,
        *output_update,
        *gateup_update,
        *down_update,
    )


def solution(mesh):
    devices = mesh.devices.reshape(-1, 2, 2, 2, 2)
    split = Mesh(devices, WIDE + NARROW)
    token_matrix = P(WIDE, None)
    token_vector = P(WIDE)
    gains = P(None, WIDE + NARROW)
    query = P(WIDE, NARROW)
    by_narrow = P(NARROW, WIDE)
    keyvalue = P(WIDE + NARROW, None)
    keyvalue_bias = P(WIDE + NARROW)
    gateup = P(WIDE, None, NARROW)
    parameters = (gains, query, by_narrow, keyvalue, keyvalue_bias, by_narrow, gateup, by_narrow)
    in_specs = (token_matrix, token_matrix, token_vector, token_vector)
    out_specs = (token_matrix, token_matrix)
    for spec in parameters:
        in_specs += (spec,) * 3
        out_specs += (spec,) * 2
    return jax.shard_map(local, mesh=split, in_specs=in_specs, out_specs=out_specs, check_vma=False)
```

```python
import jax
import jax.numpy as jnp
from jax import lax
from jax.experimental import pallas as pl
from jax.experimental.layout import Layout, with_layout_constraint
from jax.experimental.pallas import tpu as pltpu
from jax.sharding import Mesh
from jax.sharding import PartitionSpec as P

D = 1536
H = 12
KV = 2
HD = 128
LENGTH = 4096
LANES = 128

norm_eps = 1e-06
rope_base = 1000000.0
beta_first = 0.9
beta_second = 0.95
adam_eps = 1e-08
decay_rate = 0.1
first_fix = 1.0 - 0.9**10
second_fix = 1.0 - 0.95**10
masked_score = -1e30

WIDE = ("hi", "lo", "x")
NARROW = ("y", "c")
BLOCK_Q = 256
BLOCK_K = 512


def low(a):
    return a.astype(jnp.bfloat16)


def wide_float(a):
    return a.astype(jnp.float32)


def matmul(left, right):
    return jnp.dot(left, right, preferred_element_type=jnp.float32)


def matmul_nt(left, right):
    return lax.dot_general(left, right, (((1,), (1,)), ((), ())), preferred_element_type=jnp.float32)


def matmul_tn(left, right):
    return lax.dot_general(left, right, (((0,), (0,)), ((), ())), preferred_element_type=jnp.float32)


def swap(block, axis, distance=1):
    size = 1
    for name in axis if isinstance(axis, tuple) else (axis,):
        size *= lax.axis_size(name)
    return lax.ppermute(block, axis, [(i, i ^ distance) for i in range(size)])


def pick(stacked, index):
    return lax.dynamic_index_in_dim(stacked, index, axis=0, keepdims=False)


def pair(mine, other, index):
    return jnp.where(index == 0, jnp.stack([mine, other]), jnp.stack([other, mine]))


def after(value, *needed):
    return lax.optimization_barrier((value, needed))[0]


def wide_columns(block, cut):
    lo = lax.axis_index("lo")
    count = lax.axis_size("hi")
    mine = [block] + [swap(block, "hi", d) for d in range(1, count)]
    other = [swap(part, "lo") for part in mine]
    left = [pair(m[:, :cut], o[:, :cut], lo) for m, o in zip(mine, other)]
    right = [pair(m[:, cut:], o[:, cut:], lo) for m, o in zip(mine, other)]
    return left, right


def stack_rows(blocks, slots, into=None, count=None):
    height, width = blocks[0].shape
    count = len(blocks) if count is None else count
    olds = [] if into is None else [into]

    def kernel(slot_ref, *refs):
        out_ref, sem = refs[-2:]
        copies = []
        for i, block_ref in enumerate(refs[: len(blocks)]):
            start = pl.multiple_of(slot_ref[i] * height, 16)
            copies.append(
                pltpu.make_async_copy(block_ref, out_ref.at[pl.ds(start, height), :], sem.at[i])
            )
        for copy in copies:
            copy.start()
        for copy in copies:
            copy.wait()

    anywhere = pl.BlockSpec(memory_space=pl.ANY)
    slots = jnp.stack([jnp.asarray(slot, jnp.int32) for slot in slots])
    return pl.pallas_call(
        kernel,
        in_specs=[pl.BlockSpec(memory_space=pltpu.SMEM)]
        + [pl.BlockSpec(memory_space=pltpu.VMEM)] * len(blocks)
        + [anywhere] * len(olds),
        out_specs=anywhere,
        out_shape=jax.ShapeDtypeStruct((count * height, width), blocks[0].dtype),
        scratch_shapes=[pltpu.SemaphoreType.DMA((len(blocks),))],
        input_output_aliases={len(blocks) + 1: 0} if olds else {},
        name="stack_rows",
    )(slots, *blocks, *olds)


def assemble(columns, others, rows):
    count = len(columns)
    _, height, width = columns[0].shape
    kind = columns[0].dtype

    def kernel(at_ref, *refs):
        main_ref, extra_ref = refs[-2:]
        for d in range(count):
            for k in range(2):
                part = refs[2 * d + k]
                for low_bit in range(2):
                    index = (at_ref[0] ^ d) * 4 + low_bit * 2 + (at_ref[1] ^ k)
                    start = pl.multiple_of(index * rows, 16)
                    main_ref[pl.ds(start, rows), :] = part[low_bit, :rows]
                    extra_ref[index] = part[low_bit, rows:]

    parts = [part for both in zip(columns, others) for part in both]
    at = jnp.stack([lax.axis_index("hi"), lax.axis_index("x")]).astype(jnp.int32)
    return pl.pallas_call(
        kernel,
        in_specs=[pl.BlockSpec(memory_space=pltpu.SMEM)]
        + [pl.BlockSpec(memory_space=pltpu.VMEM)] * len(parts),
        out_specs=[pl.BlockSpec(memory_space=pltpu.VMEM)] * 2,
        out_shape=[
            jax.ShapeDtypeStruct((count * 4 * rows, width), kind),
            jax.ShapeDtypeStruct((count * 4, height - rows, width), kind),
        ],
        name="assemble",
    )(at, *parts)


def send_x(parts):
    x = lax.axis_index("x")
    parts = parts.reshape((-1, 2, 2) + parts.shape[1:])
    kept = lax.dynamic_index_in_dim(parts, x, axis=2, keepdims=False)
    sent = lax.dynamic_index_in_dim(parts, 1 - x, axis=2, keepdims=False)
    return kept, swap(sent, "x")


def send_hi(parts):
    hi = lax.axis_index("hi")
    turns = range(1, lax.axis_size("hi"))
    return [pick(parts, hi)] + [swap(pick(parts, hi ^ d), "hi", d) for d in turns]


def send_lo(parts):
    lo = lax.axis_index("lo")
    return pick(parts, lo), swap(low(pick(parts, 1 - lo)), "lo")


def add_up(parts):
    return sum(wide_float(part) for part in parts)


def send_hidden(total):
    x = lax.axis_index("x")
    total = total.reshape((2, -1) + total.shape[1:])
    return pick(total, x), swap(pick(total, 1 - x), "x")


def join_hidden(mine, other):
    x = lax.axis_index("x")
    first = jnp.where(x == 0, mine, other)
    second = jnp.where(x == 0, other, mine)
    return wide_float(jnp.concatenate([first, second], axis=1))


def hidden_pair(shards):
    x = lax.axis_index("x")
    half = shards[0].shape[1] // 2

    def part(at):
        return jnp.concatenate(
            [lax.dynamic_slice_in_dim(shard, at * half, half, axis=1) for shard in shards], axis=1
        )

    both = pair(part(x), swap(part(1 - x), "x"), x)
    return both.reshape((-1,) + both.shape[2:])


def exchange_narrow(blocks):
    y, c = (lax.axis_index(name) for name in NARROW)
    shape = blocks.shape[2:]
    flat = blocks.reshape((4,) + shape)
    me = y * 2 + c
    got = [pick(flat, me)] + [swap(pick(flat, me ^ d), NARROW, d) for d in range(1, 4)]
    near, far = pair(got[0], got[1], c), pair(got[2], got[3], c)
    return pair(near, far, y)


def gather_tokens(block, *needed):
    return spread_core(block, after(swap(block, "y"), *needed))


def spread_core(block, by_y):
    y, c = (lax.axis_index(name) for name in NARROW)
    own = c * 2 + y
    return stack_rows(
        [block, by_y, swap(block, "c"), swap(by_y, "c")], [own, own ^ 1, own ^ 2, own ^ 3]
    )


def rotation(positions):
    half = HD // 2
    freqs = rope_base ** (-2.0 * jnp.arange(half, dtype=jnp.float32) / HD)
    angles = positions.astype(jnp.float32)[:, None] * freqs[None, :]
    cosine, sine = jnp.cos(angles), jnp.sin(angles)
    return jnp.concatenate([cosine, cosine], axis=1), jnp.concatenate([-sine, sine], axis=1)


def rms_back(grad_unit, unit, inverse):
    return inverse * (grad_unit - unit * jnp.mean(grad_unit * unit, axis=-1, keepdims=True))


def adam_update(grad, master, first, second, decay, count):
    mean_grad = grad / count
    first_new = beta_first * first + (1.0 - beta_first) * mean_grad
    second_new = beta_second * second + (1.0 - beta_second) * mean_grad * mean_grad
    update = first_new / first_fix / (jnp.sqrt(second_new / second_fix) + adam_eps)
    if decay:
        update = update + decay_rate * master
    return (grad, update)


def project(layer_input, weight, bias, cosine, sine, kv_cosine, kv_sine, heads):
    tokens = layer_input.shape[0]
    width = weight.shape[1]
    block = 256
    scale = HD ** (-0.5)

    def kernel(x_ref, w_ref, b_ref, c_ref, s_ref, kc_ref, ks_ref, a_ref, q_ref, kv_ref):
        x = wide_float(x_ref[...])
        inverse = lax.rsqrt(jnp.mean(x * x, axis=1, keepdims=True) + norm_eps)
        normed = low(x * inverse)
        a_ref[...] = normed
        linear = matmul(normed, w_ref[...]) + b_ref[...]
        for h in range(heads + 1):
            part = linear[:, h * HD : (h + 1) * HD]
            turned = pltpu.roll(part, HD // 2, axis=1)
            if h < heads:
                out = (part * c_ref[...] + turned * s_ref[...]) * scale
                q_ref[:, h * HD : (h + 1) * HD] = low(out)
            else:
                kv_ref[...] = low(part * kc_ref[...] + turned * ks_ref[...])

    def by_tokens(columns):
        return pl.BlockSpec((block, columns), lambda i: (i, 0))

    def whole(a):
        return pl.BlockSpec(a.shape, lambda i: (0, 0))

    return pl.pallas_call(
        kernel,
        grid=(tokens // block,),
        in_specs=[by_tokens(D), whole(weight), whole(bias)] + [by_tokens(HD)] * 4,
        out_specs=[by_tokens(D), by_tokens(heads * HD), by_tokens(HD)],
        out_shape=[
            jax.ShapeDtypeStruct((tokens, D), jnp.bfloat16),
            jax.ShapeDtypeStruct((tokens, heads * HD), jnp.bfloat16),
            jax.ShapeDtypeStruct((tokens, HD), jnp.bfloat16),
        ],
        name="project",
    )(layer_input, weight, bias, cosine, sine, kv_cosine, kv_sine)


def feed_forward(tokens_in, grads_in, w_gateup, half, at, count, into=None):
    tokens = tokens_in.shape[0]
    block = 512
    olds = [] if into is None else list(into)
    skip = at // block

    def kernel(b_ref, g_ref, wgu_ref, *refs):
        hid_ref, dgu_ref = refs[-2:]
        both = matmul(b_ref[...], wgu_ref[...])
        gate, upward = both[:, :half], both[:, half:]
        grad = wide_float(g_ref[...])
        logistic = jax.nn.sigmoid(gate)
        active = gate * logistic
        hid_ref[...] = low(active * upward)
        slope = logistic + active * (1.0 - logistic)
        dgu_ref[:, :half] = low(grad * upward * slope)
        dgu_ref[:, half:] = low(grad * active)

    def by_tokens(columns):
        return pl.BlockSpec((block, columns), lambda i: (i + skip, 0))

    return pl.pallas_call(
        kernel,
        grid=(count // block,),
        in_specs=[
            by_tokens(D),
            by_tokens(half),
            pl.BlockSpec(w_gateup.shape, lambda i: (0, 0), pipeline_mode=pl.Buffered(1)),
        ]
        + [pl.BlockSpec(memory_space=pl.ANY)] * len(olds),
        out_specs=[by_tokens(half), by_tokens(2 * half)],
        out_shape=[
            jax.ShapeDtypeStruct((tokens, half), jnp.bfloat16),
            jax.ShapeDtypeStruct((tokens, 2 * half), jnp.bfloat16),
        ],
        input_output_aliases={3: 0, 4: 1} if olds else {},
        name="feed_forward",
    )(tokens_in, grads_in, w_gateup, *olds)


def stacked_heads(ref, heads):
    return jnp.concatenate([ref[:, h * HD : (h + 1) * HD] for h in range(heads)], axis=0)


def attention_forward(queries, keys, values, begins, starts, place):
    tokens, columns = queries.shape
    heads = columns // HD
    length = keys.shape[0]
    rows = heads * BLOCK_Q

    def kernel(starts_ref, place_ref, q_ref, k_ref, v_ref, begin_ref, o_ref, lse_ref):
        step = pl.program_id(0)
        base = place_ref[0] * tokens + step * BLOCK_Q
        q = stacked_heads(q_ref, heads)
        row = base + lax.broadcasted_iota(jnp.int32, (BLOCK_Q, 1), 0)
        row = jnp.concatenate([row] * heads, axis=0)
        begin = jnp.concatenate([begin_ref[...]] * heads, axis=0)

        def body(j, carry):
            top, total, acc = carry
            at = pl.multiple_of(j * BLOCK_K, BLOCK_K)
            k = k_ref[pl.ds(at, BLOCK_K), :]
            v = v_ref[pl.ds(at, BLOCK_K), :]
            s = matmul_nt(q, k)
            col = at + lax.broadcasted_iota(jnp.int32, (1, BLOCK_K), 1)
            s = jnp.where((col <= row) & (col >= begin), s, masked_score)
            new_top = jnp.maximum(top, jnp.max(s, axis=1, keepdims=True))
            p = jnp.exp(s - new_top)
            scale = jnp.exp(top - new_top)
            total = scale * total + jnp.sum(p, axis=1, keepdims=True)
            acc = scale * acc + matmul(low(p), v)
            return new_top, total, acc

        first = starts_ref[step] // BLOCK_K
        last = (base + BLOCK_Q - 1) // BLOCK_K
        top, total, acc = lax.fori_loop(
            first,
            last + 1,
            body,
            (
                jnp.full((rows, 1), masked_score, jnp.float32),
                jnp.zeros((rows, 1), jnp.float32),
                jnp.zeros((rows, HD), jnp.float32),
            ),
        )
        out = acc / total
        for h in range(heads):
            o_ref[:, h * HD : (h + 1) * HD] = out[h * BLOCK_Q : (h + 1) * BLOCK_Q]
        lse_ref[...] = (top + jnp.log(total)).reshape(heads, BLOCK_Q, 1)

    block = pl.BlockSpec((BLOCK_Q, columns), lambda i, *_: (i, 0))
    whole = pl.BlockSpec((length, HD), lambda i, *_: (0, 0))
    return pl.pallas_call(
        kernel,
        grid_spec=pltpu.PrefetchScalarGridSpec(
            num_scalar_prefetch=2,
            grid=(tokens // BLOCK_Q,),
            in_specs=[block, whole, whole, pl.BlockSpec((BLOCK_Q, 1), lambda i, *_: (i, 0))],
            out_specs=[block, pl.BlockSpec((heads, BLOCK_Q, 1), lambda i, *_: (0, i, 0))],
        ),
        out_shape=[
            jax.ShapeDtypeStruct((tokens, columns), jnp.float32),
            jax.ShapeDtypeStruct((heads, tokens, 1), jnp.float32),
        ],
        compiler_params=pltpu.CompilerParams(dimension_semantics=("arbitrary",)),
        name="attention_forward",
    )(starts, place, queries, keys, values, begins)


def attention_backward(
    queries, keys, values, begins, starts, place, grads, lse, outputs, cosine, sine
):
    tokens, columns = queries.shape
    heads = columns // HD
    length = keys.shape[0]
    rows = heads * BLOCK_Q

    def kernel(
        starts_ref, place_ref, q_ref, k_ref, v_ref, begin_ref, g_ref, lse_ref, o_ref,
        c_ref, s_ref, dq_ref, dk_ref, dv_ref,
    ):
        step = pl.program_id(0)

        @pl.when(step == 0)
        def _():
            dk_ref[...] = jnp.zeros_like(dk_ref)
            dv_ref[...] = jnp.zeros_like(dv_ref)

        base = place_ref[0] * tokens + step * BLOCK_Q
        q = stacked_heads(q_ref, heads)
        g = stacked_heads(g_ref, heads)
        delta = jnp.sum(wide_float(g) * stacked_heads(o_ref, heads), axis=1, keepdims=True)
        lse = lse_ref[...].reshape(rows, 1)
        row = base + lax.broadcasted_iota(jnp.int32, (BLOCK_Q, 1), 0)
        row = jnp.concatenate([row] * heads, axis=0)
        begin = jnp.concatenate([begin_ref[...]] * heads, axis=0)

        def body(j, dq):
            at = pl.multiple_of(j * BLOCK_K, BLOCK_K)
            k = k_ref[pl.ds(at, BLOCK_K), :]
            v = v_ref[pl.ds(at, BLOCK_K), :]
            col = at + lax.broadcasted_iota(jnp.int32, (1, BLOCK_K), 1)
            s = jnp.where((col <= row) & (col >= begin), matmul_nt(q, k), masked_score)
            p = jnp.exp(s - lse)
            dp = matmul_nt(g, v)
            ds = low(p * (dp - delta))
            dk_ref[pl.ds(at, BLOCK_K), :] += matmul_tn(ds, q)
            dv_ref[pl.ds(at, BLOCK_K), :] += matmul_tn(low(p), g)
            return dq + matmul(ds, k)

        first = starts_ref[step] // BLOCK_K
        last = (base + BLOCK_Q - 1) // BLOCK_K
        dq = lax.fori_loop(first, last + 1, body, jnp.zeros((rows, HD), jnp.float32))
        for h in range(heads):
            part = dq[h * BLOCK_Q : (h + 1) * BLOCK_Q]
            turned = pltpu.roll(part, HD // 2, axis=1)
            part = (part * c_ref[...] - turned * s_ref[...]) * HD ** (-0.5)
            dq_ref[:, h * HD : (h + 1) * HD] = low(part)

    block = pl.BlockSpec((BLOCK_Q, columns), lambda i, *_: (i, 0))
    whole = pl.BlockSpec((length, HD), lambda i, *_: (0, 0))
    return pl.pallas_call(
        kernel,
        grid_spec=pltpu.PrefetchScalarGridSpec(
            num_scalar_prefetch=2,
            grid=(tokens // BLOCK_Q,),
            in_specs=[
                block,
                whole,
                whole,
                pl.BlockSpec((BLOCK_Q, 1), lambda i, *_: (i, 0)),
                block,
                pl.BlockSpec((heads, BLOCK_Q, 1), lambda i, *_: (0, i, 0)),
                block,
                pl.BlockSpec((BLOCK_Q, HD), lambda i, *_: (i, 0)),
                pl.BlockSpec((BLOCK_Q, HD), lambda i, *_: (i, 0)),
            ],
            out_specs=[block, whole, whole],
        ),
        out_shape=[
            jax.ShapeDtypeStruct((tokens, columns), jnp.bfloat16),
            jax.ShapeDtypeStruct((length, HD), jnp.float32),
            jax.ShapeDtypeStruct((length, HD), jnp.float32),
        ],
        compiler_params=pltpu.CompilerParams(dimension_semantics=("arbitrary",)),
        cost_estimate=pl.CostEstimate(
            flops=20 * tokens * tokens * columns, transcendentals=0, bytes_accessed=0
        ),
        name="attention_backward",
    )(starts, place, queries, keys, values, begins, grads, lse, outputs, cosine, sine)


def local(
    layer_input,
    grad_out,
    segment_ids,
    positions,
    norm_gains,
    norm_gains_first,
    norm_gains_second,
    query_weight,
    query_weight_first,
    query_weight_second,
    query_bias,
    query_bias_first,
    query_bias_second,
    keyvalue_weight,
    keyvalue_weight_first,
    keyvalue_weight_second,
    keyvalue_bias,
    keyvalue_bias_first,
    keyvalue_bias_second,
    output_weight,
    output_weight_first,
    output_weight_second,
    gateup_weight,
    gateup_weight_first,
    gateup_weight_second,
    down_weight,
    down_weight_first,
    down_weight_second,
):
    hi, lo, x, y, c = (lax.axis_index(name) for name in WIDE + NARROW)
    wide = lax.axis_size("hi") * 4
    tokens = layer_input.shape[0]
    quarter = tokens // 4
    heads = query_bias.shape[0]
    token_count = float(tokens * wide)
    rows = D // wide
    narrow_rows = rows // 4
    bias_part = query_bias.shape[1]
    kv_part = keyvalue_bias.shape[0]
    column_block = c * KV + y
    hidden = gateup_weight.shape[2]
    half = -(-hidden // (2 * LANES)) * LANES
    padding = 2 * half - hidden
    own = c * 2 + y

    kv_columns = low(keyvalue_weight).reshape(narrow_rows, 2, KV, HD)
    kv_columns = jnp.transpose(kv_columns, (2, 1, 0, 3))
    small = jnp.concatenate([low(norm_gains).reshape(-1), low(keyvalue_bias)])
    small = jnp.pad(small, (0, HD - small.shape[0])).reshape(1, 1, 1, HD)
    small = jnp.pad(small, ((0, 0), (0, 0), (0, 15), (0, 0)))
    blocks = jnp.concatenate([kv_columns, jnp.broadcast_to(small, (2, 2, 16, HD))], axis=2)
    blocks = exchange_narrow(blocks).reshape(4, narrow_rows + 16, HD)
    kv_mine = blocks[:, :narrow_rows].reshape(rows, HD)
    small_row = blocks[:, narrow_rows].reshape(1, 4 * HD)
    row_gains = wide_float(blocks[:, narrow_rows, : 2 * narrow_rows])
    row_gains = jnp.transpose(row_gains.reshape(4, 2, narrow_rows), (1, 0, 2)).reshape(2, rows, 1)
    bias_row = jnp.pad(low(query_bias).reshape(1, -1), ((0, 0), (0, 4 * HD - heads * bias_part)))
    extra = jnp.pad(jnp.concatenate([small_row, bias_row]), ((0, 14), (0, 0)))
    my_qkv = wide_float(jnp.concatenate([low(query_weight), kv_mine], axis=1))
    packed = jnp.concatenate([low(my_qkv * row_gains[0]), extra], axis=0)
    side = jnp.pad(low(output_weight).T, ((0, 16), (0, 0)))
    packed = jnp.concatenate([packed, side], axis=1)
    columns, out_columns = wide_columns(packed, 4 * HD)
    others = [swap(column, "x") for column in columns]
    out_others = [swap(column, "x") for column in after(out_columns, others)]
    w_qkv, small_all = assemble(columns, others, rows)
    small_all = wide_float(small_all)
    b_query = small_all[:, 1, : heads * bias_part].reshape(wide, heads, bias_part)
    small_all = small_all[:, 0].reshape(wide, 4, HD)
    gains = small_all[:, :, : 2 * narrow_rows].reshape(wide, 4, 2, narrow_rows)
    gains = jnp.transpose(gains, (2, 0, 1, 3)).reshape(2, D)
    b_kv = small_all[:, :, 2 * narrow_rows : 2 * narrow_rows + kv_part].reshape(2 * KV, HD)
    b_query = jnp.transpose(b_query, (1, 0, 2)).reshape(heads * HD)
    b_qkv = jnp.concatenate([b_query, pick(b_kv, column_block)])
    gain_two = gains[1]

    def padded(shard):
        return jnp.pad(low(shard), ((0, 0), (0, padding)))

    down_shard = hidden_pair([padded(down_weight.T)])
    w_down = lax.all_gather(after(down_shard, columns), ("hi", "lo"), axis=0, tiled=True)
    gateup_shard = hidden_pair(
        after([padded(gateup_weight[:, 0]), padded(gateup_weight[:, 1])], others)
    )
    w_gateup = lax.all_gather(gateup_shard, ("hi", "lo"), axis=0, tiled=True)

    cosine, sine = rotation(positions)
    kv_cosine = jnp.where(c == 0, cosine, 1.0)
    kv_sine = jnp.where(c == 0, sine, 0.0)
    normed_one, queries, kv_own = project(
        layer_input, w_qkv, b_qkv[None], cosine, sine, kv_cosine, kv_sine, heads
    )
    both = after(pair(kv_own, swap(kv_own, "lo"), lo), gateup_shard)
    by_place = pair(both, swap(both, "x"), x)
    kv_row = jnp.transpose(by_place, (1, 0, 2, 3)).reshape(4 * tokens, HD)
    kv_other = swap(kv_row, "c")
    keys = jnp.where(c == 0, kv_row, kv_other)
    values = jnp.where(c == 0, kv_other, kv_row)
    begins = segment_ids - hi * (4 * tokens)
    starts = begins[::BLOCK_Q]
    begins = begins[:, None]
    place = (lo * 2 + x).reshape(1).astype(jnp.int32)
    grad_blocks = grad_out.reshape(4, quarter, D)
    grad_near = [pick(grad_blocks, own ^ d) for d in range(4)]
    grad_far = [swap(part, "x") for part in after(grad_near[:2], kv_row)]
    attention, log_total = attention_forward(queries, keys, values, begins, starts, place)
    w_output, _ = assemble(*after((out_columns, out_others), attention), rows)
    grad_far = after(grad_far, attention)
    ff_grad = stack_rows(grad_near + grad_far + [swap(part, "c") for part in grad_far], range(8))
    attention_low = low(attention)

    def halves(block):
        split = block.reshape(2, -1, block.shape[-1])
        return pick(split, c), pick(split, 1 - c)

    def send_core(kept, sent):
        return kept + wide_float(swap(low(sent), "c"))

    attention_kept, attention_sent = halves(attention_low)
    sent = matmul_nt(attention_sent, w_output)
    out_total = send_core(matmul_nt(attention_kept, w_output), sent)
    out_split = out_total.reshape(2, quarter, D)
    out_other = swap(low(pick(out_split, 1 - y)), "y")
    grad_hidden = low(matmul(after(ff_grad, out_total), w_down))
    out_other = after(out_other, grad_hidden)
    residual = wide_float(pick(layer_input.reshape(4, quarter, D), own))
    residual = residual + pick(out_split, y) + wide_float(out_other)
    inverse_two = lax.rsqrt(jnp.mean(residual * residual, axis=-1, keepdims=True) + norm_eps)
    unit_two = residual * inverse_two
    normed_two = low(unit_two * gain_two)

    by_y = swap(normed_two, "y")
    by_x = swap(normed_two, "x")
    by_both = [swap(by_y[:, : D // 2], "x"), swap(by_x[:, D // 2 :], "y")]
    count = 4 * quarter
    ff_input = stack_rows(
        [normed_two, by_y, swap(normed_two, "c"), swap(by_y, "c")], range(4), count=8
    )
    firsts = feed_forward(ff_input, grad_hidden, w_gateup, half, 0, count)
    by_x, by_both = after((by_x, by_both), firsts[0])
    by_both = jnp.concatenate(by_both, axis=1)
    ff_input = stack_rows(
        [by_x, by_both, swap(by_x, "c"), swap(by_both, "c")], range(4, 8), into=ff_input, count=8
    )
    hidden_all, both_all = feed_forward(
        ff_input, grad_hidden, w_gateup, half, count, count, into=firsts
    )

    half_d = D // 2

    def join_core(sums):
        return wide_float(sums[: 2 * quarter]) + wide_float(swap(sums[2 * quarter :], "c"))

    def first_sends(far_sums, near_sums):
        to_x = low(far_sums[:, :half_d])
        to_y = low(jnp.concatenate([near_sums[quarter:, half_d:], far_sums[quarter:, half_d:]]))
        return to_x, to_y

    def second_sends(far_sums, near_sums, from_x, from_y):
        left = near_sums[:, :half_d] + wide_float(from_x)
        right = near_sums[:quarter, half_d:] + wide_float(from_y[:quarter])
        to_x = low(far_sums[:quarter, half_d:] + wide_float(from_y[quarter:]))
        return (left[:quarter], right), (low(left[quarter:]), to_x)

    def finish_sums(kept, from_y, from_x):
        return jnp.concatenate([kept[0] + wide_float(from_y), kept[1] + wide_float(from_x)], axis=1)

    grad_gateup = low(matmul_tn(ff_input, both_all))
    both_all = after(both_all, grad_gateup)
    feed_far = low(matmul_nt(both_all[count:], w_gateup))
    feed_near = low(matmul_nt(after(both_all, feed_far)[:count], w_gateup))

    def over_rows(grad):
        return lax.psum_scatter(grad, ("hi", "lo"), scatter_dimension=0, tiled=True)

    far_sums, near_sums = join_core(feed_far), join_core(feed_near)
    to_x, to_y = first_sends(far_sums, near_sums)
    from_x, from_y = swap(to_x, "x"), swap(to_y, "y")
    hidden_late = after(hidden_all, to_x, to_y)
    mlp_far = low(matmul_nt(hidden_late[count:], w_down))
    mlp_near = low(matmul_nt(after(hidden_late, mlp_far)[:count], w_down))
    from_x, from_y = after((from_x, from_y), mlp_near)
    kept, (to_y, to_x) = second_sends(far_sums, near_sums, from_x, from_y)
    from_x, from_y = swap(to_x, "x"), swap(to_y, "y")
    grad_normed_two = finish_sums(kept, from_y, from_x)
    grad_residual = wide_float(grad_near[0]) + rms_back(
        grad_normed_two * gain_two, unit_two, inverse_two
    )
    residual_own = low(grad_residual)
    ff_late, hidden_all = after((ff_grad, hidden_all), swap(residual_own, "c"))
    grad_down = low(matmul_tn(ff_late, hidden_all))
    rows_gateup, rows_down = over_rows(grad_gateup), over_rows(grad_down)
    mlp_far, mlp_near = after((mlp_far, mlp_near), residual_own)
    mlp_far, mlp_near = low(join_core(mlp_far)), join_core(mlp_near)
    residual_low = gather_tokens(residual_own, grad_down, mlp_near)

    grad_attention = low(matmul(residual_low, w_output))
    x_output = send_x(
        low(matmul_tn(residual_low, attention_low)).reshape(wide, rows, heads * HD)
    )
    from_far = swap(after(mlp_far, residual_low), "x")
    grad_queries, grad_keys, grad_values = attention_backward(
        queries, keys, values, begins, starts, place, grad_attention, log_total, attention,
        cosine, sine,
    )
    kv_sent = low(jnp.where(c == 0, grad_values, grad_keys))
    kv_sent, from_far, x_output = after((kv_sent, from_far, x_output), grad_queries, rows_gateup)
    rows_output = over_rows(low(add_up(x_output)).reshape(-1, heads * HD))
    mlp_sums = mlp_near + wide_float(from_far)
    from_y = swap(low(mlp_sums[quarter:]), "y")
    kv_grad = jnp.where(c == 0, grad_keys, grad_values) + wide_float(swap(kv_sent, "c"))
    kv_grad = kv_grad.reshape(2, 2, tokens, HD)
    kv_kept, kv_sent = (
        lax.dynamic_index_in_dim(kv_grad, at, axis=1, keepdims=False) for at in (x, 1 - x)
    )
    kv_grad = kv_kept + wide_float(swap(low(kv_sent), "x"))
    parts_gateup = send_hidden(after(rows_gateup, kv_grad))
    from_y = after(from_y, kv_grad)
    layer_own = low(residual + mlp_sums[:quarter] + wide_float(from_y))
    kv_grad = pick(kv_grad, lo) + wide_float(swap(low(pick(kv_grad, 1 - lo)), "lo"))
    turned = jnp.concatenate([kv_grad[:, HD // 2 :], kv_grad[:, : HD // 2]], axis=1)
    grad_kv = low(kv_grad * kv_cosine - turned * kv_sine)
    grad_kv = after(grad_kv, parts_gateup)

    w_query, w_kv = w_qkv[:, : heads * HD], w_qkv[:, heads * HD :]

    def input_part(kv_part_grad, query_part_grad):
        return matmul_nt(query_part_grad, w_query) + matmul_nt(kv_part_grad, w_kv)

    query_kept, query_sent = halves(grad_queries)
    kv_kept, kv_sent = halves(grad_kv)
    part_sent = low(input_part(kv_sent, query_sent))
    part_kept = input_part(kv_kept, query_kept)
    part_total = send_core(part_kept, part_sent)
    part_other = swap(low(part_total), "y")
    layer_by_y = swap(after(layer_own, part_other), "y")
    grad_normed_one = part_total + wide_float(part_other)
    core_input = wide_float(pick(layer_input.reshape(2, 2 * quarter, D), c))
    core_inverse = lax.rsqrt(jnp.mean(core_input * core_input, axis=-1, keepdims=True) + norm_eps)
    core_grad = wide_float(pick(residual_low.reshape(2, 2 * quarter, D), c)) + rms_back(
        grad_normed_one, core_input * core_inverse, core_inverse
    )
    core_grad = low(core_grad)
    input_grad = stack_rows([core_grad, swap(core_grad, "c")], [c, 1 - c])
    layer_output = spread_core(layer_own, after(layer_by_y, core_grad))

    grad_query_weight = low(matmul_tn(normed_one, grad_queries)).reshape(wide, rows, heads * HD)
    grad_kv_weight = low(matmul_tn(normed_one, grad_kv)).reshape(wide, rows, HD)
    bias_query = jnp.sum(wide_float(grad_queries), axis=0).reshape(heads, wide, bias_part)
    bias_query = jnp.transpose(bias_query, (1, 0, 2)).reshape(wide, heads * bias_part)
    kv_sums = jnp.sum(wide_float(grad_kv), axis=0, keepdims=True)
    bias_kv = jnp.where(jnp.arange(2 * KV)[:, None] == column_block, kv_sums, 0.0)
    bias_kv = bias_kv.reshape(wide, 4 * kv_part)
    bias_all = jnp.concatenate([bias_query, bias_kv], axis=1)
    bias_all = jnp.pad(bias_all, ((0, 0), (0, HD - bias_all.shape[1])))
    extra = jnp.pad(low(bias_all)[:, None], ((0, 0), (0, 15), (0, 3 * HD)))
    grad_qkv = jnp.concatenate([grad_query_weight, grad_kv_weight], axis=2)
    x_qkv = send_x(jnp.concatenate([grad_qkv, extra], axis=1))
    sums_qkv = low(add_up(after(x_qkv, part_total, rows_output, rows_down)))
    summed = wide_float(over_rows(sums_qkv.reshape(-1, 4 * HD)))
    summed_query = summed[:rows, : heads * HD]
    summed_kv = summed[:rows, heads * HD :]
    summed_query_bias = summed[rows, : heads * bias_part].reshape(heads, bias_part)
    kv_bias = summed[rows, heads * bias_part : heads * bias_part + 4 * kv_part]
    parts_gateup = after(parts_gateup, sums_qkv)
    parts_down = send_hidden(after(rows_down, sums_qkv))
    summed_gate = join_hidden(*(part[:, :half] for part in parts_gateup))
    summed_up = join_hidden(*(part[:, half:] for part in parts_gateup))
    summed_output = wide_float(after(rows_output, core_grad))

    grad_gain_one = jnp.sum(
        summed_query * my_qkv[:, : heads * HD], axis=1
    ) + jnp.sum(summed_kv * my_qkv[:, heads * HD :], axis=1)
    summed_query = summed_query * row_gains[0]
    summed_kv = summed_kv * row_gains[0]
    summed_gateup = jnp.stack([summed_gate[:, :hidden], summed_up[:, :hidden]], axis=1)
    summed_gateup = with_layout_constraint(summed_gateup, Layout((0, 1, 2)))
    grad_gain_two = (
        jnp.sum(summed_gateup * wide_float(low(gateup_weight)), axis=(1, 2)) / row_gains[1, :, 0]
    )
    gain_parts = jnp.stack([grad_gain_one, grad_gain_two]).reshape(2, 4, narrow_rows)
    gain_parts = jnp.transpose(gain_parts, (1, 0, 2)).reshape(4, 2 * narrow_rows)
    last = jnp.concatenate([gain_parts, kv_bias.reshape(4, kv_part)], axis=1)
    last = jnp.pad(last, ((0, 0), (0, HD - last.shape[1])))[:, None]
    last = jnp.pad(last, ((0, 0), (0, 7), (0, 0)))
    last = jnp.concatenate([summed_kv.reshape(4, narrow_rows, HD), last], axis=1)
    last = exchange_narrow(last.reshape((2, 2) + last.shape[1:]))
    summed_keyvalue = jnp.transpose(last[:, :, :narrow_rows], (2, 1, 0, 3))
    summed_keyvalue = summed_keyvalue.reshape(narrow_rows, 2 * KV * HD)
    small_sums = jnp.sum(last[:, :, narrow_rows], axis=(0, 1))
    summed_gains = small_sums[: 2 * narrow_rows].reshape(2, narrow_rows)
    summed_keyvalue_bias = small_sums[2 * narrow_rows : 2 * narrow_rows + kv_part]
    summed_output = summed_output.T

    gains_update = adam_update(
        summed_gains, norm_gains, norm_gains_first, norm_gains_second, False, token_count
    )
    query_update = adam_update(
        summed_query, query_weight, query_weight_first, query_weight_second, True, token_count
    )
    qbias_update = adam_update(
        summed_query_bias, query_bias, query_bias_first, query_bias_second, False, token_count
    )
    keyvalue_update = adam_update(
        summed_keyvalue,
        keyvalue_weight,
        keyvalue_weight_first,
        keyvalue_weight_second,
        True,
        token_count,
    )
    kvbias_update = adam_update(
        summed_keyvalue_bias,
        keyvalue_bias,
        keyvalue_bias_first,
        keyvalue_bias_second,
        False,
        token_count,
    )
    output_update = adam_update(
        summed_output, output_weight, output_weight_first, output_weight_second, True, token_count
    )
    gateup_update = adam_update(
        summed_gateup, gateup_weight, gateup_weight_first, gateup_weight_second, True, token_count
    )
    summed_down = join_hidden(*after(parts_down, core_grad))[:, :hidden].T
    down_update = adam_update(
        summed_down, down_weight, down_weight_first, down_weight_second, True, token_count
    )
    return (
        layer_output,
        input_grad,
        *gains_update,
        *query_update,
        *qbias_update,
        *keyvalue_update,
        *kvbias_update,
        *output_update,
        *gateup_update,
        *down_update,
    )


def solution(mesh):
    devices = mesh.devices.reshape(-1, 2, 2, 2, 2)
    split = Mesh(devices, WIDE + NARROW)
    token_matrix = P(WIDE, None)
    token_vector = P(WIDE)
    gains = P(None, WIDE + NARROW)
    query = P(WIDE, NARROW)
    by_narrow = P(NARROW, WIDE)
    keyvalue = P(WIDE + NARROW, None)
    keyvalue_bias = P(WIDE + NARROW)
    gateup = P(WIDE, None, NARROW)
    parameters = (gains, query, by_narrow, keyvalue, keyvalue_bias, by_narrow, gateup, by_narrow)
    in_specs = (token_matrix, token_matrix, token_vector, token_vector)
    out_specs = (token_matrix, token_matrix)
    for spec in parameters:
        in_specs += (spec,) * 3
        out_specs += (spec,) * 2
    return jax.shard_map(local, mesh=split, in_specs=in_specs, out_specs=out_specs, check_vma=False)
```

```python
import jax
import jax.numpy as jnp
from jax import lax
from jax.experimental import pallas as pl
from jax.experimental.layout import Layout, with_layout_constraint
from jax.experimental.pallas import tpu as pltpu
from jax.sharding import Mesh
from jax.sharding import PartitionSpec as P

D = 1536
H = 12
KV = 2
HD = 128
LENGTH = 4096
LANES = 128

norm_eps = 1e-06
rope_base = 1000000.0
beta_first = 0.9
beta_second = 0.95
adam_eps = 1e-08
decay_rate = 0.1
first_fix = 1.0 - 0.9**10
second_fix = 1.0 - 0.95**10
masked_score = -1e30

WIDE = ("hi", "lo", "x")
NARROW = ("y", "c")
BLOCK_Q = 512
BLOCK_K = 512


def low(a):
    return a.astype(jnp.bfloat16)


def wide_float(a):
    return a.astype(jnp.float32)


def matmul(left, right):
    return jnp.dot(left, right, preferred_element_type=jnp.float32)


def matmul_nt(left, right):
    return lax.dot_general(left, right, (((1,), (1,)), ((), ())), preferred_element_type=jnp.float32)


def matmul_tn(left, right):
    return lax.dot_general(left, right, (((0,), (0,)), ((), ())), preferred_element_type=jnp.float32)


def swap(block, axis, distance=1):
    size = 1
    for name in axis if isinstance(axis, tuple) else (axis,):
        size *= lax.axis_size(name)
    return lax.ppermute(block, axis, [(i, i ^ distance) for i in range(size)])


def pick(stacked, index):
    return lax.dynamic_index_in_dim(stacked, index, axis=0, keepdims=False)


def pair(mine, other, index):
    return jnp.where(index == 0, jnp.stack([mine, other]), jnp.stack([other, mine]))


def after(value, *needed):
    return lax.optimization_barrier((value, needed))[0]


def wide_columns(block, cut):
    lo = lax.axis_index("lo")
    count = lax.axis_size("hi")
    mine = [block] + [swap(block, "hi", d) for d in range(1, count)]
    other = [swap(part, "lo") for part in mine]
    left = [pair(m[:, :cut], o[:, :cut], lo) for m, o in zip(mine, other)]
    right = [pair(m[:, cut:], o[:, cut:], lo) for m, o in zip(mine, other)]
    return left, right


def stack_rows(blocks, slots, into=None, count=None):
    height, width = blocks[0].shape
    count = len(blocks) if count is None else count
    olds = [] if into is None else [into]

    def kernel(slot_ref, *refs):
        out_ref, sem = refs[-2:]
        copies = []
        for i, block_ref in enumerate(refs[: len(blocks)]):
            start = pl.multiple_of(slot_ref[i] * height, 16)
            copies.append(
                pltpu.make_async_copy(block_ref, out_ref.at[pl.ds(start, height), :], sem.at[i])
            )
        for copy in copies:
            copy.start()
        for copy in copies:
            copy.wait()

    anywhere = pl.BlockSpec(memory_space=pl.ANY)
    slots = jnp.stack([jnp.asarray(slot, jnp.int32) for slot in slots])
    return pl.pallas_call(
        kernel,
        in_specs=[pl.BlockSpec(memory_space=pltpu.SMEM)]
        + [pl.BlockSpec(memory_space=pltpu.VMEM)] * len(blocks)
        + [anywhere] * len(olds),
        out_specs=anywhere,
        out_shape=jax.ShapeDtypeStruct((count * height, width), blocks[0].dtype),
        scratch_shapes=[pltpu.SemaphoreType.DMA((len(blocks),))],
        input_output_aliases={len(blocks) + 1: 0} if olds else {},
        name="stack_rows",
    )(slots, *blocks, *olds)


def assemble(columns, others, rows):
    count = len(columns)
    _, height, width = columns[0].shape
    kind = columns[0].dtype

    def kernel(at_ref, *refs):
        main_ref, extra_ref = refs[-2:]
        for d in range(count):
            for k in range(2):
                part = refs[2 * d + k]
                for low_bit in range(2):
                    index = (at_ref[0] ^ d) * 4 + low_bit * 2 + (at_ref[1] ^ k)
                    start = pl.multiple_of(index * rows, 16)
                    main_ref[pl.ds(start, rows), :] = part[low_bit, :rows]
                    extra_ref[index] = part[low_bit, rows:]

    parts = [part for both in zip(columns, others) for part in both]
    at = jnp.stack([lax.axis_index("hi"), lax.axis_index("x")]).astype(jnp.int32)
    return pl.pallas_call(
        kernel,
        in_specs=[pl.BlockSpec(memory_space=pltpu.SMEM)]
        + [pl.BlockSpec(memory_space=pltpu.VMEM)] * len(parts),
        out_specs=[pl.BlockSpec(memory_space=pltpu.VMEM)] * 2,
        out_shape=[
            jax.ShapeDtypeStruct((count * 4 * rows, width), kind),
            jax.ShapeDtypeStruct((count * 4, height - rows, width), kind),
        ],
        name="assemble",
    )(at, *parts)


def send_x(parts):
    x = lax.axis_index("x")
    parts = parts.reshape((-1, 2, 2) + parts.shape[1:])
    kept = lax.dynamic_index_in_dim(parts, x, axis=2, keepdims=False)
    sent = lax.dynamic_index_in_dim(parts, 1 - x, axis=2, keepdims=False)
    return kept, swap(sent, "x")


def send_hi(parts):
    hi = lax.axis_index("hi")
    turns = range(1, lax.axis_size("hi"))
    return [pick(parts, hi)] + [swap(pick(parts, hi ^ d), "hi", d) for d in turns]


def send_lo(parts):
    lo = lax.axis_index("lo")
    return pick(parts, lo), swap(low(pick(parts, 1 - lo)), "lo")


def add_up(parts):
    return sum(wide_float(part) for part in parts)


def send_hidden(total):
    x = lax.axis_index("x")
    total = total.reshape((2, -1) + total.shape[1:])
    return pick(total, x), swap(pick(total, 1 - x), "x")


def join_hidden(mine, other):
    x = lax.axis_index("x")
    first = jnp.where(x == 0, mine, other)
    second = jnp.where(x == 0, other, mine)
    return wide_float(jnp.concatenate([first, second], axis=1))


def hidden_halves(shards):
    x = lax.axis_index("x")
    half = shards[0].shape[1] // 2

    def part(at):
        return jnp.concatenate(
            [lax.dynamic_slice_in_dim(shard, at * half, half, axis=1) for shard in shards], axis=1
        )

    return part(x), swap(part(1 - x), "x")


def join_rows(mine, other):
    both = pair(mine, other, lax.axis_index("x"))
    return both.reshape((-1,) + both.shape[2:])


def exchange_narrow(blocks):
    y, c = (lax.axis_index(name) for name in NARROW)
    shape = blocks.shape[2:]
    flat = blocks.reshape((4,) + shape)
    me = y * 2 + c
    got = [pick(flat, me)] + [swap(pick(flat, me ^ d), NARROW, d) for d in range(1, 4)]
    near, far = pair(got[0], got[1], c), pair(got[2], got[3], c)
    return pair(near, far, y)


def gather_tokens(block, *needed):
    return spread_core(block, after(swap(block, "y"), *needed))


def spread_core(block, by_y):
    y, c = (lax.axis_index(name) for name in NARROW)
    own = c * 2 + y
    return stack_rows(
        [block, by_y, swap(block, "c"), swap(by_y, "c")], [own, own ^ 1, own ^ 2, own ^ 3]
    )


def rotation(positions):
    half = HD // 2
    freqs = rope_base ** (-2.0 * jnp.arange(half, dtype=jnp.float32) / HD)
    angles = positions.astype(jnp.float32)[:, None] * freqs[None, :]
    cosine, sine = jnp.cos(angles), jnp.sin(angles)
    return jnp.concatenate([cosine, cosine], axis=1), jnp.concatenate([-sine, sine], axis=1)


def rms_back(grad_unit, unit, inverse):
    return inverse * (grad_unit - unit * jnp.mean(grad_unit * unit, axis=-1, keepdims=True))


def adam_update(grad, master, first, second, decay, count):
    mean_grad = grad / count
    first_new = beta_first * first + (1.0 - beta_first) * mean_grad
    second_new = beta_second * second + (1.0 - beta_second) * mean_grad * mean_grad
    update = first_new / first_fix / (jnp.sqrt(second_new / second_fix) + adam_eps)
    if decay:
        update = update + decay_rate * master
    return (grad, update)


def project(layer_input, weight, bias, cosine, sine, kv_cosine, kv_sine, heads):
    tokens = layer_input.shape[0]
    width = weight.shape[1]
    block = 256
    scale = HD ** (-0.5)

    def kernel(x_ref, w_ref, b_ref, c_ref, s_ref, kc_ref, ks_ref, a_ref, q_ref, kv_ref):
        x = wide_float(x_ref[...])
        inverse = lax.rsqrt(jnp.mean(x * x, axis=1, keepdims=True) + norm_eps)
        normed = low(x * inverse)
        a_ref[...] = normed
        linear = matmul(normed, w_ref[...]) + b_ref[...]
        for h in range(heads + 1):
            part = linear[:, h * HD : (h + 1) * HD]
            turned = pltpu.roll(part, HD // 2, axis=1)
            if h < heads:
                out = (part * c_ref[...] + turned * s_ref[...]) * scale
                q_ref[:, h * HD : (h + 1) * HD] = low(out)
            else:
                kv_ref[...] = low(part * kc_ref[...] + turned * ks_ref[...])

    def by_tokens(columns):
        return pl.BlockSpec((block, columns), lambda i: (i, 0))

    def whole(a):
        return pl.BlockSpec(a.shape, lambda i: (0, 0))

    return pl.pallas_call(
        kernel,
        grid=(tokens // block,),
        in_specs=[by_tokens(D), whole(weight), whole(bias)] + [by_tokens(HD)] * 4,
        out_specs=[by_tokens(D), by_tokens(heads * HD), by_tokens(HD)],
        out_shape=[
            jax.ShapeDtypeStruct((tokens, D), jnp.bfloat16),
            jax.ShapeDtypeStruct((tokens, heads * HD), jnp.bfloat16),
            jax.ShapeDtypeStruct((tokens, HD), jnp.bfloat16),
        ],
        name="project",
    )(layer_input, weight, bias, cosine, sine, kv_cosine, kv_sine)


def feed_forward(tokens_in, grads_in, w_gateup, half, at, count, into=None):
    tokens = tokens_in.shape[0]
    block = 512
    olds = [] if into is None else list(into)
    skip = at // block

    def kernel(b_ref, g_ref, wgu_ref, *refs):
        hid_ref, dgu_ref = refs[-2:]
        both = matmul(b_ref[...], wgu_ref[...])
        gate, upward = both[:, :half], both[:, half:]
        grad = wide_float(g_ref[...])
        logistic = jax.nn.sigmoid(gate)
        active = gate * logistic
        hid_ref[...] = low(active * upward)
        slope = logistic + active * (1.0 - logistic)
        dgu_ref[:, :half] = low(grad * upward * slope)
        dgu_ref[:, half:] = low(grad * active)

    def by_tokens(columns):
        return pl.BlockSpec((block, columns), lambda i: (i + skip, 0))

    return pl.pallas_call(
        kernel,
        grid=(count // block,),
        in_specs=[
            by_tokens(D),
            by_tokens(half),
            pl.BlockSpec(w_gateup.shape, lambda i: (0, 0), pipeline_mode=pl.Buffered(1)),
        ]
        + [pl.BlockSpec(memory_space=pl.ANY)] * len(olds),
        out_specs=[by_tokens(half), by_tokens(2 * half)],
        out_shape=[
            jax.ShapeDtypeStruct((tokens, half), jnp.bfloat16),
            jax.ShapeDtypeStruct((tokens, 2 * half), jnp.bfloat16),
        ],
        input_output_aliases={3: 0, 4: 1} if olds else {},
        name="feed_forward",
    )(tokens_in, grads_in, w_gateup, *olds)


def over_blocks(first_begin, last_begin, base, run, carry):
    first = first_begin // BLOCK_K
    end = (base + BLOCK_Q - 1) // BLOCK_K + 1
    clear = jnp.minimum((last_begin + BLOCK_K - 1) // BLOCK_K, end)
    clear_end = jnp.maximum((base + 1) // BLOCK_K, clear)
    before = clear - first

    def edge(t, carry):
        return run(jnp.where(t < before, first + t, clear_end + t - before), carry, True)

    carry = lax.fori_loop(clear, clear_end, lambda j, carry: run(j, carry, False), carry)
    return lax.fori_loop(0, before + end - clear_end, edge, carry)


def stacked_heads(ref, heads):
    return jnp.concatenate([ref[:, h * HD : (h + 1) * HD] for h in range(heads)], axis=0)


def attention_forward(queries, keys, values, begins, starts, place):
    tokens, columns = queries.shape
    heads = columns // HD
    length = keys.shape[0]
    rows = heads * BLOCK_Q

    def kernel(starts_ref, place_ref, q_ref, k_ref, v_ref, begin_ref, o_ref, lse_ref):
        step = pl.program_id(0)
        base = place_ref[0] * tokens + step * BLOCK_Q
        q = stacked_heads(q_ref, heads)
        row = base + lax.broadcasted_iota(jnp.int32, (BLOCK_Q, 1), 0)
        row = jnp.concatenate([row] * heads, axis=0)
        begin = jnp.concatenate([begin_ref[...]] * heads, axis=0)

        def run(j, carry, masked):
            top, total, acc = carry
            at = pl.multiple_of(j * BLOCK_K, BLOCK_K)
            k = k_ref[pl.ds(at, BLOCK_K), :]
            v = v_ref[pl.ds(at, BLOCK_K), :]
            s = matmul_nt(q, k)
            if masked:
                col = at + lax.broadcasted_iota(jnp.int32, (1, BLOCK_K), 1)
                s = jnp.where((col <= row) & (col >= begin), s, masked_score)
            new_top = jnp.maximum(top, jnp.max(s, axis=1, keepdims=True))
            p = jnp.exp(s - new_top)
            scale = jnp.exp(top - new_top)
            total = scale * total + jnp.sum(p, axis=1, keepdims=True)
            acc = scale * acc + matmul(low(p), v)
            return new_top, total, acc

        top, total, acc = over_blocks(
            starts_ref[2 * step],
            starts_ref[2 * step + 1],
            base,
            run,
            (
                jnp.full((rows, 1), masked_score, jnp.float32),
                jnp.zeros((rows, 1), jnp.float32),
                jnp.zeros((rows, HD), jnp.float32),
            ),
        )
        out = acc / total
        for h in range(heads):
            o_ref[:, h * HD : (h + 1) * HD] = out[h * BLOCK_Q : (h + 1) * BLOCK_Q]
        lse_ref[...] = (top + jnp.log(total)).reshape(heads, BLOCK_Q, 1)

    block = pl.BlockSpec((BLOCK_Q, columns), lambda i, *_: (i, 0))
    whole = pl.BlockSpec((length, HD), lambda i, *_: (0, 0))
    return pl.pallas_call(
        kernel,
        grid_spec=pltpu.PrefetchScalarGridSpec(
            num_scalar_prefetch=2,
            grid=(tokens // BLOCK_Q,),
            in_specs=[block, whole, whole, pl.BlockSpec((BLOCK_Q, 1), lambda i, *_: (i, 0))],
            out_specs=[block, pl.BlockSpec((heads, BLOCK_Q, 1), lambda i, *_: (0, i, 0))],
        ),
        out_shape=[
            jax.ShapeDtypeStruct((tokens, columns), jnp.float32),
            jax.ShapeDtypeStruct((heads, tokens, 1), jnp.float32),
        ],
        compiler_params=pltpu.CompilerParams(dimension_semantics=("arbitrary",)),
        name="attention_forward",
    )(starts, place, queries, keys, values, begins)


def attention_backward(
    queries, keys, values, begins, starts, place, grads, lse, outputs, cosine, sine
):
    tokens, columns = queries.shape
    heads = columns // HD
    length = keys.shape[0]
    rows = heads * BLOCK_Q

    def kernel(
        starts_ref, place_ref, q_ref, k_ref, v_ref, begin_ref, g_ref, lse_ref, o_ref,
        c_ref, s_ref, dq_ref, dk_ref, dv_ref,
    ):
        step = pl.program_id(0)

        @pl.when(step == 0)
        def _():
            dk_ref[...] = jnp.zeros_like(dk_ref)
            dv_ref[...] = jnp.zeros_like(dv_ref)

        base = place_ref[0] * tokens + step * BLOCK_Q
        q = stacked_heads(q_ref, heads)
        g = stacked_heads(g_ref, heads)
        delta = jnp.sum(wide_float(g) * stacked_heads(o_ref, heads), axis=1, keepdims=True)
        lse = lse_ref[...].reshape(rows, 1)
        row = base + lax.broadcasted_iota(jnp.int32, (BLOCK_Q, 1), 0)
        row = jnp.concatenate([row] * heads, axis=0)
        begin = jnp.concatenate([begin_ref[...]] * heads, axis=0)

        def less(a, column):
            high = low(-column)
            middle = low(-column - wide_float(high))
            last = low(-column - wide_float(high) - wide_float(middle))
            lane = lax.broadcasted_iota(jnp.int32, (rows, HD), 1)
            parts = jnp.where(lane == 1, middle, jnp.where(lane == 2, last, jnp.zeros_like(last)))
            return jnp.concatenate([a, jnp.where(lane == 0, high, parts)], axis=1)

        q_less = less(q, lse)
        g_less = less(g, delta)
        ones = jnp.ones((BLOCK_K, HD), jnp.bfloat16)

        def run(j, dq, masked):
            at = pl.multiple_of(j * BLOCK_K, BLOCK_K)
            k = k_ref[pl.ds(at, BLOCK_K), :]
            v = v_ref[pl.ds(at, BLOCK_K), :]
            s = matmul_nt(q_less, jnp.concatenate([k, ones], axis=1))
            if masked:
                col = at + lax.broadcasted_iota(jnp.int32, (1, BLOCK_K), 1)
                s = jnp.where((col <= row) & (col >= begin), s, masked_score)
            p = jnp.exp(s)
            ds = low(p * matmul_nt(g_less, jnp.concatenate([v, ones], axis=1)))
            dk_ref[pl.ds(at, BLOCK_K), :] += matmul_tn(ds, q)
            dv_ref[pl.ds(at, BLOCK_K), :] += matmul_tn(low(p), g)
            return dq + matmul(ds, k)

        dq = over_blocks(
            starts_ref[2 * step],
            starts_ref[2 * step + 1],
            base,
            run,
            jnp.zeros((rows, HD), jnp.float32),
        )
        for h in range(heads):
            part = dq[h * BLOCK_Q : (h + 1) * BLOCK_Q]
            turned = pltpu.roll(part, HD // 2, axis=1)
            part = (part * c_ref[...] - turned * s_ref[...]) * HD ** (-0.5)
            dq_ref[:, h * HD : (h + 1) * HD] = low(part)

    block = pl.BlockSpec((BLOCK_Q, columns), lambda i, *_: (i, 0))
    whole = pl.BlockSpec((length, HD), lambda i, *_: (0, 0))
    return pl.pallas_call(
        kernel,
        grid_spec=pltpu.PrefetchScalarGridSpec(
            num_scalar_prefetch=2,
            grid=(tokens // BLOCK_Q,),
            in_specs=[
                block,
                whole,
                whole,
                pl.BlockSpec((BLOCK_Q, 1), lambda i, *_: (i, 0)),
                block,
                pl.BlockSpec((heads, BLOCK_Q, 1), lambda i, *_: (0, i, 0)),
                block,
                pl.BlockSpec((BLOCK_Q, HD), lambda i, *_: (i, 0)),
                pl.BlockSpec((BLOCK_Q, HD), lambda i, *_: (i, 0)),
            ],
            out_specs=[block, whole, whole],
        ),
        out_shape=[
            jax.ShapeDtypeStruct((tokens, columns), jnp.bfloat16),
            jax.ShapeDtypeStruct((length, HD), jnp.float32),
            jax.ShapeDtypeStruct((length, HD), jnp.float32),
        ],
        compiler_params=pltpu.CompilerParams(dimension_semantics=("arbitrary",)),
        cost_estimate=pl.CostEstimate(
            flops=20 * tokens * tokens * columns, transcendentals=0, bytes_accessed=0
        ),
        name="attention_backward",
    )(starts, place, queries, keys, values, begins, grads, lse, outputs, cosine, sine)


def local(
    layer_input,
    grad_out,
    segment_ids,
    positions,
    norm_gains,
    norm_gains_first,
    norm_gains_second,
    query_weight,
    query_weight_first,
    query_weight_second,
    query_bias,
    query_bias_first,
    query_bias_second,
    keyvalue_weight,
    keyvalue_weight_first,
    keyvalue_weight_second,
    keyvalue_bias,
    keyvalue_bias_first,
    keyvalue_bias_second,
    output_weight,
    output_weight_first,
    output_weight_second,
    gateup_weight,
    gateup_weight_first,
    gateup_weight_second,
    down_weight,
    down_weight_first,
    down_weight_second,
):
    hi, lo, x, y, c = (lax.axis_index(name) for name in WIDE + NARROW)
    wide = lax.axis_size("hi") * 4
    tokens = layer_input.shape[0]
    quarter = tokens // 4
    heads = query_bias.shape[0]
    token_count = float(tokens * wide)
    rows = D // wide
    narrow_rows = rows // 4
    bias_part = query_bias.shape[1]
    kv_part = keyvalue_bias.shape[0]
    column_block = c * KV + y
    hidden = gateup_weight.shape[2]
    half = -(-hidden // (2 * LANES)) * LANES
    padding = 2 * half - hidden
    own = c * 2 + y

    kv_columns = low(keyvalue_weight).reshape(narrow_rows, 2, KV, HD)
    kv_columns = jnp.transpose(kv_columns, (2, 1, 0, 3))
    small = jnp.concatenate([low(norm_gains).reshape(-1), low(keyvalue_bias)])
    small = jnp.pad(small, (0, HD - small.shape[0])).reshape(1, 1, 1, HD)
    small = jnp.pad(small, ((0, 0), (0, 0), (0, 15), (0, 0)))
    blocks = jnp.concatenate([kv_columns, jnp.broadcast_to(small, (2, 2, 16, HD))], axis=2)
    blocks = exchange_narrow(blocks).reshape(4, narrow_rows + 16, HD)
    kv_mine = blocks[:, :narrow_rows].reshape(rows, HD)
    small_row = blocks[:, narrow_rows].reshape(1, 4 * HD)
    row_gains = wide_float(blocks[:, narrow_rows, : 2 * narrow_rows])
    row_gains = jnp.transpose(row_gains.reshape(4, 2, narrow_rows), (1, 0, 2)).reshape(2, rows, 1)
    bias_row = jnp.pad(low(query_bias).reshape(1, -1), ((0, 0), (0, 4 * HD - heads * bias_part)))
    extra = jnp.pad(jnp.concatenate([small_row, bias_row]), ((0, 14), (0, 0)))
    my_qkv = wide_float(jnp.concatenate([low(query_weight), kv_mine], axis=1))
    packed = jnp.concatenate([low(my_qkv * row_gains[0]), extra], axis=0)
    side = jnp.pad(low(output_weight).T, ((0, 16), (0, 0)))
    packed = jnp.concatenate([packed, side], axis=1)
    columns, out_columns = wide_columns(packed, 4 * HD)
    others = [swap(column, "x") for column in columns]
    out_others = [swap(column, "x") for column in after(out_columns, others)]
    w_qkv, small_all = assemble(columns, others, rows)
    small_all = wide_float(small_all)
    b_query = small_all[:, 1, : heads * bias_part].reshape(wide, heads, bias_part)
    small_all = small_all[:, 0].reshape(wide, 4, HD)
    gains = small_all[:, :, : 2 * narrow_rows].reshape(wide, 4, 2, narrow_rows)
    gains = jnp.transpose(gains, (2, 0, 1, 3)).reshape(2, D)
    b_kv = small_all[:, :, 2 * narrow_rows : 2 * narrow_rows + kv_part].reshape(2 * KV, HD)
    b_query = jnp.transpose(b_query, (1, 0, 2)).reshape(heads * HD)
    b_qkv = jnp.concatenate([b_query, pick(b_kv, column_block)])
    gain_two = gains[1]

    def padded(shard):
        return jnp.pad(low(shard), ((0, 0), (0, padding)))

    down_shard = join_rows(*hidden_halves([padded(down_weight.T)]))
    w_down = lax.all_gather(after(down_shard, columns), ("hi", "lo"), axis=0, tiled=True)
    gateup_halves = hidden_halves(
        after([padded(gateup_weight[:, 0]), padded(gateup_weight[:, 1])], others)
    )

    cosine, sine = rotation(positions)
    kv_cosine = jnp.where(c == 0, cosine, 1.0)
    kv_sine = jnp.where(c == 0, sine, 0.0)
    normed_one, queries, kv_own = project(
        layer_input, w_qkv, b_qkv[None], cosine, sine, kv_cosine, kv_sine, heads
    )
    gateup_shard = join_rows(*after(gateup_halves, kv_own))
    w_gateup = lax.all_gather(gateup_shard, ("hi", "lo"), axis=0, tiled=True)
    both = after(pair(kv_own, swap(kv_own, "lo"), lo), gateup_shard)
    by_place = pair(both, swap(both, "x"), x)
    kv_row = jnp.transpose(by_place, (1, 0, 2, 3)).reshape(4 * tokens, HD)
    kv_other = swap(kv_row, "c")
    keys = jnp.where(c == 0, kv_row, kv_other)
    values = jnp.where(c == 0, kv_other, kv_row)
    begins = segment_ids - hi * (4 * tokens)
    starts = jnp.stack([begins[::BLOCK_Q], begins[BLOCK_Q - 1 :: BLOCK_Q]], axis=1).reshape(-1)
    begins = begins[:, None]
    place = (lo * 2 + x).reshape(1).astype(jnp.int32)
    grad_blocks = grad_out.reshape(4, quarter, D)
    grad_near = [pick(grad_blocks, own ^ d) for d in range(4)]
    grad_far = [swap(part, "x") for part in after(grad_near[:2], kv_row)]
    attention, log_total = attention_forward(queries, keys, values, begins, starts, place)
    w_output, _ = assemble(*after((out_columns, out_others), attention), rows)
    grad_far = after(grad_far, attention)
    ff_grad = stack_rows(grad_near + grad_far + [swap(part, "c") for part in grad_far], range(8))
    attention_low = low(attention)

    def halves(block):
        split = block.reshape(2, -1, block.shape[-1])
        return pick(split, c), pick(split, 1 - c)

    def send_core(kept, sent):
        return kept + wide_float(swap(low(sent), "c"))

    attention_kept, attention_sent = halves(attention_low)
    sent = matmul_nt(attention_sent, w_output)
    out_total = send_core(matmul_nt(attention_kept, w_output), sent)
    out_split = out_total.reshape(2, quarter, D)
    out_other = swap(low(pick(out_split, 1 - y)), "y")
    grad_hidden = low(matmul(after(ff_grad, out_total), w_down))
    out_other = after(out_other, grad_hidden)
    residual = wide_float(pick(layer_input.reshape(4, quarter, D), own))
    residual = residual + pick(out_split, y) + wide_float(out_other)
    inverse_two = lax.rsqrt(jnp.mean(residual * residual, axis=-1, keepdims=True) + norm_eps)
    unit_two = residual * inverse_two
    normed_two = low(unit_two * gain_two)

    by_y = swap(normed_two, "y")
    by_x = swap(normed_two, "x")
    by_both = [swap(by_y[:, : D // 2], "x"), swap(by_x[:, D // 2 :], "y")]
    count = 4 * quarter
    ff_input = stack_rows(
        [normed_two, by_y, swap(normed_two, "c"), swap(by_y, "c")], range(4), count=8
    )
    firsts = feed_forward(ff_input, grad_hidden, w_gateup, half, 0, count)
    by_x, by_both = after((by_x, by_both), firsts[0])
    by_both = jnp.concatenate(by_both, axis=1)
    ff_input = stack_rows(
        [by_x, by_both, swap(by_x, "c"), swap(by_both, "c")], range(4, 8), into=ff_input, count=8
    )
    hidden_all, both_all = feed_forward(
        ff_input, grad_hidden, w_gateup, half, count, count, into=firsts
    )

    half_d = D // 2

    def join_core(sums):
        return wide_float(sums[: 2 * quarter]) + wide_float(swap(sums[2 * quarter :], "c"))

    def first_sends(far_sums, near_sums):
        to_x = low(far_sums[:, :half_d])
        to_y = low(jnp.concatenate([near_sums[quarter:, half_d:], far_sums[quarter:, half_d:]]))
        return to_x, to_y

    def second_sends(far_sums, near_sums, from_x, from_y):
        left = near_sums[:, :half_d] + wide_float(from_x)
        right = near_sums[:quarter, half_d:] + wide_float(from_y[:quarter])
        to_x = low(far_sums[:quarter, half_d:] + wide_float(from_y[quarter:]))
        return (left[:quarter], right), (low(left[quarter:]), to_x)

    def finish_sums(kept, from_y, from_x):
        return jnp.concatenate([kept[0] + wide_float(from_y), kept[1] + wide_float(from_x)], axis=1)

    grad_gateup = low(matmul_tn(ff_input, both_all))
    both_all = after(both_all, grad_gateup)
    feed_far = low(matmul_nt(both_all[count:], w_gateup))
    feed_near = low(matmul_nt(after(both_all, feed_far)[:count], w_gateup))

    def over_rows(grad):
        return lax.psum_scatter(grad, ("hi", "lo"), scatter_dimension=0, tiled=True)

    far_sums, near_sums = join_core(feed_far), join_core(feed_near)
    to_x, to_y = first_sends(far_sums, near_sums)
    from_x, from_y = swap(to_x, "x"), swap(to_y, "y")
    hidden_late = after(hidden_all, to_x, to_y)
    mlp_far = low(matmul_nt(hidden_late[count:], w_down))
    mlp_near = low(matmul_nt(after(hidden_late, mlp_far)[:count], w_down))
    from_x, from_y = after((from_x, from_y), mlp_near)
    kept, (to_y, to_x) = second_sends(far_sums, near_sums, from_x, from_y)
    from_x, from_y = swap(to_x, "x"), swap(to_y, "y")
    grad_normed_two = finish_sums(kept, from_y, from_x)
    grad_residual = wide_float(grad_near[0]) + rms_back(
        grad_normed_two * gain_two, unit_two, inverse_two
    )
    residual_own = low(grad_residual)
    ff_late, hidden_all = after((ff_grad, hidden_all), swap(residual_own, "c"))
    grad_down = low(matmul_tn(ff_late, hidden_all))
    rows_gateup, rows_down = over_rows(grad_gateup), over_rows(grad_down)
    mlp_far, mlp_near = after((mlp_far, mlp_near), residual_own)
    mlp_far, mlp_near = low(join_core(mlp_far)), join_core(mlp_near)
    residual_low = gather_tokens(residual_own, grad_down, mlp_near)

    grad_attention = low(matmul(residual_low, w_output))
    x_output = send_x(
        low(matmul_tn(residual_low, attention_low)).reshape(wide, rows, heads * HD)
    )
    from_far = swap(after(mlp_far, residual_low), "x")
    grad_queries, grad_keys, grad_values = attention_backward(
        queries, keys, values, begins, starts, place, grad_attention, log_total, attention,
        cosine, sine,
    )
    kv_sent = low(jnp.where(c == 0, grad_values, grad_keys))
    kv_sent, from_far, x_output = after((kv_sent, from_far, x_output), grad_queries, rows_gateup)
    rows_output = over_rows(low(add_up(x_output)).reshape(-1, heads * HD))
    mlp_sums = mlp_near + wide_float(from_far)
    from_y = swap(low(mlp_sums[quarter:]), "y")
    kv_grad = jnp.where(c == 0, grad_keys, grad_values) + wide_float(swap(kv_sent, "c"))
    kv_grad = kv_grad.reshape(2, 2, tokens, HD)
    kv_kept, kv_sent = (
        lax.dynamic_index_in_dim(kv_grad, at, axis=1, keepdims=False) for at in (x, 1 - x)
    )
    kv_grad = kv_kept + wide_float(swap(low(kv_sent), "x"))
    parts_gateup = send_hidden(after(rows_gateup, kv_grad))
    from_y = after(from_y, kv_grad)
    layer_own = low(residual + mlp_sums[:quarter] + wide_float(from_y))
    kv_grad = pick(kv_grad, lo) + wide_float(swap(low(pick(kv_grad, 1 - lo)), "lo"))
    turned = jnp.concatenate([kv_grad[:, HD // 2 :], kv_grad[:, : HD // 2]], axis=1)
    grad_kv = low(kv_grad * kv_cosine - turned * kv_sine)
    grad_kv = after(grad_kv, parts_gateup)

    w_query, w_kv = w_qkv[:, : heads * HD], w_qkv[:, heads * HD :]

    def input_part(kv_part_grad, query_part_grad):
        return matmul_nt(query_part_grad, w_query) + matmul_nt(kv_part_grad, w_kv)

    query_kept, query_sent = halves(grad_queries)
    kv_kept, kv_sent = halves(grad_kv)
    part_sent = low(input_part(kv_sent, query_sent))
    part_kept = input_part(kv_kept, query_kept)
    part_total = send_core(part_kept, part_sent)
    part_other = swap(low(part_total), "y")
    layer_by_y = swap(after(layer_own, part_other), "y")
    grad_normed_one = part_total + wide_float(part_other)
    core_input = wide_float(pick(layer_input.reshape(2, 2 * quarter, D), c))
    core_inverse = lax.rsqrt(jnp.mean(core_input * core_input, axis=-1, keepdims=True) + norm_eps)
    core_grad = wide_float(pick(residual_low.reshape(2, 2 * quarter, D), c)) + rms_back(
        grad_normed_one, core_input * core_inverse, core_inverse
    )
    core_grad = low(core_grad)
    input_grad = stack_rows([core_grad, swap(core_grad, "c")], [c, 1 - c])
    layer_output = spread_core(layer_own, after(layer_by_y, core_grad))

    grad_query_weight = low(matmul_tn(normed_one, grad_queries)).reshape(wide, rows, heads * HD)
    grad_kv_weight = low(matmul_tn(normed_one, grad_kv)).reshape(wide, rows, HD)
    bias_query = jnp.sum(wide_float(grad_queries), axis=0).reshape(heads, wide, bias_part)
    bias_query = jnp.transpose(bias_query, (1, 0, 2)).reshape(wide, heads * bias_part)
    kv_sums = jnp.sum(wide_float(grad_kv), axis=0, keepdims=True)
    bias_kv = jnp.where(jnp.arange(2 * KV)[:, None] == column_block, kv_sums, 0.0)
    bias_kv = bias_kv.reshape(wide, 4 * kv_part)
    bias_all = jnp.concatenate([bias_query, bias_kv], axis=1)
    bias_all = jnp.pad(bias_all, ((0, 0), (0, HD - bias_all.shape[1])))
    extra = jnp.pad(low(bias_all)[:, None], ((0, 0), (0, 15), (0, 3 * HD)))
    grad_qkv = jnp.concatenate([grad_query_weight, grad_kv_weight], axis=2)
    x_qkv = send_x(jnp.concatenate([grad_qkv, extra], axis=1))
    sums_qkv = low(add_up(after(x_qkv, part_total, rows_output, rows_down)))
    summed = wide_float(over_rows(sums_qkv.reshape(-1, 4 * HD)))
    summed_query = summed[:rows, : heads * HD]
    summed_kv = summed[:rows, heads * HD :]
    summed_query_bias = summed[rows, : heads * bias_part].reshape(heads, bias_part)
    kv_bias = summed[rows, heads * bias_part : heads * bias_part + 4 * kv_part]
    parts_gateup = after(parts_gateup, sums_qkv)
    parts_down = send_hidden(after(rows_down, sums_qkv))
    summed_gate = join_hidden(*(part[:, :half] for part in parts_gateup))
    summed_up = join_hidden(*(part[:, half:] for part in parts_gateup))
    summed_output = wide_float(after(rows_output, core_grad))

    grad_gain_one = jnp.sum(
        summed_query * my_qkv[:, : heads * HD], axis=1
    ) + jnp.sum(summed_kv * my_qkv[:, heads * HD :], axis=1)
    summed_query = summed_query * row_gains[0]
    summed_kv = summed_kv * row_gains[0]
    summed_gateup = jnp.stack([summed_gate[:, :hidden], summed_up[:, :hidden]], axis=1)
    summed_gateup = with_layout_constraint(summed_gateup, Layout((0, 1, 2)))
    grad_gain_two = (
        jnp.sum(summed_gateup * wide_float(low(gateup_weight)), axis=(1, 2)) / row_gains[1, :, 0]
    )
    gain_parts = jnp.stack([grad_gain_one, grad_gain_two]).reshape(2, 4, narrow_rows)
    gain_parts = jnp.transpose(gain_parts, (1, 0, 2)).reshape(4, 2 * narrow_rows)
    last = jnp.concatenate([gain_parts, kv_bias.reshape(4, kv_part)], axis=1)
    last = jnp.pad(last, ((0, 0), (0, HD - last.shape[1])))[:, None]
    last = jnp.pad(last, ((0, 0), (0, 7), (0, 0)))
    last = jnp.concatenate([summed_kv.reshape(4, narrow_rows, HD), last], axis=1)
    last = exchange_narrow(last.reshape((2, 2) + last.shape[1:]))
    summed_keyvalue = jnp.transpose(last[:, :, :narrow_rows], (2, 1, 0, 3))
    summed_keyvalue = summed_keyvalue.reshape(narrow_rows, 2 * KV * HD)
    small_sums = jnp.sum(last[:, :, narrow_rows], axis=(0, 1))
    summed_gains = small_sums[: 2 * narrow_rows].reshape(2, narrow_rows)
    summed_keyvalue_bias = small_sums[2 * narrow_rows : 2 * narrow_rows + kv_part]
    summed_output = summed_output.T

    gains_update = adam_update(
        summed_gains, norm_gains, norm_gains_first, norm_gains_second, False, token_count
    )
    query_update = adam_update(
        summed_query, query_weight, query_weight_first, query_weight_second, True, token_count
    )
    qbias_update = adam_update(
        summed_query_bias, query_bias, query_bias_first, query_bias_second, False, token_count
    )
    keyvalue_update = adam_update(
        summed_keyvalue,
        keyvalue_weight,
        keyvalue_weight_first,
        keyvalue_weight_second,
        True,
        token_count,
    )
    kvbias_update = adam_update(
        summed_keyvalue_bias,
        keyvalue_bias,
        keyvalue_bias_first,
        keyvalue_bias_second,
        False,
        token_count,
    )
    output_update = adam_update(
        summed_output, output_weight, output_weight_first, output_weight_second, True, token_count
    )
    gateup_update = adam_update(
        summed_gateup, gateup_weight, gateup_weight_first, gateup_weight_second, True, token_count
    )
    summed_down = join_hidden(*after(parts_down, core_grad))[:, :hidden].T
    down_update = adam_update(
        summed_down, down_weight, down_weight_first, down_weight_second, True, token_count
    )
    return (
        layer_output,
        input_grad,
        *gains_update,
        *query_update,
        *qbias_update,
        *keyvalue_update,
        *kvbias_update,
        *output_update,
        *gateup_update,
        *down_update,
    )


def solution(mesh):
    devices = mesh.devices.reshape(-1, 2, 2, 2, 2)
    split = Mesh(devices, WIDE + NARROW)
    token_matrix = P(WIDE, None)
    token_vector = P(WIDE)
    gains = P(None, WIDE + NARROW)
    query = P(WIDE, NARROW)
    by_narrow = P(NARROW, WIDE)
    keyvalue = P(WIDE + NARROW, None)
    keyvalue_bias = P(WIDE + NARROW)
    gateup = P(WIDE, None, NARROW)
    parameters = (gains, query, by_narrow, keyvalue, keyvalue_bias, by_narrow, gateup, by_narrow)
    in_specs = (token_matrix, token_matrix, token_vector, token_vector)
    out_specs = (token_matrix, token_matrix)
    for spec in parameters:
        in_specs += (spec,) * 3
        out_specs += (spec,) * 2
    return jax.shard_map(local, mesh=split, in_specs=in_specs, out_specs=out_specs, check_vma=False)
```

```python
import jax
import jax.numpy as jnp
from jax import lax
from jax.experimental import pallas as pl
from jax.experimental.layout import Layout, with_layout_constraint
from jax.experimental.pallas import tpu as pltpu
from jax.sharding import Mesh
from jax.sharding import PartitionSpec as P

D = 1536
H = 12
KV = 2
HD = 128
LENGTH = 4096
LANES = 128

norm_eps = 1e-06
rope_base = 1000000.0
beta_first = 0.9
beta_second = 0.95
adam_eps = 1e-08
decay_rate = 0.1
first_fix = 1.0 - 0.9**10
second_fix = 1.0 - 0.95**10
masked_score = -1e30

WIDE = ("hi", "lo", "x")
NARROW = ("y", "c")
BLOCK_Q = 512
BLOCK_K = 512


def low(a):
    return a.astype(jnp.bfloat16)


def wide_float(a):
    return a.astype(jnp.float32)


def matmul(left, right):
    return jnp.dot(left, right, preferred_element_type=jnp.float32)


def matmul_nt(left, right):
    return lax.dot_general(left, right, (((1,), (1,)), ((), ())), preferred_element_type=jnp.float32)


def matmul_tn(left, right):
    return lax.dot_general(left, right, (((0,), (0,)), ((), ())), preferred_element_type=jnp.float32)


def swap(block, axis, distance=1):
    size = 1
    for name in axis if isinstance(axis, tuple) else (axis,):
        size *= lax.axis_size(name)
    return lax.ppermute(block, axis, [(i, i ^ distance) for i in range(size)])


def pick(stacked, index):
    return lax.dynamic_index_in_dim(stacked, index, axis=0, keepdims=False)


def pair(mine, other, index):
    return jnp.where(index == 0, jnp.stack([mine, other]), jnp.stack([other, mine]))


def after(value, *needed):
    return lax.optimization_barrier((value, needed))[0]


def wide_columns(block, cut):
    lo = lax.axis_index("lo")
    count = lax.axis_size("hi")
    mine = [block] + [swap(block, "hi", d) for d in range(1, count)]
    other = [swap(part, "lo") for part in mine]
    left = [pair(m[:, :cut], o[:, :cut], lo) for m, o in zip(mine, other)]
    right = [pair(m[:, cut:], o[:, cut:], lo) for m, o in zip(mine, other)]
    return left, right


def stack_rows(blocks, slots, into=None, count=None):
    height, width = blocks[0].shape
    count = len(blocks) if count is None else count
    olds = [] if into is None else [into]

    def kernel(slot_ref, *refs):
        out_ref, sem = refs[-2:]
        copies = []
        for i, block_ref in enumerate(refs[: len(blocks)]):
            start = pl.multiple_of(slot_ref[i] * height, 16)
            copies.append(
                pltpu.make_async_copy(block_ref, out_ref.at[pl.ds(start, height), :], sem.at[i])
            )
        for copy in copies:
            copy.start()
        for copy in copies:
            copy.wait()

    anywhere = pl.BlockSpec(memory_space=pl.ANY)
    slots = jnp.stack([jnp.asarray(slot, jnp.int32) for slot in slots])
    return pl.pallas_call(
        kernel,
        in_specs=[pl.BlockSpec(memory_space=pltpu.SMEM)]
        + [pl.BlockSpec(memory_space=pltpu.VMEM)] * len(blocks)
        + [anywhere] * len(olds),
        out_specs=anywhere,
        out_shape=jax.ShapeDtypeStruct((count * height, width), blocks[0].dtype),
        scratch_shapes=[pltpu.SemaphoreType.DMA((len(blocks),))],
        input_output_aliases={len(blocks) + 1: 0} if olds else {},
        name="stack_rows",
    )(slots, *blocks, *olds)


def assemble(columns, others, rows):
    count = len(columns)
    _, height, width = columns[0].shape
    kind = columns[0].dtype

    def kernel(at_ref, *refs):
        main_ref, extra_ref = refs[-2:]
        for d in range(count):
            for k in range(2):
                part = refs[2 * d + k]
                for low_bit in range(2):
                    index = (at_ref[0] ^ d) * 4 + low_bit * 2 + (at_ref[1] ^ k)
                    start = pl.multiple_of(index * rows, 16)
                    main_ref[pl.ds(start, rows), :] = part[low_bit, :rows]
                    extra_ref[index] = part[low_bit, rows:]

    parts = [part for both in zip(columns, others) for part in both]
    at = jnp.stack([lax.axis_index("hi"), lax.axis_index("x")]).astype(jnp.int32)
    return pl.pallas_call(
        kernel,
        in_specs=[pl.BlockSpec(memory_space=pltpu.SMEM)]
        + [pl.BlockSpec(memory_space=pltpu.VMEM)] * len(parts),
        out_specs=[pl.BlockSpec(memory_space=pltpu.VMEM)] * 2,
        out_shape=[
            jax.ShapeDtypeStruct((count * 4 * rows, width), kind),
            jax.ShapeDtypeStruct((count * 4, height - rows, width), kind),
        ],
        name="assemble",
    )(at, *parts)


def send_x(parts):
    x = lax.axis_index("x")
    parts = parts.reshape((-1, 2, 2) + parts.shape[1:])
    kept = lax.dynamic_index_in_dim(parts, x, axis=2, keepdims=False)
    sent = lax.dynamic_index_in_dim(parts, 1 - x, axis=2, keepdims=False)
    return kept, swap(sent, "x")


def send_hi(parts):
    hi = lax.axis_index("hi")
    turns = range(1, lax.axis_size("hi"))
    return [pick(parts, hi)] + [swap(pick(parts, hi ^ d), "hi", d) for d in turns]


def send_lo(parts):
    lo = lax.axis_index("lo")
    return pick(parts, lo), swap(low(pick(parts, 1 - lo)), "lo")


def add_up(parts):
    return sum(wide_float(part) for part in parts)


def send_hidden(total):
    x = lax.axis_index("x")
    total = total.reshape((2, -1) + total.shape[1:])
    return pick(total, x), swap(pick(total, 1 - x), "x")


def join_hidden(mine, other):
    x = lax.axis_index("x")
    first = jnp.where(x == 0, mine, other)
    second = jnp.where(x == 0, other, mine)
    return wide_float(jnp.concatenate([first, second], axis=1))


def hidden_halves(shards):
    x = lax.axis_index("x")
    half = shards[0].shape[1] // 2

    def part(at):
        return jnp.concatenate(
            [lax.dynamic_slice_in_dim(shard, at * half, half, axis=1) for shard in shards], axis=1
        )

    return part(x), swap(part(1 - x), "x")


def join_rows(mine, other):
    both = pair(mine, other, lax.axis_index("x"))
    return both.reshape((-1,) + both.shape[2:])


def exchange_narrow(blocks):
    y, c = (lax.axis_index(name) for name in NARROW)
    shape = blocks.shape[2:]
    flat = blocks.reshape((4,) + shape)
    me = y * 2 + c
    got = [pick(flat, me)] + [swap(pick(flat, me ^ d), NARROW, d) for d in range(1, 4)]
    near, far = pair(got[0], got[1], c), pair(got[2], got[3], c)
    return pair(near, far, y)


def gather_tokens(block, *needed):
    return spread_core(block, after(swap(block, "y"), *needed))


def spread_core(block, by_y):
    y, c = (lax.axis_index(name) for name in NARROW)
    own = c * 2 + y
    return stack_rows(
        [block, by_y, swap(block, "c"), swap(by_y, "c")], [own, own ^ 1, own ^ 2, own ^ 3]
    )


def rotation(positions):
    half = HD // 2
    freqs = rope_base ** (-2.0 * jnp.arange(half, dtype=jnp.float32) / HD)
    angles = positions.astype(jnp.float32)[:, None] * freqs[None, :]
    cosine, sine = jnp.cos(angles), jnp.sin(angles)
    return jnp.concatenate([cosine, cosine], axis=1), jnp.concatenate([-sine, sine], axis=1)


def rms_back(grad_unit, unit, inverse):
    return inverse * (grad_unit - unit * jnp.mean(grad_unit * unit, axis=-1, keepdims=True))


def adam_update(grad, master, first, second, decay, count):
    mean_grad = grad / count
    first_new = beta_first * first + (1.0 - beta_first) * mean_grad
    second_new = beta_second * second + (1.0 - beta_second) * mean_grad * mean_grad
    update = first_new / first_fix / (jnp.sqrt(second_new / second_fix) + adam_eps)
    if decay:
        update = update + decay_rate * master
    return (grad, update)


def project(layer_input, weight, bias, cosine, sine, kv_cosine, kv_sine, heads):
    tokens = layer_input.shape[0]
    width = weight.shape[1]
    block = 256
    scale = HD ** (-0.5)

    def kernel(x_ref, w_ref, b_ref, c_ref, s_ref, kc_ref, ks_ref, a_ref, q_ref, kv_ref):
        x = wide_float(x_ref[...])
        inverse = lax.rsqrt(jnp.mean(x * x, axis=1, keepdims=True) + norm_eps)
        normed = low(x * inverse)
        a_ref[...] = normed
        linear = matmul(normed, w_ref[...]) + b_ref[...]
        for h in range(heads + 1):
            part = linear[:, h * HD : (h + 1) * HD]
            turned = pltpu.roll(part, HD // 2, axis=1)
            if h < heads:
                out = (part * c_ref[...] + turned * s_ref[...]) * scale
                q_ref[:, h * HD : (h + 1) * HD] = low(out)
            else:
                kv_ref[...] = low(part * kc_ref[...] + turned * ks_ref[...])

    def by_tokens(columns):
        return pl.BlockSpec((block, columns), lambda i: (i, 0))

    def whole(a):
        return pl.BlockSpec(a.shape, lambda i: (0, 0))

    return pl.pallas_call(
        kernel,
        grid=(tokens // block,),
        in_specs=[by_tokens(D), whole(weight), whole(bias)] + [by_tokens(HD)] * 4,
        out_specs=[by_tokens(D), by_tokens(heads * HD), by_tokens(HD)],
        out_shape=[
            jax.ShapeDtypeStruct((tokens, D), jnp.bfloat16),
            jax.ShapeDtypeStruct((tokens, heads * HD), jnp.bfloat16),
            jax.ShapeDtypeStruct((tokens, HD), jnp.bfloat16),
        ],
        name="project",
    )(layer_input, weight, bias, cosine, sine, kv_cosine, kv_sine)


def feed_forward(tokens_in, grads_in, w_gateup, half, at, count, into=None):
    tokens = tokens_in.shape[0]
    block = 512
    olds = [] if into is None else list(into)
    skip = at // block

    def kernel(b_ref, g_ref, wgu_ref, *refs):
        hid_ref, dgu_ref = refs[-2:]
        both = matmul(b_ref[...], wgu_ref[...])
        gate, upward = both[:, :half], both[:, half:]
        grad = wide_float(g_ref[...])
        logistic = jax.nn.sigmoid(gate)
        active = gate * logistic
        hid_ref[...] = low(active * upward)
        slope = logistic + active * (1.0 - logistic)
        dgu_ref[:, :half] = low(grad * upward * slope)
        dgu_ref[:, half:] = low(grad * active)

    def by_tokens(columns):
        return pl.BlockSpec((block, columns), lambda i: (i + skip, 0))

    return pl.pallas_call(
        kernel,
        grid=(count // block,),
        in_specs=[
            by_tokens(D),
            by_tokens(half),
            pl.BlockSpec(w_gateup.shape, lambda i: (0, 0), pipeline_mode=pl.Buffered(1)),
        ]
        + [pl.BlockSpec(memory_space=pl.ANY)] * len(olds),
        out_specs=[by_tokens(half), by_tokens(2 * half)],
        out_shape=[
            jax.ShapeDtypeStruct((tokens, half), jnp.bfloat16),
            jax.ShapeDtypeStruct((tokens, 2 * half), jnp.bfloat16),
        ],
        input_output_aliases={3: 0, 4: 1} if olds else {},
        name="feed_forward",
    )(tokens_in, grads_in, w_gateup, *olds)


def over_blocks(first_begin, last_begin, base, run, carry):
    first = first_begin // BLOCK_K
    end = (base + BLOCK_Q - 1) // BLOCK_K + 1
    clear = jnp.minimum((last_begin + BLOCK_K - 1) // BLOCK_K, end)
    clear_end = jnp.maximum((base + 1) // BLOCK_K, clear)
    before = clear - first

    def edge(t, carry):
        return run(jnp.where(t < before, first + t, clear_end + t - before), carry, True)

    carry = lax.fori_loop(clear, clear_end, lambda j, carry: run(j, carry, False), carry)
    return lax.fori_loop(0, before + end - clear_end, edge, carry)


def stacked_heads(ref, heads):
    return jnp.concatenate([ref[:, h * HD : (h + 1) * HD] for h in range(heads)], axis=0)


def attention_forward(queries, keys, values, begins, starts, place):
    tokens, columns = queries.shape
    heads = columns // HD
    length = keys.shape[0]
    rows = heads * BLOCK_Q

    def kernel(starts_ref, place_ref, q_ref, k_ref, v_ref, begin_ref, o_ref, lse_ref):
        step = pl.program_id(0)
        base = place_ref[0] * tokens + step * BLOCK_Q
        q = stacked_heads(q_ref, heads)
        row = base + lax.broadcasted_iota(jnp.int32, (BLOCK_Q, 1), 0)
        row = jnp.concatenate([row] * heads, axis=0)
        begin = jnp.concatenate([begin_ref[...]] * heads, axis=0)

        def run(j, carry, masked):
            top, total, acc = carry
            at = pl.multiple_of(j * BLOCK_K, BLOCK_K)
            k = k_ref[pl.ds(at, BLOCK_K), :]
            v = v_ref[pl.ds(at, BLOCK_K), :]
            s = matmul_nt(q, k)
            if masked:
                col = at + lax.broadcasted_iota(jnp.int32, (1, BLOCK_K), 1)
                s = jnp.where((col <= row) & (col >= begin), s, masked_score)
            new_top = jnp.maximum(top, jnp.max(s, axis=1, keepdims=True))
            p = jnp.exp(s - new_top)
            scale = jnp.exp(top - new_top)
            total = scale * total + jnp.sum(p, axis=1, keepdims=True)
            acc = scale * acc + matmul(low(p), v)
            return new_top, total, acc

        top, total, acc = over_blocks(
            starts_ref[2 * step],
            starts_ref[2 * step + 1],
            base,
            run,
            (
                jnp.full((rows, 1), masked_score, jnp.float32),
                jnp.zeros((rows, 1), jnp.float32),
                jnp.zeros((rows, HD), jnp.float32),
            ),
        )
        out = acc / total
        for h in range(heads):
            o_ref[:, h * HD : (h + 1) * HD] = out[h * BLOCK_Q : (h + 1) * BLOCK_Q]
        lse_ref[...] = (top + jnp.log(total)).reshape(heads, BLOCK_Q, 1)

    block = pl.BlockSpec((BLOCK_Q, columns), lambda i, *_: (i, 0))
    whole = pl.BlockSpec((length, HD), lambda i, *_: (0, 0))
    return pl.pallas_call(
        kernel,
        grid_spec=pltpu.PrefetchScalarGridSpec(
            num_scalar_prefetch=2,
            grid=(tokens // BLOCK_Q,),
            in_specs=[block, whole, whole, pl.BlockSpec((BLOCK_Q, 1), lambda i, *_: (i, 0))],
            out_specs=[block, pl.BlockSpec((heads, BLOCK_Q, 1), lambda i, *_: (0, i, 0))],
        ),
        out_shape=[
            jax.ShapeDtypeStruct((tokens, columns), jnp.float32),
            jax.ShapeDtypeStruct((heads, tokens, 1), jnp.float32),
        ],
        compiler_params=pltpu.CompilerParams(dimension_semantics=("arbitrary",)),
        name="attention_forward",
    )(starts, place, queries, keys, values, begins)


def attention_backward(
    queries, keys, values, begins, starts, place, grads, lse, outputs, cosine, sine
):
    tokens, columns = queries.shape
    heads = columns // HD
    length = keys.shape[0]
    rows = heads * BLOCK_Q

    def kernel(
        starts_ref, place_ref, q_ref, k_ref, v_ref, begin_ref, g_ref, lse_ref, o_ref,
        c_ref, s_ref, dq_ref, dk_ref, dv_ref,
    ):
        step = pl.program_id(0)

        @pl.when(step == 0)
        def _():
            dk_ref[...] = jnp.zeros_like(dk_ref)
            dv_ref[...] = jnp.zeros_like(dv_ref)

        base = place_ref[0] * tokens + step * BLOCK_Q
        q = stacked_heads(q_ref, heads)
        g = stacked_heads(g_ref, heads)
        delta = jnp.sum(wide_float(g) * stacked_heads(o_ref, heads), axis=1, keepdims=True)
        lse = lse_ref[...].reshape(rows, 1)
        row = base + lax.broadcasted_iota(jnp.int32, (BLOCK_Q, 1), 0)
        row = jnp.concatenate([row] * heads, axis=0)
        begin = jnp.concatenate([begin_ref[...]] * heads, axis=0)

        def less(a, column):
            high = low(-column)
            middle = low(-column - wide_float(high))
            last = low(-column - wide_float(high) - wide_float(middle))
            lane = lax.broadcasted_iota(jnp.int32, (rows, HD), 1)
            parts = jnp.where(lane == 1, middle, jnp.where(lane == 2, last, jnp.zeros_like(last)))
            return jnp.concatenate([a, jnp.where(lane == 0, high, parts)], axis=1)

        q_less = less(q, lse)
        g_less = less(g, delta)
        ones = jnp.ones((BLOCK_K, HD), jnp.bfloat16)

        def run(j, dq, masked):
            at = pl.multiple_of(j * BLOCK_K, BLOCK_K)
            k = k_ref[pl.ds(at, BLOCK_K), :]
            v = v_ref[pl.ds(at, BLOCK_K), :]
            s = matmul_nt(q_less, jnp.concatenate([k, ones], axis=1))
            if masked:
                col = at + lax.broadcasted_iota(jnp.int32, (1, BLOCK_K), 1)
                s = jnp.where((col <= row) & (col >= begin), s, masked_score)
            p = jnp.exp(s)
            ds = low(p * matmul_nt(g_less, jnp.concatenate([v, ones], axis=1)))
            dk_ref[pl.ds(at, BLOCK_K), :] += matmul_tn(ds, q)
            dv_ref[pl.ds(at, BLOCK_K), :] += matmul_tn(low(p), g)
            return dq + matmul(ds, k)

        dq = over_blocks(
            starts_ref[2 * step],
            starts_ref[2 * step + 1],
            base,
            run,
            jnp.zeros((rows, HD), jnp.float32),
        )
        for h in range(heads):
            part = dq[h * BLOCK_Q : (h + 1) * BLOCK_Q]
            turned = pltpu.roll(part, HD // 2, axis=1)
            part = (part * c_ref[...] - turned * s_ref[...]) * HD ** (-0.5)
            dq_ref[:, h * HD : (h + 1) * HD] = low(part)

    block = pl.BlockSpec((BLOCK_Q, columns), lambda i, *_: (i, 0))
    whole = pl.BlockSpec((length, HD), lambda i, *_: (0, 0))
    return pl.pallas_call(
        kernel,
        grid_spec=pltpu.PrefetchScalarGridSpec(
            num_scalar_prefetch=2,
            grid=(tokens // BLOCK_Q,),
            in_specs=[
                block,
                whole,
                whole,
                pl.BlockSpec((BLOCK_Q, 1), lambda i, *_: (i, 0)),
                block,
                pl.BlockSpec((heads, BLOCK_Q, 1), lambda i, *_: (0, i, 0)),
                block,
                pl.BlockSpec((BLOCK_Q, HD), lambda i, *_: (i, 0)),
                pl.BlockSpec((BLOCK_Q, HD), lambda i, *_: (i, 0)),
            ],
            out_specs=[block, whole, whole],
        ),
        out_shape=[
            jax.ShapeDtypeStruct((tokens, columns), jnp.bfloat16),
            jax.ShapeDtypeStruct((length, HD), jnp.float32),
            jax.ShapeDtypeStruct((length, HD), jnp.float32),
        ],
        compiler_params=pltpu.CompilerParams(dimension_semantics=("arbitrary",)),
        cost_estimate=pl.CostEstimate(
            flops=20 * tokens * tokens * columns, transcendentals=0, bytes_accessed=0
        ),
        name="attention_backward",
    )(starts, place, queries, keys, values, begins, grads, lse, outputs, cosine, sine)


def local(
    layer_input,
    grad_out,
    segment_ids,
    positions,
    norm_gains,
    norm_gains_first,
    norm_gains_second,
    query_weight,
    query_weight_first,
    query_weight_second,
    query_bias,
    query_bias_first,
    query_bias_second,
    keyvalue_weight,
    keyvalue_weight_first,
    keyvalue_weight_second,
    keyvalue_bias,
    keyvalue_bias_first,
    keyvalue_bias_second,
    output_weight,
    output_weight_first,
    output_weight_second,
    gateup_weight,
    gateup_weight_first,
    gateup_weight_second,
    down_weight,
    down_weight_first,
    down_weight_second,
):
    hi, lo, x, y, c = (lax.axis_index(name) for name in WIDE + NARROW)
    wide = lax.axis_size("hi") * 4
    tokens = layer_input.shape[0]
    quarter = tokens // 4
    heads = query_bias.shape[0]
    token_count = float(tokens * wide)
    rows = D // wide
    narrow_rows = rows // 4
    bias_part = query_bias.shape[1]
    kv_part = keyvalue_bias.shape[0]
    column_block = c * KV + y
    hidden = gateup_weight.shape[2]
    half = -(-hidden // (2 * LANES)) * LANES
    padding = 2 * half - hidden
    own = c * 2 + y

    kv_columns = low(keyvalue_weight).reshape(narrow_rows, 2, KV, HD)
    kv_columns = jnp.transpose(kv_columns, (2, 1, 0, 3))
    small = jnp.concatenate([low(norm_gains).reshape(-1), low(keyvalue_bias)])
    small = jnp.pad(small, (0, HD - small.shape[0])).reshape(1, 1, 1, HD)
    small = jnp.pad(small, ((0, 0), (0, 0), (0, 15), (0, 0)))
    blocks = jnp.concatenate([kv_columns, jnp.broadcast_to(small, (2, 2, 16, HD))], axis=2)
    blocks = exchange_narrow(blocks).reshape(4, narrow_rows + 16, HD)
    kv_mine = blocks[:, :narrow_rows].reshape(rows, HD)
    small_row = blocks[:, narrow_rows].reshape(1, 4 * HD)
    row_gains = wide_float(blocks[:, narrow_rows, : 2 * narrow_rows])
    row_gains = jnp.transpose(row_gains.reshape(4, 2, narrow_rows), (1, 0, 2)).reshape(2, rows, 1)
    bias_row = jnp.pad(low(query_bias).reshape(1, -1), ((0, 0), (0, 4 * HD - heads * bias_part)))
    extra = jnp.pad(jnp.concatenate([small_row, bias_row]), ((0, 14), (0, 0)))
    my_qkv = wide_float(jnp.concatenate([low(query_weight), kv_mine], axis=1))
    packed = jnp.concatenate([low(my_qkv * row_gains[0]), extra], axis=0)
    side = jnp.pad(low(output_weight).T, ((0, 16), (0, 0)))
    packed = jnp.concatenate([packed, side], axis=1)
    columns, out_columns = wide_columns(packed, 4 * HD)
    others = [swap(column, "x") for column in columns]
    out_others = [swap(column, "x") for column in after(out_columns, others)]
    w_qkv, small_all = assemble(columns, others, rows)
    small_all = wide_float(small_all)
    b_query = small_all[:, 1, : heads * bias_part].reshape(wide, heads, bias_part)
    small_all = small_all[:, 0].reshape(wide, 4, HD)
    gains = small_all[:, :, : 2 * narrow_rows].reshape(wide, 4, 2, narrow_rows)
    gains = jnp.transpose(gains, (2, 0, 1, 3)).reshape(2, D)
    b_kv = small_all[:, :, 2 * narrow_rows : 2 * narrow_rows + kv_part].reshape(2 * KV, HD)
    b_query = jnp.transpose(b_query, (1, 0, 2)).reshape(heads * HD)
    b_qkv = jnp.concatenate([b_query, pick(b_kv, column_block)])
    gain_two = gains[1]

    def padded(shard):
        return jnp.pad(low(shard), ((0, 0), (0, padding)))

    down_shard = join_rows(*hidden_halves([padded(down_weight.T)]))
    w_down = lax.all_gather(after(down_shard, columns), ("hi", "lo"), axis=0, tiled=True)
    gateup_halves = hidden_halves(
        after([padded(gateup_weight[:, 0]), padded(gateup_weight[:, 1])], others)
    )

    cosine, sine = rotation(positions)
    kv_cosine = jnp.where(c == 0, cosine, 1.0)
    kv_sine = jnp.where(c == 0, sine, 0.0)
    normed_one, queries, kv_own = project(
        layer_input, w_qkv, b_qkv[None], cosine, sine, kv_cosine, kv_sine, heads
    )
    gateup_shard = join_rows(*after(gateup_halves, kv_own))
    w_gateup = lax.all_gather(gateup_shard, ("hi", "lo"), axis=0, tiled=True)
    both = after(pair(kv_own, swap(kv_own, "lo"), lo), gateup_shard)
    by_place = pair(both, swap(both, "x"), x)
    kv_row = jnp.transpose(by_place, (1, 0, 2, 3)).reshape(4 * tokens, HD)
    kv_other = swap(kv_row, "c")
    keys = jnp.where(c == 0, kv_row, kv_other)
    values = jnp.where(c == 0, kv_other, kv_row)
    begins = segment_ids - hi * (4 * tokens)
    starts = jnp.stack([begins[::BLOCK_Q], begins[BLOCK_Q - 1 :: BLOCK_Q]], axis=1).reshape(-1)
    begins = begins[:, None]
    place = (lo * 2 + x).reshape(1).astype(jnp.int32)
    grad_blocks = grad_out.reshape(4, quarter, D)
    grad_near = [pick(grad_blocks, own ^ d) for d in range(4)]
    grad_far = [swap(part, "x") for part in after(grad_near[:2], kv_row)]
    attention, log_total = attention_forward(queries, keys, values, begins, starts, place)
    w_output, _ = assemble(*after((out_columns, out_others), attention), rows)
    grad_far = after(grad_far, attention)
    ff_grad = stack_rows(grad_near + grad_far + [swap(part, "c") for part in grad_far], range(8))
    attention_low = low(attention)

    def halves(block):
        split = block.reshape(2, -1, block.shape[-1])
        return pick(split, c), pick(split, 1 - c)

    def send_core(kept, sent):
        return kept + wide_float(swap(low(sent), "c"))

    attention_kept, attention_sent = halves(attention_low)
    sent = matmul_nt(attention_sent, w_output)
    out_total = send_core(matmul_nt(attention_kept, w_output), sent)
    out_split = out_total.reshape(2, quarter, D)
    out_other = swap(low(pick(out_split, 1 - y)), "y")
    grad_hidden = low(matmul(after(ff_grad, out_total), w_down))
    out_other = after(out_other, grad_hidden)
    residual = wide_float(pick(layer_input.reshape(4, quarter, D), own))
    residual = residual + pick(out_split, y) + wide_float(out_other)
    inverse_two = lax.rsqrt(jnp.mean(residual * residual, axis=-1, keepdims=True) + norm_eps)
    unit_two = residual * inverse_two
    normed_two = low(unit_two * gain_two)

    by_y = swap(normed_two, "y")
    by_x = swap(normed_two, "x")
    by_both = [swap(by_y[:, : D // 2], "x"), swap(by_x[:, D // 2 :], "y")]
    count = 4 * quarter
    ff_input = stack_rows(
        [normed_two, by_y, swap(normed_two, "c"), swap(by_y, "c")], range(4), count=8
    )
    firsts = feed_forward(ff_input, grad_hidden, w_gateup, half, 0, count)
    by_both = after(by_both, firsts[0])
    by_both = jnp.concatenate(by_both, axis=1)
    ff_input = stack_rows(
        [by_x, by_both, swap(by_x, "c"), swap(by_both, "c")], range(4, 8), into=ff_input, count=8
    )
    hidden_all, both_all = feed_forward(
        ff_input, grad_hidden, w_gateup, half, count, count, into=firsts
    )

    half_d = D // 2

    def join_core(sums):
        return wide_float(sums[: 2 * quarter]) + wide_float(swap(sums[2 * quarter :], "c"))

    def first_sends(far_sums, near_sums):
        to_x = low(far_sums[:, :half_d])
        to_y = low(jnp.concatenate([near_sums[quarter:, half_d:], far_sums[quarter:, half_d:]]))
        return to_x, to_y

    def second_sends(far_sums, near_sums, from_x, from_y):
        left = near_sums[:, :half_d] + wide_float(from_x)
        right = near_sums[:quarter, half_d:] + wide_float(from_y[:quarter])
        to_x = low(far_sums[:quarter, half_d:] + wide_float(from_y[quarter:]))
        return (left[:quarter], right), (low(left[quarter:]), to_x)

    def finish_sums(kept, from_y, from_x):
        return jnp.concatenate([kept[0] + wide_float(from_y), kept[1] + wide_float(from_x)], axis=1)

    grad_gateup = low(matmul_tn(ff_input, both_all))
    both_all = after(both_all, grad_gateup)
    feed_far = low(matmul_nt(both_all[count:], w_gateup))
    feed_near = low(matmul_nt(after(both_all, feed_far)[:count], w_gateup))

    def over_rows(grad):
        return lax.psum_scatter(grad, ("hi", "lo"), scatter_dimension=0, tiled=True)

    far_sums, near_sums = join_core(feed_far), join_core(feed_near)
    to_x, to_y = first_sends(far_sums, near_sums)
    from_x, from_y = swap(to_x, "x"), swap(to_y, "y")
    hidden_late = after(hidden_all, to_x, to_y)
    mlp_far = low(matmul_nt(hidden_late[count:], w_down))
    mlp_near = low(matmul_nt(after(hidden_late, mlp_far)[:count], w_down))
    from_x, from_y = after((from_x, from_y), mlp_near)
    kept, (to_y, to_x) = second_sends(far_sums, near_sums, from_x, from_y)
    from_x, from_y = swap(to_x, "x"), swap(to_y, "y")
    grad_normed_two = finish_sums(kept, from_y, from_x)
    grad_residual = wide_float(grad_near[0]) + rms_back(
        grad_normed_two * gain_two, unit_two, inverse_two
    )
    residual_own = low(grad_residual)
    ff_late, hidden_all = after((ff_grad, hidden_all), swap(residual_own, "c"))
    grad_down = low(matmul_tn(ff_late, hidden_all))
    rows_gateup, rows_down = over_rows(grad_gateup), over_rows(grad_down)
    mlp_far, mlp_near = after((mlp_far, mlp_near), residual_own)
    mlp_far, mlp_near = low(join_core(mlp_far)), join_core(mlp_near)
    residual_low = gather_tokens(residual_own, grad_down, mlp_near)

    grad_attention = low(matmul(residual_low, w_output))
    x_output = send_x(
        low(matmul_tn(residual_low, attention_low)).reshape(wide, rows, heads * HD)
    )
    from_far = swap(after(mlp_far, residual_low), "x")
    grad_queries, grad_keys, grad_values = attention_backward(
        queries, keys, values, begins, starts, place, grad_attention, log_total, attention,
        cosine, sine,
    )
    kv_sent = low(jnp.where(c == 0, grad_values, grad_keys))
    kv_sent, from_far, x_output = after((kv_sent, from_far, x_output), grad_queries, rows_gateup)
    kv_grad = jnp.where(c == 0, grad_keys, grad_values) + wide_float(swap(kv_sent, "c"))
    kv_grad = kv_grad.reshape(2, 2, tokens, HD)
    kv_kept, kv_sent = (
        lax.dynamic_index_in_dim(kv_grad, at, axis=1, keepdims=False) for at in (x, 1 - x)
    )
    kv_sent = low(kv_sent)
    from_far, x_output, mlp_near, normed_late = after(
        (from_far, x_output, mlp_near, normed_one), kv_sent
    )
    rows_output = over_rows(low(add_up(x_output)).reshape(-1, heads * HD))
    mlp_sums = mlp_near + wide_float(from_far)
    from_y = swap(low(mlp_sums[quarter:]), "y")
    kv_grad = kv_kept + wide_float(swap(kv_sent, "x"))
    parts_gateup = send_hidden(after(rows_gateup, kv_grad))
    from_y = after(from_y, kv_grad)
    layer_own = low(residual + mlp_sums[:quarter] + wide_float(from_y))
    kv_grad = pick(kv_grad, lo) + wide_float(swap(low(pick(kv_grad, 1 - lo)), "lo"))
    turned = jnp.concatenate([kv_grad[:, HD // 2 :], kv_grad[:, : HD // 2]], axis=1)
    grad_kv = low(kv_grad * kv_cosine - turned * kv_sine)
    grad_kv = after(grad_kv, parts_gateup)

    w_query, w_kv = w_qkv[:, : heads * HD], w_qkv[:, heads * HD :]

    def input_part(kv_part_grad, query_part_grad):
        return matmul_nt(query_part_grad, w_query) + matmul_nt(kv_part_grad, w_kv)

    query_kept, query_sent = halves(grad_queries)
    kv_kept, kv_sent = halves(grad_kv)
    part_sent = low(input_part(kv_sent, query_sent))
    part_kept = input_part(kv_kept, query_kept)
    part_total = send_core(part_kept, part_sent)
    part_other = swap(low(part_total), "y")
    layer_by_y = swap(after(layer_own, part_other), "y")
    grad_normed_one = part_total + wide_float(part_other)
    core_input = pick(after(layer_input, part_total).reshape(2, 2 * quarter, D), c)
    core_input = wide_float(core_input)
    core_inverse = lax.rsqrt(jnp.mean(core_input * core_input, axis=-1, keepdims=True) + norm_eps)
    core_grad = wide_float(pick(residual_low.reshape(2, 2 * quarter, D), c)) + rms_back(
        grad_normed_one, core_input * core_inverse, core_inverse
    )
    core_grad = low(core_grad)
    input_grad = stack_rows([core_grad, swap(core_grad, "c")], [c, 1 - c])
    layer_output = spread_core(layer_own, after(layer_by_y, core_grad))

    grad_query_weight = low(matmul_tn(normed_late, grad_queries)).reshape(wide, rows, heads * HD)
    grad_kv_weight = low(matmul_tn(normed_one, grad_kv)).reshape(wide, rows, HD)
    bias_query = jnp.sum(wide_float(grad_queries), axis=0).reshape(heads, wide, bias_part)
    bias_query = jnp.transpose(bias_query, (1, 0, 2)).reshape(wide, heads * bias_part)
    kv_sums = jnp.sum(wide_float(grad_kv), axis=0, keepdims=True)
    bias_kv = jnp.where(jnp.arange(2 * KV)[:, None] == column_block, kv_sums, 0.0)
    bias_kv = bias_kv.reshape(wide, 4 * kv_part)
    bias_all = jnp.concatenate([bias_query, bias_kv], axis=1)
    bias_all = jnp.pad(bias_all, ((0, 0), (0, HD - bias_all.shape[1])))
    extra = jnp.pad(low(bias_all)[:, None], ((0, 0), (0, 15), (0, 3 * HD)))
    grad_qkv = jnp.concatenate([grad_query_weight, grad_kv_weight], axis=2)
    x_qkv = send_x(jnp.concatenate([grad_qkv, extra], axis=1))
    parts_gateup = after(parts_gateup, part_total)
    summed_gate = join_hidden(*(part[:, :half] for part in parts_gateup))
    summed_up = join_hidden(*(part[:, half:] for part in parts_gateup))
    summed_gateup = jnp.stack([summed_gate[:, :hidden], summed_up[:, :hidden]], axis=1)
    summed_gateup = with_layout_constraint(summed_gateup, Layout((0, 1, 2)))
    gateup_update = adam_update(
        summed_gateup, gateup_weight, gateup_weight_first, gateup_weight_second, True, token_count
    )
    sums_qkv = low(add_up(after(x_qkv, gateup_update[1], rows_output, rows_down)))
    summed = wide_float(over_rows(sums_qkv.reshape(-1, 4 * HD)))
    summed_query = summed[:rows, : heads * HD]
    summed_kv = summed[:rows, heads * HD :]
    summed_query_bias = summed[rows, : heads * bias_part].reshape(heads, bias_part)
    kv_bias = summed[rows, heads * bias_part : heads * bias_part + 4 * kv_part]
    parts_down = send_hidden(after(rows_down, sums_qkv))
    summed_output = wide_float(after(rows_output, sums_qkv))

    grad_gain_one = jnp.sum(
        summed_query * my_qkv[:, : heads * HD], axis=1
    ) + jnp.sum(summed_kv * my_qkv[:, heads * HD :], axis=1)
    summed_query = summed_query * row_gains[0]
    summed_kv = summed_kv * row_gains[0]
    grad_gain_two = (
        jnp.sum(summed_gateup * wide_float(low(gateup_weight)), axis=(1, 2)) / row_gains[1, :, 0]
    )
    gain_parts = jnp.stack([grad_gain_one, grad_gain_two]).reshape(2, 4, narrow_rows)
    gain_parts = jnp.transpose(gain_parts, (1, 0, 2)).reshape(4, 2 * narrow_rows)
    last = jnp.concatenate([gain_parts, kv_bias.reshape(4, kv_part)], axis=1)
    last = jnp.pad(last, ((0, 0), (0, HD - last.shape[1])))[:, None]
    last = jnp.pad(last, ((0, 0), (0, 7), (0, 0)))
    last = jnp.concatenate([summed_kv.reshape(4, narrow_rows, HD), last], axis=1)
    last = exchange_narrow(last.reshape((2, 2) + last.shape[1:]))
    summed_keyvalue = jnp.transpose(last[:, :, :narrow_rows], (2, 1, 0, 3))
    summed_keyvalue = summed_keyvalue.reshape(narrow_rows, 2 * KV * HD)
    small_sums = jnp.sum(last[:, :, narrow_rows], axis=(0, 1))
    summed_gains = small_sums[: 2 * narrow_rows].reshape(2, narrow_rows)
    summed_keyvalue_bias = small_sums[2 * narrow_rows : 2 * narrow_rows + kv_part]
    summed_output = summed_output.T

    gains_update = adam_update(
        summed_gains, norm_gains, norm_gains_first, norm_gains_second, False, token_count
    )
    query_update = adam_update(
        summed_query, query_weight, query_weight_first, query_weight_second, True, token_count
    )
    qbias_update = adam_update(
        summed_query_bias, query_bias, query_bias_first, query_bias_second, False, token_count
    )
    keyvalue_update = adam_update(
        summed_keyvalue,
        keyvalue_weight,
        keyvalue_weight_first,
        keyvalue_weight_second,
        True,
        token_count,
    )
    kvbias_update = adam_update(
        summed_keyvalue_bias,
        keyvalue_bias,
        keyvalue_bias_first,
        keyvalue_bias_second,
        False,
        token_count,
    )
    output_update = adam_update(
        summed_output, output_weight, output_weight_first, output_weight_second, True, token_count
    )
    summed_down = join_hidden(*after(parts_down, core_grad))[:, :hidden].T
    down_update = adam_update(
        summed_down, down_weight, down_weight_first, down_weight_second, True, token_count
    )
    return (
        layer_output,
        input_grad,
        *gains_update,
        *query_update,
        *qbias_update,
        *keyvalue_update,
        *kvbias_update,
        *output_update,
        *gateup_update,
        *down_update,
    )


def solution(mesh):
    devices = mesh.devices.reshape(-1, 2, 2, 2, 2)
    split = Mesh(devices, WIDE + NARROW)
    token_matrix = P(WIDE, None)
    token_vector = P(WIDE)
    gains = P(None, WIDE + NARROW)
    query = P(WIDE, NARROW)
    by_narrow = P(NARROW, WIDE)
    keyvalue = P(WIDE + NARROW, None)
    keyvalue_bias = P(WIDE + NARROW)
    gateup = P(WIDE, None, NARROW)
    parameters = (gains, query, by_narrow, keyvalue, keyvalue_bias, by_narrow, gateup, by_narrow)
    in_specs = (token_matrix, token_matrix, token_vector, token_vector)
    out_specs = (token_matrix, token_matrix)
    for spec in parameters:
        in_specs += (spec,) * 3
        out_specs += (spec,) * 2
    return jax.shard_map(local, mesh=split, in_specs=in_specs, out_specs=out_specs, check_vma=False)
```

```python
import jax
import jax.numpy as jnp
from jax import lax
from jax.experimental import pallas as pl
from jax.experimental.layout import Layout, with_layout_constraint
from jax.experimental.pallas import tpu as pltpu
from jax.sharding import Mesh
from jax.sharding import PartitionSpec as P

D = 1536
H = 12
KV = 2
HD = 128
LENGTH = 4096
LANES = 128

norm_eps = 1e-06
rope_base = 1000000.0
beta_first = 0.9
beta_second = 0.95
adam_eps = 1e-08
decay_rate = 0.1
first_fix = 1.0 - 0.9**10
second_fix = 1.0 - 0.95**10
masked_score = -1e30

WIDE = ("hi", "lo", "x")
NARROW = ("y", "c")
BLOCK_Q = 512
BLOCK_K = 512
FORWARD_K = 1024


def low(a):
    return a.astype(jnp.bfloat16)


def wide_float(a):
    return a.astype(jnp.float32)


def matmul(left, right):
    return jnp.dot(left, right, preferred_element_type=jnp.float32)


def matmul_nt(left, right):
    return lax.dot_general(left, right, (((1,), (1,)), ((), ())), preferred_element_type=jnp.float32)


def matmul_tn(left, right):
    return lax.dot_general(left, right, (((0,), (0,)), ((), ())), preferred_element_type=jnp.float32)


def swap(block, axis, distance=1):
    size = 1
    for name in axis if isinstance(axis, tuple) else (axis,):
        size *= lax.axis_size(name)
    return lax.ppermute(block, axis, [(i, i ^ distance) for i in range(size)])


def pick(stacked, index):
    return lax.dynamic_index_in_dim(stacked, index, axis=0, keepdims=False)


def pair(mine, other, index):
    return jnp.where(index == 0, jnp.stack([mine, other]), jnp.stack([other, mine]))


def after(value, *needed):
    return lax.optimization_barrier((value, needed))[0]


def wide_columns(block, cut):
    lo = lax.axis_index("lo")
    count = lax.axis_size("hi")
    mine = [block] + [swap(block, "hi", d) for d in range(1, count)]
    other = [swap(part, "lo") for part in mine]
    left = [pair(m[:, :cut], o[:, :cut], lo) for m, o in zip(mine, other)]
    right = [pair(m[:, cut:], o[:, cut:], lo) for m, o in zip(mine, other)]
    return left, right


def stack_rows(blocks, slots, into=None, count=None):
    height, width = blocks[0].shape
    count = len(blocks) if count is None else count
    olds = [] if into is None else [into]

    def kernel(slot_ref, *refs):
        out_ref, sem = refs[-2:]
        copies = []
        for i, block_ref in enumerate(refs[: len(blocks)]):
            start = pl.multiple_of(slot_ref[i] * height, 16)
            copies.append(
                pltpu.make_async_copy(block_ref, out_ref.at[pl.ds(start, height), :], sem.at[i])
            )
        for copy in copies:
            copy.start()
        for copy in copies:
            copy.wait()

    anywhere = pl.BlockSpec(memory_space=pl.ANY)
    slots = jnp.stack([jnp.asarray(slot, jnp.int32) for slot in slots])
    return pl.pallas_call(
        kernel,
        in_specs=[pl.BlockSpec(memory_space=pltpu.SMEM)]
        + [pl.BlockSpec(memory_space=pltpu.VMEM)] * len(blocks)
        + [anywhere] * len(olds),
        out_specs=anywhere,
        out_shape=jax.ShapeDtypeStruct((count * height, width), blocks[0].dtype),
        scratch_shapes=[pltpu.SemaphoreType.DMA((len(blocks),))],
        input_output_aliases={len(blocks) + 1: 0} if olds else {},
        name="stack_rows",
    )(slots, *blocks, *olds)


def assemble(columns, others, rows):
    count = len(columns)
    _, height, width = columns[0].shape
    kind = columns[0].dtype

    def kernel(at_ref, *refs):
        main_ref, extra_ref = refs[-2:]
        for d in range(count):
            for k in range(2):
                part = refs[2 * d + k]
                for low_bit in range(2):
                    index = (at_ref[0] ^ d) * 4 + low_bit * 2 + (at_ref[1] ^ k)
                    start = pl.multiple_of(index * rows, 16)
                    main_ref[pl.ds(start, rows), :] = part[low_bit, :rows]
                    extra_ref[index] = part[low_bit, rows:]

    parts = [part for both in zip(columns, others) for part in both]
    at = jnp.stack([lax.axis_index("hi"), lax.axis_index("x")]).astype(jnp.int32)
    return pl.pallas_call(
        kernel,
        in_specs=[pl.BlockSpec(memory_space=pltpu.SMEM)]
        + [pl.BlockSpec(memory_space=pltpu.VMEM)] * len(parts),
        out_specs=[pl.BlockSpec(memory_space=pltpu.VMEM)] * 2,
        out_shape=[
            jax.ShapeDtypeStruct((count * 4 * rows, width), kind),
            jax.ShapeDtypeStruct((count * 4, height - rows, width), kind),
        ],
        name="assemble",
    )(at, *parts)


def send_x(parts):
    x = lax.axis_index("x")
    parts = parts.reshape((-1, 2, 2) + parts.shape[1:])
    kept = lax.dynamic_index_in_dim(parts, x, axis=2, keepdims=False)
    sent = lax.dynamic_index_in_dim(parts, 1 - x, axis=2, keepdims=False)
    return kept, swap(sent, "x")


def send_hi(parts):
    hi = lax.axis_index("hi")
    turns = range(1, lax.axis_size("hi"))
    return [pick(parts, hi)] + [swap(pick(parts, hi ^ d), "hi", d) for d in turns]


def send_lo(parts):
    lo = lax.axis_index("lo")
    return pick(parts, lo), swap(low(pick(parts, 1 - lo)), "lo")


def add_up(parts):
    return sum(wide_float(part) for part in parts)


def send_hidden(total):
    x = lax.axis_index("x")
    total = total.reshape((2, -1) + total.shape[1:])
    return pick(total, x), swap(pick(total, 1 - x), "x")


def join_hidden(mine, other):
    x = lax.axis_index("x")
    first = jnp.where(x == 0, mine, other)
    second = jnp.where(x == 0, other, mine)
    return wide_float(jnp.concatenate([first, second], axis=1))


def hidden_halves(shards):
    x = lax.axis_index("x")
    half = shards[0].shape[1] // 2

    def part(at):
        return jnp.concatenate(
            [lax.dynamic_slice_in_dim(shard, at * half, half, axis=1) for shard in shards], axis=1
        )

    return part(x), swap(part(1 - x), "x")


def join_rows(mine, other):
    both = pair(mine, other, lax.axis_index("x"))
    return both.reshape((-1,) + both.shape[2:])


def exchange_narrow(blocks):
    y, c = (lax.axis_index(name) for name in NARROW)
    shape = blocks.shape[2:]
    flat = blocks.reshape((4,) + shape)
    me = y * 2 + c
    got = [pick(flat, me)] + [swap(pick(flat, me ^ d), NARROW, d) for d in range(1, 4)]
    near, far = pair(got[0], got[1], c), pair(got[2], got[3], c)
    return pair(near, far, y)


def gather_tokens(block, *needed):
    return spread_core(block, after(swap(block, "y"), *needed))


def spread_core(block, by_y):
    y, c = (lax.axis_index(name) for name in NARROW)
    own = c * 2 + y
    return stack_rows(
        [block, by_y, swap(block, "c"), swap(by_y, "c")], [own, own ^ 1, own ^ 2, own ^ 3]
    )


def rotation(positions):
    half = HD // 2
    freqs = rope_base ** (-2.0 * jnp.arange(half, dtype=jnp.float32) / HD)
    angles = positions.astype(jnp.float32)[:, None] * freqs[None, :]
    cosine, sine = jnp.cos(angles), jnp.sin(angles)
    return jnp.concatenate([cosine, cosine], axis=1), jnp.concatenate([-sine, sine], axis=1)


def rms_back(grad_unit, unit, inverse):
    return inverse * (grad_unit - unit * jnp.mean(grad_unit * unit, axis=-1, keepdims=True))


def adam_update(grad, master, first, second, decay, count):
    mean_grad = grad / count
    first_new = beta_first * first + (1.0 - beta_first) * mean_grad
    second_new = beta_second * second + (1.0 - beta_second) * mean_grad * mean_grad
    update = first_new / first_fix / (jnp.sqrt(second_new / second_fix) + adam_eps)
    if decay:
        update = update + decay_rate * master
    return (grad, update)


def project(layer_input, weight, bias, cosine, sine, kv_cosine, kv_sine, heads):
    tokens = layer_input.shape[0]
    width = weight.shape[1]
    block = 256
    scale = HD ** (-0.5)

    def kernel(x_ref, w_ref, b_ref, c_ref, s_ref, kc_ref, ks_ref, a_ref, q_ref, kv_ref):
        x = wide_float(x_ref[...])
        inverse = lax.rsqrt(jnp.mean(x * x, axis=1, keepdims=True) + norm_eps)
        normed = low(x * inverse)
        a_ref[...] = normed
        linear = matmul(normed, w_ref[...]) + b_ref[...]
        for h in range(heads + 1):
            part = linear[:, h * HD : (h + 1) * HD]
            turned = pltpu.roll(part, HD // 2, axis=1)
            if h < heads:
                out = (part * c_ref[...] + turned * s_ref[...]) * scale
                q_ref[:, h * HD : (h + 1) * HD] = low(out)
            else:
                kv_ref[...] = low(part * kc_ref[...] + turned * ks_ref[...])

    def by_tokens(columns):
        return pl.BlockSpec((block, columns), lambda i: (i, 0))

    def whole(a):
        return pl.BlockSpec(a.shape, lambda i: (0, 0))

    return pl.pallas_call(
        kernel,
        grid=(tokens // block,),
        in_specs=[by_tokens(D), whole(weight), whole(bias)] + [by_tokens(HD)] * 4,
        out_specs=[by_tokens(D), by_tokens(heads * HD), by_tokens(HD)],
        out_shape=[
            jax.ShapeDtypeStruct((tokens, D), jnp.bfloat16),
            jax.ShapeDtypeStruct((tokens, heads * HD), jnp.bfloat16),
            jax.ShapeDtypeStruct((tokens, HD), jnp.bfloat16),
        ],
        name="project",
    )(layer_input, weight, bias, cosine, sine, kv_cosine, kv_sine)


def feed_forward(tokens_in, grads_in, w_gateup, half, at, count, into=None):
    tokens = tokens_in.shape[0]
    block = 512
    olds = [] if into is None else list(into)
    skip = at // block

    def kernel(b_ref, g_ref, wgu_ref, *refs):
        hid_ref, dgu_ref = refs[-2:]
        both = matmul(b_ref[...], wgu_ref[...])
        gate, upward = both[:, :half], both[:, half:]
        grad = wide_float(g_ref[...])
        logistic = jax.nn.sigmoid(gate)
        active = gate * logistic
        hid_ref[...] = low(active * upward)
        slope = logistic + active * (1.0 - logistic)
        dgu_ref[:, :half] = low(grad * upward * slope)
        dgu_ref[:, half:] = low(grad * active)

    def by_tokens(columns):
        return pl.BlockSpec((block, columns), lambda i: (i + skip, 0))

    return pl.pallas_call(
        kernel,
        grid=(count // block,),
        in_specs=[
            by_tokens(D),
            by_tokens(half),
            pl.BlockSpec(w_gateup.shape, lambda i: (0, 0), pipeline_mode=pl.Buffered(1)),
        ]
        + [pl.BlockSpec(memory_space=pl.ANY)] * len(olds),
        out_specs=[by_tokens(half), by_tokens(2 * half)],
        out_shape=[
            jax.ShapeDtypeStruct((tokens, half), jnp.bfloat16),
            jax.ShapeDtypeStruct((tokens, 2 * half), jnp.bfloat16),
        ],
        input_output_aliases={3: 0, 4: 1} if olds else {},
        name="feed_forward",
    )(tokens_in, grads_in, w_gateup, *olds)


def over_blocks(first_begin, last_begin, base, run, width, carry):
    first = first_begin // width
    end = (base + BLOCK_Q - 1) // width + 1
    clear = jnp.minimum((last_begin + width - 1) // width, end)
    clear_end = jnp.maximum((base + 1) // width, clear)
    before = clear - first

    def edge(t, carry):
        return run(jnp.where(t < before, first + t, clear_end + t - before), carry, True)

    carry = lax.fori_loop(clear, clear_end, lambda j, carry: run(j, carry, False), carry)
    return lax.fori_loop(0, before + end - clear_end, edge, carry)


def stacked_heads(ref, heads):
    return jnp.concatenate([ref[:, h * HD : (h + 1) * HD] for h in range(heads)], axis=0)


def attention_forward(queries, keys, values, begins, starts, place):
    tokens, columns = queries.shape
    heads = columns // HD
    length = keys.shape[0]
    rows = heads * BLOCK_Q

    def kernel(starts_ref, place_ref, q_ref, k_ref, v_ref, begin_ref, o_ref, lse_ref):
        step = pl.program_id(0)
        base = place_ref[0] * tokens + step * BLOCK_Q
        q = stacked_heads(q_ref, heads)
        row = base + lax.broadcasted_iota(jnp.int32, (BLOCK_Q, 1), 0)
        row = jnp.concatenate([row] * heads, axis=0)
        begin = jnp.concatenate([begin_ref[...]] * heads, axis=0)

        def run(j, carry, masked):
            top, total, acc = carry
            at = pl.multiple_of(j * FORWARD_K, FORWARD_K)
            k = k_ref[pl.ds(at, FORWARD_K), :]
            v = v_ref[pl.ds(at, FORWARD_K), :]
            s = matmul_nt(q, k)
            if masked:
                col = at + lax.broadcasted_iota(jnp.int32, (1, FORWARD_K), 1)
                s = jnp.where((col <= row) & (col >= begin), s, masked_score)
            new_top = jnp.maximum(top, jnp.max(s, axis=1, keepdims=True))
            p = jnp.exp(s - new_top)
            scale = jnp.exp(top - new_top)
            total = scale * total + jnp.sum(p, axis=1, keepdims=True)
            acc = scale * acc + matmul(low(p), v)
            return new_top, total, acc

        top, total, acc = over_blocks(
            starts_ref[2 * step],
            starts_ref[2 * step + 1],
            base,
            run,
            FORWARD_K,
            (
                jnp.full((rows, 1), masked_score, jnp.float32),
                jnp.zeros((rows, 1), jnp.float32),
                jnp.zeros((rows, HD), jnp.float32),
            ),
        )
        out = acc / total
        for h in range(heads):
            o_ref[:, h * HD : (h + 1) * HD] = out[h * BLOCK_Q : (h + 1) * BLOCK_Q]
        lse_ref[...] = (top + jnp.log(total)).reshape(heads, BLOCK_Q, 1)

    block = pl.BlockSpec((BLOCK_Q, columns), lambda i, *_: (i, 0))
    whole = pl.BlockSpec((length, HD), lambda i, *_: (0, 0))
    return pl.pallas_call(
        kernel,
        grid_spec=pltpu.PrefetchScalarGridSpec(
            num_scalar_prefetch=2,
            grid=(tokens // BLOCK_Q,),
            in_specs=[block, whole, whole, pl.BlockSpec((BLOCK_Q, 1), lambda i, *_: (i, 0))],
            out_specs=[block, pl.BlockSpec((heads, BLOCK_Q, 1), lambda i, *_: (0, i, 0))],
        ),
        out_shape=[
            jax.ShapeDtypeStruct((tokens, columns), jnp.float32),
            jax.ShapeDtypeStruct((heads, tokens, 1), jnp.float32),
        ],
        compiler_params=pltpu.CompilerParams(dimension_semantics=("arbitrary",)),
        name="attention_forward",
    )(starts, place, queries, keys, values, begins)


def attention_backward(
    queries, keys, values, begins, starts, place, grads, lse, outputs, cosine, sine
):
    tokens, columns = queries.shape
    heads = columns // HD
    length = keys.shape[0]
    rows = heads * BLOCK_Q

    def kernel(
        starts_ref, place_ref, q_ref, k_ref, v_ref, begin_ref, g_ref, lse_ref, o_ref,
        c_ref, s_ref, dq_ref, dk_ref, dv_ref,
    ):
        step = pl.program_id(0)

        @pl.when(step == 0)
        def _():
            dk_ref[...] = jnp.zeros_like(dk_ref)
            dv_ref[...] = jnp.zeros_like(dv_ref)

        base = place_ref[0] * tokens + step * BLOCK_Q
        q = stacked_heads(q_ref, heads)
        g = stacked_heads(g_ref, heads)
        delta = jnp.sum(wide_float(g) * stacked_heads(o_ref, heads), axis=1, keepdims=True)
        lse = lse_ref[...].reshape(rows, 1)
        row = base + lax.broadcasted_iota(jnp.int32, (BLOCK_Q, 1), 0)
        row = jnp.concatenate([row] * heads, axis=0)
        begin = jnp.concatenate([begin_ref[...]] * heads, axis=0)

        def less(a, column):
            high = low(-column)
            middle = low(-column - wide_float(high))
            last = low(-column - wide_float(high) - wide_float(middle))
            lane = lax.broadcasted_iota(jnp.int32, (rows, HD), 1)
            parts = jnp.where(lane == 1, middle, jnp.where(lane == 2, last, jnp.zeros_like(last)))
            return jnp.concatenate([a, jnp.where(lane == 0, high, parts)], axis=1)

        q_less = less(q, lse)
        g_less = less(g, delta)
        ones = jnp.ones((BLOCK_K, HD), jnp.bfloat16)

        def run(j, dq, masked):
            at = pl.multiple_of(j * BLOCK_K, BLOCK_K)
            k = k_ref[pl.ds(at, BLOCK_K), :]
            v = v_ref[pl.ds(at, BLOCK_K), :]
            s = matmul_nt(q_less, jnp.concatenate([k, ones], axis=1))
            if masked:
                col = at + lax.broadcasted_iota(jnp.int32, (1, BLOCK_K), 1)
                s = jnp.where((col <= row) & (col >= begin), s, masked_score)
            p = jnp.exp(s)
            ds = low(p * matmul_nt(g_less, jnp.concatenate([v, ones], axis=1)))
            dk_ref[pl.ds(at, BLOCK_K), :] += matmul_tn(ds, q)
            dv_ref[pl.ds(at, BLOCK_K), :] += matmul_tn(low(p), g)
            return dq + matmul(ds, k)

        dq = over_blocks(
            starts_ref[2 * step],
            starts_ref[2 * step + 1],
            base,
            run,
            BLOCK_K,
            jnp.zeros((rows, HD), jnp.float32),
        )
        for h in range(heads):
            part = dq[h * BLOCK_Q : (h + 1) * BLOCK_Q]
            turned = pltpu.roll(part, HD // 2, axis=1)
            part = (part * c_ref[...] - turned * s_ref[...]) * HD ** (-0.5)
            dq_ref[:, h * HD : (h + 1) * HD] = low(part)

    block = pl.BlockSpec((BLOCK_Q, columns), lambda i, *_: (i, 0))
    whole = pl.BlockSpec((length, HD), lambda i, *_: (0, 0))
    return pl.pallas_call(
        kernel,
        grid_spec=pltpu.PrefetchScalarGridSpec(
            num_scalar_prefetch=2,
            grid=(tokens // BLOCK_Q,),
            in_specs=[
                block,
                whole,
                whole,
                pl.BlockSpec((BLOCK_Q, 1), lambda i, *_: (i, 0)),
                block,
                pl.BlockSpec((heads, BLOCK_Q, 1), lambda i, *_: (0, i, 0)),
                block,
                pl.BlockSpec((BLOCK_Q, HD), lambda i, *_: (i, 0)),
                pl.BlockSpec((BLOCK_Q, HD), lambda i, *_: (i, 0)),
            ],
            out_specs=[block, whole, whole],
        ),
        out_shape=[
            jax.ShapeDtypeStruct((tokens, columns), jnp.bfloat16),
            jax.ShapeDtypeStruct((length, HD), jnp.float32),
            jax.ShapeDtypeStruct((length, HD), jnp.float32),
        ],
        compiler_params=pltpu.CompilerParams(dimension_semantics=("arbitrary",)),
        cost_estimate=pl.CostEstimate(
            flops=20 * tokens * tokens * columns, transcendentals=0, bytes_accessed=0
        ),
        name="attention_backward",
    )(starts, place, queries, keys, values, begins, grads, lse, outputs, cosine, sine)


def local(
    layer_input,
    grad_out,
    segment_ids,
    positions,
    norm_gains,
    norm_gains_first,
    norm_gains_second,
    query_weight,
    query_weight_first,
    query_weight_second,
    query_bias,
    query_bias_first,
    query_bias_second,
    keyvalue_weight,
    keyvalue_weight_first,
    keyvalue_weight_second,
    keyvalue_bias,
    keyvalue_bias_first,
    keyvalue_bias_second,
    output_weight,
    output_weight_first,
    output_weight_second,
    gateup_weight,
    gateup_weight_first,
    gateup_weight_second,
    down_weight,
    down_weight_first,
    down_weight_second,
):
    hi, lo, x, y, c = (lax.axis_index(name) for name in WIDE + NARROW)
    wide = lax.axis_size("hi") * 4
    tokens = layer_input.shape[0]
    quarter = tokens // 4
    heads = query_bias.shape[0]
    token_count = float(tokens * wide)
    rows = D // wide
    narrow_rows = rows // 4
    bias_part = query_bias.shape[1]
    kv_part = keyvalue_bias.shape[0]
    column_block = c * KV + y
    hidden = gateup_weight.shape[2]
    half = -(-hidden // (2 * LANES)) * LANES
    padding = 2 * half - hidden
    own = c * 2 + y

    kv_columns = low(keyvalue_weight).reshape(narrow_rows, 2, KV, HD)
    kv_columns = jnp.transpose(kv_columns, (2, 1, 0, 3))
    small = jnp.concatenate([low(norm_gains).reshape(-1), low(keyvalue_bias)])
    small = jnp.pad(small, (0, HD - small.shape[0])).reshape(1, 1, 1, HD)
    small = jnp.pad(small, ((0, 0), (0, 0), (0, 15), (0, 0)))
    blocks = jnp.concatenate([kv_columns, jnp.broadcast_to(small, (2, 2, 16, HD))], axis=2)
    blocks = exchange_narrow(blocks).reshape(4, narrow_rows + 16, HD)
    kv_mine = blocks[:, :narrow_rows].reshape(rows, HD)
    small_row = blocks[:, narrow_rows].reshape(1, 4 * HD)
    row_gains = wide_float(blocks[:, narrow_rows, : 2 * narrow_rows])
    row_gains = jnp.transpose(row_gains.reshape(4, 2, narrow_rows), (1, 0, 2)).reshape(2, rows, 1)
    bias_row = jnp.pad(low(query_bias).reshape(1, -1), ((0, 0), (0, 4 * HD - heads * bias_part)))
    extra = jnp.pad(jnp.concatenate([small_row, bias_row]), ((0, 14), (0, 0)))
    my_qkv = wide_float(jnp.concatenate([low(query_weight), kv_mine], axis=1))
    packed = jnp.concatenate([low(my_qkv * row_gains[0]), extra], axis=0)
    side = jnp.pad(low(output_weight).T, ((0, 16), (0, 0)))
    packed = jnp.concatenate([packed, side], axis=1)
    columns, out_columns = wide_columns(packed, 4 * HD)
    others = [swap(column, "x") for column in columns]
    out_others = [swap(column, "x") for column in after(out_columns, others)]
    w_qkv, small_all = assemble(columns, others, rows)
    small_all = wide_float(small_all)
    b_query = small_all[:, 1, : heads * bias_part].reshape(wide, heads, bias_part)
    small_all = small_all[:, 0].reshape(wide, 4, HD)
    gains = small_all[:, :, : 2 * narrow_rows].reshape(wide, 4, 2, narrow_rows)
    gains = jnp.transpose(gains, (2, 0, 1, 3)).reshape(2, D)
    b_kv = small_all[:, :, 2 * narrow_rows : 2 * narrow_rows + kv_part].reshape(2 * KV, HD)
    b_query = jnp.transpose(b_query, (1, 0, 2)).reshape(heads * HD)
    b_qkv = jnp.concatenate([b_query, pick(b_kv, column_block)])
    gain_two = gains[1]

    def padded(shard):
        return jnp.pad(low(shard), ((0, 0), (0, padding)))

    down_shard = join_rows(*hidden_halves([padded(down_weight.T)]))
    w_down = lax.all_gather(after(down_shard, columns), ("hi", "lo"), axis=0, tiled=True)
    gateup_halves = hidden_halves(
        after([padded(gateup_weight[:, 0]), padded(gateup_weight[:, 1])], others)
    )

    cosine, sine = rotation(positions)
    kv_cosine = jnp.where(c == 0, cosine, 1.0)
    kv_sine = jnp.where(c == 0, sine, 0.0)
    normed_one, queries, kv_own = project(
        layer_input, w_qkv, b_qkv[None], cosine, sine, kv_cosine, kv_sine, heads
    )
    gateup_shard = join_rows(*after(gateup_halves, kv_own))
    w_gateup = lax.all_gather(gateup_shard, ("hi", "lo"), axis=0, tiled=True)
    both = after(pair(kv_own, swap(kv_own, "lo"), lo), gateup_shard)
    by_place = pair(both, swap(both, "x"), x)
    kv_row = jnp.transpose(by_place, (1, 0, 2, 3)).reshape(4 * tokens, HD)
    kv_other = swap(kv_row, "c")
    keys = jnp.where(c == 0, kv_row, kv_other)
    values = jnp.where(c == 0, kv_other, kv_row)
    begins = segment_ids - hi * (4 * tokens)
    starts = jnp.stack([begins[::BLOCK_Q], begins[BLOCK_Q - 1 :: BLOCK_Q]], axis=1).reshape(-1)
    begins = begins[:, None]
    place = (lo * 2 + x).reshape(1).astype(jnp.int32)
    grad_blocks = grad_out.reshape(4, quarter, D)
    grad_near = [pick(grad_blocks, own ^ d) for d in range(4)]
    grad_far = [swap(part, "x") for part in after(grad_near[:2], kv_row)]
    attention, log_total = attention_forward(queries, keys, values, begins, starts, place)
    w_output, _ = assemble(*after((out_columns, out_others), attention), rows)
    grad_far = after(grad_far, attention)
    ff_grad = stack_rows(grad_near + grad_far + [swap(part, "c") for part in grad_far], range(8))
    attention_low = low(attention)

    def halves(block):
        split = block.reshape(2, -1, block.shape[-1])
        return pick(split, c), pick(split, 1 - c)

    def send_core(kept, sent):
        return kept + wide_float(swap(low(sent), "c"))

    attention_kept, attention_sent = halves(attention_low)
    sent = matmul_nt(attention_sent, w_output)
    out_total = send_core(matmul_nt(attention_kept, w_output), sent)
    out_split = out_total.reshape(2, quarter, D)
    out_other = swap(low(pick(out_split, 1 - y)), "y")
    grad_hidden = low(matmul(after(ff_grad, out_total), w_down))
    out_other = after(out_other, grad_hidden)
    residual = wide_float(pick(layer_input.reshape(4, quarter, D), own))
    residual = residual + pick(out_split, y) + wide_float(out_other)
    inverse_two = lax.rsqrt(jnp.mean(residual * residual, axis=-1, keepdims=True) + norm_eps)
    unit_two = residual * inverse_two
    normed_two = low(unit_two * gain_two)

    by_y = swap(normed_two, "y")
    by_x = swap(normed_two, "x")
    by_both = [swap(by_y[:, : D // 2], "x"), swap(by_x[:, D // 2 :], "y")]
    count = 4 * quarter
    ff_input = stack_rows(
        [normed_two, by_y, swap(normed_two, "c"), swap(by_y, "c")], range(4), count=8
    )
    firsts = feed_forward(ff_input, grad_hidden, w_gateup, half, 0, count)
    by_both = after(by_both, firsts[0])
    by_both = jnp.concatenate(by_both, axis=1)
    ff_input = stack_rows(
        [by_x, by_both, swap(by_x, "c"), swap(by_both, "c")], range(4, 8), into=ff_input, count=8
    )
    hidden_all, both_all = feed_forward(
        ff_input, grad_hidden, w_gateup, half, count, count, into=firsts
    )

    half_d = D // 2

    def join_core(sums):
        return wide_float(sums[: 2 * quarter]) + wide_float(swap(sums[2 * quarter :], "c"))

    def first_sends(far_sums, near_sums):
        to_x = low(far_sums[:, :half_d])
        to_y = low(jnp.concatenate([near_sums[quarter:, half_d:], far_sums[quarter:, half_d:]]))
        return to_x, to_y

    def second_sends(far_sums, near_sums, from_x, from_y):
        left = near_sums[:, :half_d] + wide_float(from_x)
        right = near_sums[:quarter, half_d:] + wide_float(from_y[:quarter])
        to_x = low(far_sums[:quarter, half_d:] + wide_float(from_y[quarter:]))
        return (left[:quarter], right), (low(left[quarter:]), to_x)

    def finish_sums(kept, from_y, from_x):
        return jnp.concatenate([kept[0] + wide_float(from_y), kept[1] + wide_float(from_x)], axis=1)

    grad_gateup = low(matmul_tn(ff_input, both_all))
    both_all = after(both_all, grad_gateup)
    feed_far = low(matmul_nt(both_all[count:], w_gateup))
    feed_near = low(matmul_nt(after(both_all, feed_far)[:count], w_gateup))

    def over_rows(grad):
        return lax.psum_scatter(grad, ("hi", "lo"), scatter_dimension=0, tiled=True)

    far_sums, near_sums = join_core(feed_far), join_core(feed_near)
    to_x, to_y = first_sends(far_sums, near_sums)
    from_x, from_y = swap(to_x, "x"), swap(to_y, "y")
    hidden_late = after(hidden_all, to_x, to_y)
    mlp_far = low(matmul_nt(hidden_late[count:], w_down))
    mlp_near = low(matmul_nt(after(hidden_late, mlp_far)[:count], w_down))
    from_x, from_y = after((from_x, from_y), mlp_near)
    kept, (to_y, to_x) = second_sends(far_sums, near_sums, from_x, from_y)
    from_x, from_y = swap(to_x, "x"), swap(to_y, "y")
    grad_normed_two = finish_sums(kept, from_y, from_x)
    grad_residual = wide_float(grad_near[0]) + rms_back(
        grad_normed_two * gain_two, unit_two, inverse_two
    )
    residual_own = low(grad_residual)
    ff_late, hidden_all = after((ff_grad, hidden_all), swap(residual_own, "c"))
    grad_down = low(matmul_tn(ff_late, hidden_all))
    rows_gateup, rows_down = over_rows(grad_gateup), over_rows(grad_down)
    mlp_far, mlp_near = after((mlp_far, mlp_near), residual_own)
    mlp_far, mlp_near = low(join_core(mlp_far)), join_core(mlp_near)
    residual_low = gather_tokens(residual_own, grad_down, mlp_near)

    grad_attention = low(matmul(residual_low, w_output))
    x_output = send_x(
        low(matmul_tn(residual_low, attention_low)).reshape(wide, rows, heads * HD)
    )
    from_far = swap(after(mlp_far, residual_low), "x")
    grad_queries, grad_keys, grad_values = attention_backward(
        queries, keys, values, begins, starts, place, grad_attention, log_total, attention,
        cosine, sine,
    )
    kv_sent = low(jnp.where(c == 0, grad_values, grad_keys))
    kv_sent, from_far, x_output = after((kv_sent, from_far, x_output), grad_queries, rows_gateup)
    kv_grad = jnp.where(c == 0, grad_keys, grad_values) + wide_float(swap(kv_sent, "c"))
    kv_grad = kv_grad.reshape(2, 2, tokens, HD)
    kv_kept, kv_sent = (
        lax.dynamic_index_in_dim(kv_grad, at, axis=1, keepdims=False) for at in (x, 1 - x)
    )
    kv_sent = low(kv_sent)
    from_far, x_output, mlp_near, normed_late = after(
        (from_far, x_output, mlp_near, normed_one), kv_sent
    )
    rows_output = over_rows(low(add_up(x_output)).reshape(-1, heads * HD))
    mlp_sums = mlp_near + wide_float(from_far)
    from_y = swap(low(mlp_sums[quarter:]), "y")
    kv_grad = kv_kept + wide_float(swap(kv_sent, "x"))
    parts_gateup = send_hidden(after(rows_gateup, kv_grad))
    from_y = after(from_y, kv_grad)
    layer_own = low(residual + mlp_sums[:quarter] + wide_float(from_y))
    kv_grad = pick(kv_grad, lo) + wide_float(swap(low(pick(kv_grad, 1 - lo)), "lo"))
    turned = jnp.concatenate([kv_grad[:, HD // 2 :], kv_grad[:, : HD // 2]], axis=1)
    grad_kv = low(kv_grad * kv_cosine - turned * kv_sine)
    grad_kv = after(grad_kv, parts_gateup)

    w_query, w_kv = w_qkv[:, : heads * HD], w_qkv[:, heads * HD :]

    def input_part(kv_part_grad, query_part_grad):
        return matmul_nt(query_part_grad, w_query) + matmul_nt(kv_part_grad, w_kv)

    query_kept, query_sent = halves(grad_queries)
    kv_kept, kv_sent = halves(grad_kv)
    part_sent = low(input_part(kv_sent, query_sent))
    part_kept = input_part(kv_kept, query_kept)
    part_total = send_core(part_kept, part_sent)
    part_other = swap(low(part_total), "y")
    layer_by_y = swap(after(layer_own, part_other), "y")
    grad_normed_one = part_total + wide_float(part_other)
    core_input = pick(after(layer_input, part_total).reshape(2, 2 * quarter, D), c)
    core_input = wide_float(core_input)
    core_inverse = lax.rsqrt(jnp.mean(core_input * core_input, axis=-1, keepdims=True) + norm_eps)
    core_grad = wide_float(pick(residual_low.reshape(2, 2 * quarter, D), c)) + rms_back(
        grad_normed_one, core_input * core_inverse, core_inverse
    )
    core_grad = low(core_grad)
    input_grad = stack_rows([core_grad, swap(core_grad, "c")], [c, 1 - c])
    layer_output = spread_core(layer_own, after(layer_by_y, core_grad))

    grad_query_weight = low(matmul_tn(normed_late, grad_queries)).reshape(wide, rows, heads * HD)
    grad_kv_weight = low(matmul_tn(normed_one, grad_kv)).reshape(wide, rows, HD)
    bias_query = jnp.sum(wide_float(grad_queries), axis=0).reshape(heads, wide, bias_part)
    bias_query = jnp.transpose(bias_query, (1, 0, 2)).reshape(wide, heads * bias_part)
    kv_sums = jnp.sum(wide_float(grad_kv), axis=0, keepdims=True)
    bias_kv = jnp.where(jnp.arange(2 * KV)[:, None] == column_block, kv_sums, 0.0)
    bias_kv = bias_kv.reshape(wide, 4 * kv_part)
    bias_all = jnp.concatenate([bias_query, bias_kv], axis=1)
    bias_all = jnp.pad(bias_all, ((0, 0), (0, HD - bias_all.shape[1])))
    extra = jnp.pad(low(bias_all)[:, None], ((0, 0), (0, 15), (0, 3 * HD)))
    grad_qkv = jnp.concatenate([grad_query_weight, grad_kv_weight], axis=2)
    x_qkv = send_x(jnp.concatenate([grad_qkv, extra], axis=1))
    parts_gateup = after(parts_gateup, part_total)
    summed_gate = join_hidden(*(part[:, :half] for part in parts_gateup))
    summed_up = join_hidden(*(part[:, half:] for part in parts_gateup))
    summed_gateup = jnp.stack([summed_gate[:, :hidden], summed_up[:, :hidden]], axis=1)
    summed_gateup = with_layout_constraint(summed_gateup, Layout((0, 1, 2)))
    gateup_update = adam_update(
        summed_gateup, gateup_weight, gateup_weight_first, gateup_weight_second, True, token_count
    )
    sums_qkv = low(add_up(after(x_qkv, gateup_update[1], rows_output, rows_down)))
    summed = wide_float(over_rows(sums_qkv.reshape(-1, 4 * HD)))
    summed_query = summed[:rows, : heads * HD]
    summed_kv = summed[:rows, heads * HD :]
    summed_query_bias = summed[rows, : heads * bias_part].reshape(heads, bias_part)
    kv_bias = summed[rows, heads * bias_part : heads * bias_part + 4 * kv_part]
    parts_down = send_hidden(after(rows_down, sums_qkv))
    summed_output = wide_float(after(rows_output, sums_qkv))

    grad_gain_one = jnp.sum(
        summed_query * my_qkv[:, : heads * HD], axis=1
    ) + jnp.sum(summed_kv * my_qkv[:, heads * HD :], axis=1)
    summed_query = summed_query * row_gains[0]
    summed_kv = summed_kv * row_gains[0]
    grad_gain_two = (
        jnp.sum(summed_gateup * wide_float(low(gateup_weight)), axis=(1, 2)) / row_gains[1, :, 0]
    )
    gain_parts = jnp.stack([grad_gain_one, grad_gain_two]).reshape(2, 4, narrow_rows)
    gain_parts = jnp.transpose(gain_parts, (1, 0, 2)).reshape(4, 2 * narrow_rows)
    last = jnp.concatenate([gain_parts, kv_bias.reshape(4, kv_part)], axis=1)
    last = jnp.pad(last, ((0, 0), (0, HD - last.shape[1])))[:, None]
    last = jnp.pad(last, ((0, 0), (0, 7), (0, 0)))
    last = jnp.concatenate([summed_kv.reshape(4, narrow_rows, HD), last], axis=1)
    last = exchange_narrow(last.reshape((2, 2) + last.shape[1:]))
    summed_keyvalue = jnp.transpose(last[:, :, :narrow_rows], (2, 1, 0, 3))
    summed_keyvalue = summed_keyvalue.reshape(narrow_rows, 2 * KV * HD)
    small_sums = jnp.sum(last[:, :, narrow_rows], axis=(0, 1))
    summed_gains = small_sums[: 2 * narrow_rows].reshape(2, narrow_rows)
    summed_keyvalue_bias = small_sums[2 * narrow_rows : 2 * narrow_rows + kv_part]
    summed_output = summed_output.T

    gains_update = adam_update(
        summed_gains, norm_gains, norm_gains_first, norm_gains_second, False, token_count
    )
    query_update = adam_update(
        summed_query, query_weight, query_weight_first, query_weight_second, True, token_count
    )
    qbias_update = adam_update(
        summed_query_bias, query_bias, query_bias_first, query_bias_second, False, token_count
    )
    keyvalue_update = adam_update(
        summed_keyvalue,
        keyvalue_weight,
        keyvalue_weight_first,
        keyvalue_weight_second,
        True,
        token_count,
    )
    kvbias_update = adam_update(
        summed_keyvalue_bias,
        keyvalue_bias,
        keyvalue_bias_first,
        keyvalue_bias_second,
        False,
        token_count,
    )
    output_update = adam_update(
        summed_output, output_weight, output_weight_first, output_weight_second, True, token_count
    )
    summed_down = join_hidden(*after(parts_down, core_grad))[:, :hidden].T
    down_update = adam_update(
        summed_down, down_weight, down_weight_first, down_weight_second, True, token_count
    )
    return (
        layer_output,
        input_grad,
        *gains_update,
        *query_update,
        *qbias_update,
        *keyvalue_update,
        *kvbias_update,
        *output_update,
        *gateup_update,
        *down_update,
    )


def solution(mesh):
    devices = mesh.devices.reshape(-1, 2, 2, 2, 2)
    split = Mesh(devices, WIDE + NARROW)
    token_matrix = P(WIDE, None)
    token_vector = P(WIDE)
    gains = P(None, WIDE + NARROW)
    query = P(WIDE, NARROW)
    by_narrow = P(NARROW, WIDE)
    keyvalue = P(WIDE + NARROW, None)
    keyvalue_bias = P(WIDE + NARROW)
    gateup = P(WIDE, None, NARROW)
    parameters = (gains, query, by_narrow, keyvalue, keyvalue_bias, by_narrow, gateup, by_narrow)
    in_specs = (token_matrix, token_matrix, token_vector, token_vector)
    out_specs = (token_matrix, token_matrix)
    for spec in parameters:
        in_specs += (spec,) * 3
        out_specs += (spec,) * 2
    return jax.shard_map(local, mesh=split, in_specs=in_specs, out_specs=out_specs, check_vma=False)
```
